32 devices in a mesh: seq: 32 (over z, y, x, core).
Axes of the slice: x: 2, y: 2, z: 4, core: 2. Of those that a mesh axis runs over, the one named last changes fastest.
Arguments:
- incoming_hidden: bfloat16 [2, 16384, 768], P(None, 'seq'), may hold values from -6 to 6
- packed_run_lengths: int32 [2, 8], replicated, may hold values from 1 to 8192, 16384 in all within a row
- prior_standardize_factor: float32 [768], replicated, may hold values from 0.5 to 1.5
- prior_standardize_addend: float32 [768], replicated, may hold values from -3 to 3
- respond_interpolant: float32 [768], replicated, may hold values from 0 to 1
- address_interpolant: float32 [768], replicated, may hold values from 0 to 1
- content_interpolant: float32 [768], replicated, may hold values from 0 to 1
- valve_interpolant: float32 [768], replicated, may hold values from 0 to 1
- respond_transform: bfloat16 [768, 768], replicated, may hold values from -0.21875 to 0.21875
- address_transform: bfloat16 [768, 768], replicated, may hold values from -0.21875 to 0.21875
- content_transform: bfloat16 [768, 768], replicated, may hold values from -0.21875 to 0.21875
- valve_transform: bfloat16 [768, 768], replicated, may hold values from -0.21875 to 0.21875
- damping_rates: float32 [768], replicated, may hold values from -12 to -3.4
- immediate_boost: float32 [768], replicated, may hold values from -3 to 3
- cluster_normal_factor: float32 [768], replicated, may hold values from 0.5 to 1.5
- cluster_normal_shift_term: float32 [768], replicated, may hold values from -3 to 3
- readout_transform: bfloat16 [768, 768], replicated, may hold values from -0.4375 to 0.4375
- posterior_standardize_factor: float32 [768], replicated, may hold values from 0.5 to 1.5
- posterior_standardize_addend: float32 [768], replicated, may hold values from -3 to 3
- dense_address_interpolant: float32 [768], replicated, may hold values from 0 to 1
- dense_respond_interpolant: float32 [768], replicated, may hold values from 0 to 1
- dense_address_transform: bfloat16 [768, 2688], replicated, may hold values from -0.21875 to 0.21875
- dense_content_transform: bfloat16 [2688, 768], replicated, may hold values from -0.125 to 0.125
- dense_respond_transform: bfloat16 [768, 768], replicated, may hold values from -0.21875 to 0.21875
- objective_adjoint: bfloat16 [2, 16384, 768], P(None, 'seq'), may hold values from -6 to 6
Outputs:
- block_out: bfloat16 [2, 16384, 768], P(None, 'seq')
- grad_tokens: float32 [2, 16384, 768], P(None, 'seq')
- grad_first_gain: float32 [768], replicated
- grad_first_bias: float32 [768], replicated
- grad_mix_recept: float32 [768], replicated
- grad_mix_keys: float32 [768], replicated
- grad_mix_values: float32 [768], replicated
- grad_mix_gate: float32 [768], replicated
- grad_recept_weight: float32 [768, 768], replicated
- grad_keys_weight: float32 [768, 768], replicated
- grad_values_weight: float32 [768, 768], replicated
- grad_gate_weight: float32 [768, 768], replicated
- grad_time_decay: float32 [768], replicated
- grad_time_bonus: float32 [768], replicated
- grad_group_gain: float32 [768], replicated
- grad_group_bias: float32 [768], replicated
- grad_output_weight: float32 [768, 768], replicated
- grad_second_gain: float32 [768], replicated
- grad_second_bias: float32 [768], replicated
- grad_mix_expand: float32 [768], replicated
- grad_mix_filter: float32 [768], replicated
- grad_expand_weight: float32 [768, 2688], replicated
- grad_shrink_weight: float32 [2688, 768], replicated
- grad_filter_weight: float32 [768, 768], replicated
The draws below stay inside these ranges and needn't reach their ends.
Inputs may be any that keep to these rules, and one draw needn't show every extreme that they name: `packed_run_lengths`: each row holds 8 lengths that sum to 16384; the largest of each row is exactly 8192.
All inputs are finite; a program needn't handle non-finite values.
Results may differ from the reference program's by a relative error of at most 0.001.
Values sent between devices are 32-bit elements; how exact they have to be, the bound alone decides.
A program may use at most 512 MiB of HBM per device.

```python
import math
import jax
import jax.numpy as jnp
import numpy as np
from jax import lax

HIDDEN_BREADTH = 768
LANE_FEATURES = 64
FF = 2688
MICROBATCHES = 2
SPAN = 64
NSEQ = 8
POSITIONS_EVERY = 16384
MOSTLEN = 8192


def draw_damping_rates(key, part):
    subgroup_total = HIDDEN_BREADTH // LANE_FEATURES
    pick_key = jax.random.fold_in(key, 11)
    spread_key = jax.random.fold_in(key, 12)
    slow_share = 0.5
    slow_heads = jax.random.uniform(pick_key, (subgroup_total,), jnp.float32) < slow_share
    spread = jax.random.uniform(spread_key, (subgroup_total, LANE_FEATURES), jnp.float32)
    slow_value = jnp.log(2.3 / MOSTLEN) - 2.0 * spread
    fast_value = -4.2 + 0.8 * spread
    values = jnp.where(slow_heads[:, None], slow_value, fast_value)
    return values.reshape(HIDDEN_BREADTH).astype(jnp.float32)


def shard_levels(key, shape, cuts, least, largest):
    factor_of, own = 1.0, jax.random.fold_in(key, 6)
    for axis_at, shards_of in cuts:
        draws = jnp.exp(jax.random.uniform(jax.random.fold_in(own, axis_at), (shards_of,), jnp.float32, least / len(cuts), largest / len(cuts)))
        factor_of = factor_of * jnp.repeat(draws, shape[axis_at] // shards_of).reshape([-1 if axis == axis_at else 1 for axis in range(len(shape))])
    return factor_of


def profile(amount, total, most, slope):
    weights = [(1 << 20) // math.isqrt(grade ** slope) + 1 for grade in range(2, amount + 1)]
    rest, given = total - most - (amount - 1), [1] * (amount - 1)
    while rest > 0:
        free = [i for i in range(amount - 1) if given[i] < most]
        pool, left = sum([weights[i] for i in free]), rest
        for i in free:
            more = min(most - given[i], max(1, left * weights[i] // pool), rest)
            given[i] = given[i] + more
            rest = rest - more
    return np.array([most] + given)


def ragged(key, number_of, total, most, skew):
    if number_of == 2:
        one = jax.random.randint(key, (), max(1, total - most), min(most, total - 1) + 1)
        return jnp.stack([one, total - one])
    lengths = jnp.asarray(profile(number_of, total, most, skew), jnp.int32)
    pairs = (number_of - 1) // 2
    donor, receiver = lengths[1:1 + 2 * pairs:2], lengths[2:2 + 2 * pairs:2]
    slack = jnp.minimum(donor - 1, most - receiver)
    shifted = jax.random.randint(jax.random.fold_in(key, 1), (pairs,), 0, 1 << 20) % (slack + 1)
    lengths = lengths.at[1:1 + 2 * pairs:2].set(donor - shifted).at[2:2 + 2 * pairs:2].set(receiver + shifted)
    return lengths[jax.random.permutation(jax.random.fold_in(key, 2), number_of)]


def scatter_about(rng, shape, scale, bound, pieces=(), kind=jnp.bfloat16):
    drawn = scale * jax.random.normal(rng, shape, jnp.float32)
    if pieces:
        drawn = drawn * shard_levels(rng, shape, pieces, -0.22, 0.18)
    return jnp.clip(drawn, -bound, bound).astype(kind)


def setup_inputs(seed: int = 0) -> dict:
    splits = jax.random.split(jax.random.key(seed), 26)
    return {
        "incoming_hidden": scatter_about(splits[0], (MICROBATCHES, POSITIONS_EVERY, HIDDEN_BREADTH), 1.0, 6.0, ((1, 32),)),
        "packed_run_lengths": jax.vmap(lambda own: ragged(own, NSEQ, POSITIONS_EVERY, MOSTLEN, 2))(jax.random.split(splits[1], MICROBATCHES)).reshape((MICROBATCHES, NSEQ)).astype(jnp.int32),
        "prior_standardize_factor": jnp.clip(1.0 + 0.1 * jax.random.normal(splits[2], (HIDDEN_BREADTH,), jnp.float32), 0.5, 1.5),
        "prior_standardize_addend": scatter_about(splits[3], (HIDDEN_BREADTH,), 0.3, 3.0, (), jnp.float32),
        "respond_interpolant": jnp.clip(jax.random.uniform(splits[4], (HIDDEN_BREADTH,), jnp.float32, 0.0, 1.0), 0.0, 1.0),
        "address_interpolant": jnp.clip(jax.random.uniform(splits[5], (HIDDEN_BREADTH,), jnp.float32, 0.0, 1.0), 0.0, 1.0),
        "content_interpolant": jnp.clip(jax.random.uniform(splits[6], (HIDDEN_BREADTH,), jnp.float32, 0.0, 1.0), 0.0, 1.0),
        "valve_interpolant": jnp.clip(jax.random.uniform(splits[7], (HIDDEN_BREADTH,), jnp.float32, 0.0, 1.0), 0.0, 1.0),
        "respond_transform": scatter_about(splits[8], (HIDDEN_BREADTH, HIDDEN_BREADTH), HIDDEN_BREADTH ** -0.5, 0.21875),
        "address_transform": scatter_about(splits[9], (HIDDEN_BREADTH, HIDDEN_BREADTH), HIDDEN_BREADTH ** -0.5, 0.21875),
        "content_transform": scatter_about(splits[10], (HIDDEN_BREADTH, HIDDEN_BREADTH), HIDDEN_BREADTH ** -0.5, 0.21875),
        "valve_transform": scatter_about(splits[11], (HIDDEN_BREADTH, HIDDEN_BREADTH), HIDDEN_BREADTH ** -0.5, 0.21875),
        "damping_rates": draw_damping_rates(jax.random.fold_in(splits[25], 71), 0),
        "immediate_boost": scatter_about(splits[13], (HIDDEN_BREADTH,), 1.0, 3.0, (), jnp.float32),
        "cluster_normal_factor": jnp.clip(1.0 + 0.1 * jax.random.normal(splits[14], (HIDDEN_BREADTH,), jnp.float32), 0.5, 1.5),
        "cluster_normal_shift_term": scatter_about(splits[15], (HIDDEN_BREADTH,), 0.3, 3.0, (), jnp.float32),
        "readout_transform": scatter_about(splits[16], (HIDDEN_BREADTH, HIDDEN_BREADTH), (HIDDEN_BREADTH // 4) ** -0.5, 0.4375),
        "posterior_standardize_factor": jnp.clip(1.0 + 0.1 * jax.random.normal(splits[17], (HIDDEN_BREADTH,), jnp.float32), 0.5, 1.5),
        "posterior_standardize_addend": scatter_about(splits[18], (HIDDEN_BREADTH,), 0.3, 3.0, (), jnp.float32),
        "dense_address_interpolant": jnp.clip(jax.random.uniform(splits[19], (HIDDEN_BREADTH,), jnp.float32, 0.0, 1.0), 0.0, 1.0),
        "dense_respond_interpolant": jnp.clip(jax.random.uniform(splits[20], (HIDDEN_BREADTH,), jnp.float32, 0.0, 1.0), 0.0, 1.0),
        "dense_address_transform": scatter_about(splits[21], (HIDDEN_BREADTH, FF), HIDDEN_BREADTH ** -0.5, 0.21875),
        "dense_content_transform": scatter_about(splits[22], (FF, HIDDEN_BREADTH), FF ** -0.5, 0.125),
        "dense_respond_transform": scatter_about(splits[23], (HIDDEN_BREADTH, HIDDEN_BREADTH), HIDDEN_BREADTH ** -0.5, 0.21875),
        "objective_adjoint": scatter_about(splits[24], (MICROBATCHES, POSITIONS_EVERY, HIDDEN_BREADTH), 1.0, 6.0, ((1, 32),)),
    }


@jax.custom_vjp
def low(v):
    return lax.optimization_barrier(v.astype(jnp.bfloat16)).astype(jnp.float32)

@jax.custom_vjp
def low_back(v):
    return v

def low_keep(v):
    return (low(v), None)

def low_pass(kept, grad):
    return (grad,)

def back_keep(v):
    return (v, None)

def back_low(kept, grad):
    return (low(grad),)
low.defvjp(low_keep, low_pass)
low_back.defvjp(back_keep, back_low)
highest = lax.Precision.HIGHEST

def product(factor_left, factor_right):
    return jnp.dot(factor_left, factor_right, precision=highest, preferred_element_type=jnp.float32)

def standardized_entries(values, gain_vector, bias_vector, epsilon):
    average = lax.optimization_barrier(jnp.mean(values, axis=-1, keepdims=True))
    centred = values - average
    variance = lax.optimization_barrier(jnp.mean(centred * centred, axis=-1, keepdims=True))
    return centred * lax.rsqrt(variance + epsilon) * gain_vector + bias_vector

def earlier_rows(normed, first_row, keep_rows):
    return jnp.concatenate([first_row[:, None, :], normed[:, :-1, :]], axis=1) * keep_rows[:, :, None]

def time_inputs(keep_rows, normed, first_row, respond_interpolant, address_interpolant, content_interpolant, valve_interpolant, respond_transform, address_transform, content_transform, valve_transform):
    earlier = earlier_rows(normed, first_row, keep_rows)
    difference = normed - earlier
    acceptor_lines = product(earlier + respond_interpolant * difference, respond_transform)
    lookup_projection_lines = product(earlier + address_interpolant * difference, address_transform)
    payload_projection_lines = product(earlier + content_interpolant * difference, content_transform)
    valve_entries = jax.nn.silu(product(earlier + valve_interpolant * difference, valve_transform))
    return (acceptor_lines, lookup_projection_lines, payload_projection_lines, valve_entries)

def blended_result_post(subgroup_total, readout_entries, valve_entries, cluster_normal_factor, cluster_normal_shift_term, readout_transform, skip_connection):
    arranged_entries = readout_entries.shape
    divided_entries_list = readout_entries.reshape(arranged_entries[0], arranged_entries[1], subgroup_total, arranged_entries[2] // subgroup_total)
    clustered_values = standardized_entries(divided_entries_list, 1.0, 0.0, 0.00064).reshape(arranged_entries) * cluster_normal_factor + cluster_normal_shift_term
    return skip_connection + product(clustered_values * valve_entries, readout_transform)

def channel_mix(keep_rows, normed, first_row, dense_address_interpolant, dense_respond_interpolant, dense_address_transform, dense_content_transform, dense_respond_transform, skip_connection):
    earlier = earlier_rows(normed, first_row, keep_rows)
    difference = normed - earlier
    hidden = jnp.square(jax.nn.relu(product(earlier + dense_address_interpolant * difference, dense_address_transform)))
    return skip_connection + jax.nn.sigmoid(product(earlier + dense_respond_interpolant * difference, dense_respond_transform)) * product(hidden, dense_content_transform)

def attention_recurrence_tile(recurrent_accumulator, piece_fraction, fading_logscale, reward_each_lane):
    acceptor_lines, lookup_projection_lines, payload_projection_lines, reset_markers = piece_fraction
    length = acceptor_lines.shape[1]
    steps_pos = jnp.arange(length).astype(jnp.float32)
    counts = jnp.cumsum(reset_markers, axis=1)
    fresh_rows = (counts == 0.0).astype(jnp.float32)
    intact = fresh_rows[:, -1]
    decay_query = jnp.exp(fading_logscale[None] * steps_pos[:, None, None])
    decay_key = jnp.exp(-fading_logscale[None] * (steps_pos[:, None, None] + 1.0))
    decay_end = jnp.exp(fading_logscale[None] * (length - 1.0 - steps_pos)[:, None, None])
    query_rows = acceptor_lines * decay_query[None]
    key_decayed = lookup_projection_lines * decay_key[None]
    scores = jnp.einsum('bthn,bshn->bhts', query_rows, key_decayed, precision=highest)
    causal = steps_pos[:, None] > steps_pos[None, :]
    same_doc = counts[:, :, None] == counts[:, None, :]
    allowed = jnp.logical_and(causal[None], same_doc)[:, None]
    scores = jnp.where(allowed, scores, 0.0)
    present_quantity = lax.optimization_barrier(jnp.sum(acceptor_lines * reward_each_lane[None, None] * lookup_projection_lines, axis=-1))
    output = jnp.einsum('bhts,bshm->bthm', scores, payload_projection_lines, precision=highest)
    output = output + present_quantity[..., None] * payload_projection_lines
    output = output + fresh_rows[:, :, None, None] * jnp.einsum('bthn,bhnm->bthm', query_rows, recurrent_accumulator, precision=highest)
    last_seg = (counts == counts[:, -1:]).astype(jnp.float32)
    keys_end = lookup_projection_lines * decay_end[None] * last_seg[:, :, None, None]
    recurrent_accumulator = intact[:, None, None, None] * jnp.exp(fading_logscale * length)[None, :, :, None] * recurrent_accumulator + jnp.einsum('bshn,bshm->bhnm', keys_end, payload_projection_lines, precision=highest)
    return (recurrent_accumulator, output)

def attention_recurrence_stream(acceptor_lines, lookup_projection_lines, payload_projection_lines, reset_markers, fading_logscale, reward_each_lane, recurrent_accumulator):
    batches = acceptor_lines.shape[0]
    blocks = acceptor_lines.shape[1] // SPAN

    def to_blocks(tensor):
        return jnp.moveaxis(tensor.reshape((batches, blocks, SPAN) + tensor.shape[2:]), 1, 0)
    validated_quantity = jax.checkpoint(attention_recurrence_tile)

    def advance(running_accumulator, piece_fraction):
        return validated_quantity(running_accumulator, piece_fraction, fading_logscale, reward_each_lane)
    recurrent_accumulator, outputs = lax.scan(advance, recurrent_accumulator, (to_blocks(acceptor_lines), to_blocks(lookup_projection_lines), to_blocks(payload_projection_lines), to_blocks(reset_markers)))
    return (jnp.moveaxis(outputs, 0, 1).reshape(acceptor_lines.shape), recurrent_accumulator)

def reference(incoming_hidden, packed_run_lengths, prior_standardize_factor, prior_standardize_addend, respond_interpolant, address_interpolant, content_interpolant, valve_interpolant, respond_transform, address_transform, content_transform, valve_transform, damping_rates, immediate_boost, cluster_normal_factor, cluster_normal_shift_term, readout_transform, posterior_standardize_factor, posterior_standardize_addend, dense_address_interpolant, dense_respond_interpolant, dense_address_transform, dense_content_transform, dense_respond_transform, objective_adjoint):
    subgroup_total = HIDDEN_BREADTH // LANE_FEATURES
    positions = jnp.arange(POSITIONS_EVERY).astype(jnp.int32)
    bounds = (jnp.cumsum(packed_run_lengths, axis=1) - packed_run_lengths).astype(jnp.int32)
    reset_markers = jnp.any(positions[None, :, None] == bounds[:, None, :], axis=2).astype(jnp.float32)
    keep_rows = 1.0 - reset_markers
    zero_row = jnp.zeros((MICROBATCHES, HIDDEN_BREADTH), jnp.float32)
    split_layout = (MICROBATCHES, POSITIONS_EVERY, subgroup_total, LANE_FEATURES)

    def forward(trained_coefficient_tuple):
        ordered_positions, trained_prior_factor, trained_prior_addend, trained_respond_interpolant, trained_address_interpolant, trained_content_interpolant, trained_valve_interpolant, trained_respond, trained_address, trained_content, trained_valve, trained_damping, trained_immediate_boost, trained_cluster_factor, trained_cluster_addend, trained_readout, trained_posterior_factor, trained_posterior_addend, trained_dense_address_mixer, trained_dense_respond_mixer, trained_dense_address, trained_dense_content, trained_dense_respond = trained_coefficient_tuple
        normed = standardized_entries(ordered_positions, trained_prior_factor, trained_prior_addend, 1e-05)
        acceptor_lines, lookup_projection_lines, payload_projection_lines, valve_entries = time_inputs(keep_rows, normed, zero_row, trained_respond_interpolant, trained_address_interpolant, trained_content_interpolant, trained_valve_interpolant, trained_respond, trained_address, trained_content, trained_valve)
        fading_logscale = -jnp.exp(trained_damping).reshape(subgroup_total, LANE_FEATURES)
        recurrent_accumulator = jnp.zeros((MICROBATCHES, subgroup_total, LANE_FEATURES, LANE_FEATURES), jnp.float32)
        joined_subgroups = attention_recurrence_stream(acceptor_lines.reshape(split_layout), lookup_projection_lines.reshape(split_layout), payload_projection_lines.reshape(split_layout), reset_markers, fading_logscale, trained_immediate_boost.reshape(subgroup_total, LANE_FEATURES), recurrent_accumulator)[0]
        wkv_readout = blended_result_post(subgroup_total, joined_subgroups.reshape(MICROBATCHES, POSITIONS_EVERY, HIDDEN_BREADTH), valve_entries, trained_cluster_factor, trained_cluster_addend, trained_readout, ordered_positions)
        second = standardized_entries(wkv_readout, trained_posterior_factor, trained_posterior_addend, 1e-05)
        return channel_mix(keep_rows, second, zero_row, trained_dense_address_mixer, trained_dense_respond_mixer, trained_dense_address, trained_dense_content, trained_dense_respond, wkv_readout)
    evaluation_operands = (incoming_hidden.astype(jnp.float32), prior_standardize_factor, prior_standardize_addend, respond_interpolant, address_interpolant, content_interpolant, valve_interpolant, respond_transform.astype(jnp.float32), address_transform.astype(jnp.float32), content_transform.astype(jnp.float32), valve_transform.astype(jnp.float32), damping_rates, immediate_boost, cluster_normal_factor, cluster_normal_shift_term, readout_transform.astype(jnp.float32), posterior_standardize_factor, posterior_standardize_addend, dense_address_interpolant, dense_respond_interpolant, dense_address_transform.astype(jnp.float32), dense_content_transform.astype(jnp.float32), dense_respond_transform.astype(jnp.float32))
    result, pullback = jax.vjp(forward, evaluation_operands)
    gradients = pullback(objective_adjoint.astype(jnp.float32))[0]
    return (result.astype(jnp.bfloat16), gradients[0], gradients[1], gradients[2], gradients[3], gradients[4], gradients[5], gradients[6], gradients[7], gradients[8], gradients[9], gradients[10], gradients[11], gradients[12], gradients[13], gradients[14], gradients[15], gradients[16], gradients[17], gradients[18], gradients[19], gradients[20], gradients[21], gradients[22])
```

```python
import functools

import jax
import jax.numpy as jnp
from jax import lax
from jax.experimental import pallas as pl
from jax.experimental.pallas import tpu as pltpu
from jax.sharding import PartitionSpec as P

LANE_FEATURES = 64
PAIR = 2 * LANE_FEATURES
BLOCK = 256
f32 = jnp.float32
bf16 = jnp.bfloat16
VMEM_LIMIT = 60 * 1024 * 1024


def split(x):
    high = x.astype(bf16)
    return high, (x - high.astype(f32)).astype(bf16)


def dot(a, b):
    return lax.dot_general(a, b, (((1,), (0,)), ((), ())), preferred_element_type=f32)


def dot_nt(a, b):
    return lax.dot_general(a, b, (((1,), (1,)), ((), ())), preferred_element_type=f32)


def dot_tn(a, b):
    return lax.dot_general(a, b, (((0,), (0,)), ((), ())), preferred_element_type=f32)


def times_weight(x, w):
    high, low = split(x)
    return dot(high, w) + dot(low, w)


def times_weight_t(x, w):
    high, low = split(x)
    return dot_nt(high, w) + dot_nt(low, w)


def outer_sum(a, b):
    ah, al = split(a)
    bh, bl = split(b)
    return dot_tn(ah, bh) + dot_tn(al, bh) + dot_tn(ah, bl)


def standard(x, epsilon=1e-05):
    centred = x - jnp.mean(x, axis=-1, keepdims=True)
    scale = lax.rsqrt(jnp.mean(centred * centred, axis=-1, keepdims=True) + epsilon)
    return centred * scale, scale


def standard_back(grad, normal, scale):
    return scale * (
        grad
        - jnp.mean(grad, axis=-1, keepdims=True)
        - normal * jnp.mean(grad * normal, axis=-1, keepdims=True)
    )


def first_lanes(rows):
    return lax.broadcasted_iota(jnp.int32, (rows, PAIR), 1) < LANE_FEATURES


def head_ones(scale):
    row = lax.broadcasted_iota(jnp.int32, (2 * PAIR, PAIR), 0) // LANE_FEATURES % 2
    col = lax.broadcasted_iota(jnp.int32, (2 * PAIR, PAIR), 1) // LANE_FEATURES
    return jnp.where(row == col, scale, 0.0).astype(bf16)


def head_sum(x, ones):
    return dot(jnp.concatenate(split(x), axis=1), ones)


def widen(state):
    first = first_lanes(LANE_FEATURES)
    return jnp.concatenate([jnp.where(first, state, 0.0), jnp.where(first, 0.0, state)], axis=0)


def compact(square):
    first = first_lanes(LANE_FEATURES)
    return jnp.where(first, square[:LANE_FEATURES], square[LANE_FEATURES:])


def times_state(x, square):
    xh, xl = split(x)
    sh, sl = split(square)
    return dot(jnp.concatenate([xh, xl], axis=1), jnp.concatenate([sh, sh], axis=0)) + dot(xh, sl)


def times_state_t(x, square):
    xh, xl = split(x)
    sh, sl = split(square)
    return dot_nt(jnp.concatenate([xh, xl], axis=1), jnp.concatenate([sh, sh], axis=1)) + dot_nt(xh, sl)


def cut(x):
    high = x.astype(bf16).astype(f32)
    low = x - high
    return high, low, pltpu.roll(high, LANE_FEATURES, 1), pltpu.roll(low, LANE_FEATURES, 1)


def high_low(pieces, first, head):
    high, low, high_r, low_r = pieces
    return (jnp.where(first, high, low_r) if head == 0 else jnp.where(first, high_r, low)).astype(bf16)


def doubled(pieces, first, head):
    high, low, high_r, low_r = pieces
    if head == 0:
        both = (jnp.where(first, high, high_r), jnp.where(first, low, low_r))
    else:
        both = (jnp.where(first, high_r, high), jnp.where(first, low_r, low))
    return jnp.concatenate([part.astype(bf16) for part in both], axis=1)


def twice(x):
    return jnp.concatenate([x, x], axis=1)


def folded(parts, first):
    sums = [part + pltpu.roll(part, LANE_FEATURES, 1) for part in parts]
    return jnp.where(first, sums[0], sums[1])


def decays(log_decay):
    step = lax.broadcasted_iota(jnp.int32, (BLOCK, PAIR), 0).astype(f32)
    return step, jnp.exp(log_decay * step), jnp.exp(-log_decay * (step + 1.0)), jnp.exp(log_decay * BLOCK)


def shifted(normal, row_before, keep):
    rows = lax.broadcasted_iota(jnp.int32, normal.shape, 0)
    return jnp.where(rows == 0, row_before, pltpu.roll(normal, 1, 0)) * keep


def project_kernel(count, x_ref, before_ref, cols_ref, gain_ref, bias_ref, *refs):
    mixes, weights, outs = refs[:count], refs[count : 2 * count], refs[2 * count :]
    gain, bias = gain_ref[...], bias_ref[...]
    normal = standard(x_ref[0].astype(f32))[0] * gain + bias
    before = standard(before_ref[0])[0] * gain + bias
    earlier = shifted(normal, before, cols_ref[0, :, 1:2])
    difference = normal - earlier
    for mix, weight, out in zip(mixes, weights, outs):
        out[0] = times_weight(earlier + mix[...] * difference, weight[...])


def end_state_kernel(keys_ref, values_ref, cols_ref, decay_ref, out_ref):
    length = keys_ref.shape[1]
    rows = lax.broadcasted_iota(jnp.int32, (length, PAIR), 0).astype(f32)
    tail = jnp.exp(decay_ref[...] * (length - 1.0 - rows)) * cols_ref[0, :, 3:4]
    out_ref[0, 0] = compact(outer_sum(keys_ref[0] * tail, values_ref[0]))


def allowed_here(cols_ref, row_ref, at, of, across):
    t_col = cols_ref[0, pl.ds(at * BLOCK, BLOCK), 0:1]
    s_row = row_ref[0, :, pl.ds(of * BLOCK, BLOCK)]
    mask = t_col == s_row
    if at == of:
        shape = (BLOCK, BLOCK)
        low, high = (1, 0) if not across else (0, 1)
        mask = jnp.logical_and(
            mask,
            lax.broadcasted_iota(jnp.int32, shape, low) < lax.broadcasted_iota(jnp.int32, shape, high),
        )
    return mask


def mix_kernel(recept_ref, keys_ref, values_ref, cols_ref, row_ref, decay_ref, boost_ref, out_ref):
    length = recept_ref.shape[1]
    first = first_lanes(BLOCK)
    step, fall, rise, whole = decays(decay_ref[...])
    ones = head_ones(1.0)
    queries, near, far, values = [], [], [], []
    for at in range(length // BLOCK):
        here = pl.ds(at * BLOCK, BLOCK)
        queries.append(cut(recept_ref[0, here] * fall))
        raised = keys_ref[0, here] * rise
        near.append(cut(raised))
        far.append(raised * whole)
        values.append(cut(values_ref[0, here]))
    for at in range(length // BLOCK):
        here = pl.ds(at * BLOCK, BLOCK)
        totals = [jnp.zeros((BLOCK, PAIR), f32)] * 2
        for of in range(at + 1):
            mask = allowed_here(cols_ref, row_ref, at, of, False)
            keys = near[of] if of == at else cut(far[of] * jnp.exp(decay_ref[...] * (BLOCK * (at - of - 1))))
            for head in range(2):
                scores = dot_nt(twice(high_low(queries[at], first, head)), doubled(keys, first, head))
                sh, sl = split(jnp.where(mask, scores, 0.0))
                held = high_low(values[of], first, head)
                totals[head] = totals[head] + dot(sh, held) + dot(sl, held)
        present = head_sum(recept_ref[0, here] * boost_ref[...] * keys_ref[0, here], ones)
        out_ref[0, here] = folded(totals, first) + present * values_ref[0, here]


def readout_kernel(
    mixed_ref, recept_ref, state_ref, valve_ref, cols_ref, decay_ref, x_ref, gain_ref, shift_ref,
    weight_ref, gain2_ref, bias2_ref, wkv_ref, attended_ref, second_ref,
):
    length, width = mixed_ref.shape[1:]
    rows = lax.broadcasted_iota(jnp.int32, (length, PAIR), 0).astype(f32)
    ones = head_ones(1.0 / LANE_FEATURES)
    fresh = cols_ref[0, :, 2:3]
    gated = []
    for pair in range(width // PAIR):
        lanes = slice(pair * PAIR, (pair + 1) * PAIR)
        query = recept_ref[0, :, lanes] * jnp.exp(decay_ref[:, lanes] * rows) * fresh
        wkv = mixed_ref[0, :, lanes] + times_state(query, widen(state_ref[0, pair]))
        wkv_ref[0, :, lanes] = wkv
        centred = wkv - head_sum(wkv, ones)
        normal = centred * lax.rsqrt(head_sum(centred * centred, ones) + 0.00064)
        grouped = normal * gain_ref[:, lanes] + shift_ref[:, lanes]
        gated.append(grouped * jax.nn.silu(valve_ref[0, :, lanes]))
    attended = x_ref[0].astype(f32) + times_weight(jnp.concatenate(gated, axis=1), weight_ref[...])
    attended_ref[0] = attended
    second_ref[0] = standard(attended)[0] * gain2_ref[...] + bias2_ref[...]


def pieces_of(total):
    cuts, at = [], 0
    while at < total:
        size = min(768, total - at)
        cuts.append((at, size))
        at += size
    return cuts


def channel_kernel(
    second_ref, ahead_ref, received_ref, attended_ref, grad_ref, cols_ref, mix_e_ref, mix_f_ref,
    expand_ref, shrink_ref, filter_ref,
    block_ref, d_second_ref, d_row_ref, d_expand_ref, d_shrink_ref, d_filter_ref, d_mix_e_ref, d_mix_f_ref,
    hidden_ref, carry_ref,
):
    tiles = pl.num_programs(1)
    batch, turn = pl.program_id(0), pl.program_id(1)
    tile = tiles - 1 - turn
    start = jnp.logical_and(batch == 0, turn == 0)

    @pl.when(start)
    def _():
        d_expand_ref[...] = jnp.zeros_like(d_expand_ref)
        d_shrink_ref[...] = jnp.zeros_like(d_shrink_ref)
        d_filter_ref[...] = jnp.zeros_like(d_filter_ref)
        d_mix_e_ref[...] = jnp.zeros_like(d_mix_e_ref)
        d_mix_f_ref[...] = jnp.zeros_like(d_mix_f_ref)

    keep = cols_ref[0, :, 1:2]
    second = second_ref[0]
    before = jnp.where(tile == 0, received_ref[0], ahead_ref[0, 7:8])
    earlier = shifted(second, before, keep)
    difference = second - earlier
    inner = earlier + mix_e_ref[...] * difference
    inner_h, inner_l = split(inner)
    side = earlier + mix_f_ref[...] * difference
    side_h, side_l = split(side)
    width = hidden_ref.shape[1]
    total = jnp.zeros(second.shape, f32)
    for at, size in pieces_of(width):
        lanes = slice(at, at + size)
        raw = jnp.maximum(dot(inner_h, expand_ref[:, lanes]) + dot(inner_l, expand_ref[:, lanes]), 0.0)
        hidden_ref[:, lanes] = raw
        total = total + times_weight(raw * raw, shrink_ref[lanes, :])
    gate = jax.nn.sigmoid(dot(side_h, filter_ref[...]) + dot(side_l, filter_ref[...]))
    grad = grad_ref[0].astype(f32)
    block_ref[0] = (attended_ref[0] + gate * total).astype(bf16)
    d_total = grad * gate
    d_side_raw = grad * total * (gate * (1.0 - gate))
    dt_h, dt_l = split(d_total)
    ds_h, ds_l = split(d_side_raw)
    d_filter_ref[...] += dot_tn(side_h, ds_h) + dot_tn(side_l, ds_h) + dot_tn(side_h, ds_l)
    d_side = dot_nt(ds_h, filter_ref[...]) + dot_nt(ds_l, filter_ref[...])
    d_inner = jnp.zeros(second.shape, f32)
    for at, size in pieces_of(width):
        lanes = slice(at, at + size)
        raw = hidden_ref[:, lanes]
        hid_h, hid_l = split(raw * raw)
        d_hidden = dot_nt(dt_h, shrink_ref[lanes, :]) + dot_nt(dt_l, shrink_ref[lanes, :])
        dr_h, dr_l = split(d_hidden * (2.0 * raw))
        d_shrink_ref[lanes, :] += dot_tn(hid_h, dt_h) + dot_tn(hid_l, dt_h) + dot_tn(hid_h, dt_l)
        d_expand_ref[:, lanes] += dot_tn(inner_h, dr_h) + dot_tn(inner_l, dr_h) + dot_tn(inner_h, dr_l)
        d_inner = d_inner + dot_nt(dr_h, expand_ref[:, lanes]) + dot_nt(dr_l, expand_ref[:, lanes])
    d_mix_e_ref[...] += jnp.sum(d_inner * difference, axis=0, keepdims=True)
    d_mix_f_ref[...] += jnp.sum(d_side * difference, axis=0, keepdims=True)
    direct = mix_e_ref[...] * d_inner + mix_f_ref[...] * d_side
    passed = (d_inner + d_side - direct) * keep
    rows = lax.broadcasted_iota(jnp.int32, second.shape, 0)
    above = pltpu.roll(passed, second.shape[0] - 1, 0)
    outside = jnp.where(turn == 0, 0.0, carry_ref[...])
    d_second_ref[0] = direct + jnp.where(rows == second.shape[0] - 1, outside, above)
    carry_ref[...] = passed[0:1]
    d_row_ref[0] = passed[0:1]


def attention_back_kernel(
    d_second_ref, back_ref, attended_ref, grad_ref, wkv_ref, valve_ref, recept_ref, cols_ref, decay_ref,
    gain_ref, shift_ref, weight_ref, gain2_ref,
    d_attended_ref, d_wkv_ref, d_valve_ref, carry_ref, d_weight_ref, d_gain_ref, d_shift_ref, d_gain2_ref, d_bias2_ref,
):
    length, width = attended_ref.shape[1:]

    @pl.when(pl.program_id(0) == 0)
    def _():
        for ref in (d_weight_ref, d_gain_ref, d_shift_ref, d_gain2_ref, d_bias2_ref):
            ref[...] = jnp.zeros_like(ref)

    rows = lax.broadcasted_iota(jnp.int32, (length, width), 0)
    d_second = d_second_ref[0] + jnp.where(rows == length - 1, back_ref[0], 0.0)
    normal2, scale2 = standard(attended_ref[0])
    d_gain2_ref[...] += jnp.sum(d_second * normal2, axis=0, keepdims=True)
    d_bias2_ref[...] += jnp.sum(d_second, axis=0, keepdims=True)
    d_attended = grad_ref[0].astype(f32) + standard_back(d_second * gain2_ref[...], normal2, scale2)
    d_attended_ref[0] = d_attended
    d_gated = times_weight_t(d_attended, weight_ref[...])
    steps = lax.broadcasted_iota(jnp.int32, (length, PAIR), 0).astype(f32)
    ones = head_ones(1.0 / LANE_FEATURES)
    fresh = cols_ref[0, :, 2:3]
    gated = []
    for pair in range(width // PAIR):
        lanes = slice(pair * PAIR, (pair + 1) * PAIR)
        wkv = wkv_ref[0, :, lanes]
        centred = wkv - head_sum(wkv, ones)
        scale = lax.rsqrt(head_sum(centred * centred, ones) + 0.00064)
        normal = centred * scale
        grouped = normal * gain_ref[:, lanes] + shift_ref[:, lanes]
        valve = valve_ref[0, :, lanes]
        sigmoid = jax.nn.sigmoid(valve)
        gate = valve * sigmoid
        gated.append(grouped * gate)
        d_here = d_gated[:, lanes]
        d_valve_ref[0, :, lanes] = d_here * grouped * (sigmoid * (1.0 + valve * (1.0 - sigmoid)))
        d_grouped = d_here * gate
        d_gain_ref[:, lanes] += jnp.sum(d_grouped * normal, axis=0, keepdims=True)
        d_shift_ref[:, lanes] += jnp.sum(d_grouped, axis=0, keepdims=True)
        d_normal = d_grouped * gain_ref[:, lanes]
        d_wkv = scale * (d_normal - head_sum(d_normal, ones) - normal * head_sum(d_normal * normal, ones))
        d_wkv_ref[0, :, lanes] = d_wkv
        query = recept_ref[0, :, lanes] * jnp.exp(decay_ref[:, lanes] * steps) * fresh
        carry_ref[0, pair] = compact(outer_sum(query, d_wkv))
    d_weight_ref[...] += outer_sum(jnp.concatenate(gated, axis=1), d_attended)


def mix_back_kernel(
    recept_ref, keys_ref, values_ref, grad_ref, state_ref, cols_ref, row_ref, decay_ref, boost_ref,
    d_recept_ref, d_keys_ref, d_values_ref, d_decay_ref, d_boost_ref,
):
    length = recept_ref.shape[1]
    blocks = length // BLOCK
    first = first_lanes(BLOCK)
    log_decay = decay_ref[...]
    step, fall, rise, whole = decays(log_decay)
    ones = head_ones(1.0)
    square = widen(state_ref[0, 0])
    queries, near, far, values, grads = [], [], [], [], []
    for at in range(blocks):
        here = pl.ds(at * BLOCK, BLOCK)
        queries.append(cut(recept_ref[0, here] * fall))
        raised = keys_ref[0, here] * rise
        near.append(cut(raised))
        far.append(raised * whole)
        values.append(cut(values_ref[0, here]))
        grads.append(cut(grad_ref[0, here]))
    zero = jnp.zeros((BLOCK, PAIR), f32)
    d_query = [[zero, zero] for _ in range(blocks)]
    d_value = [[zero, zero] for _ in range(blocks)]
    d_near = [[zero, zero] for _ in range(blocks)]
    d_far = [[zero, zero] for _ in range(blocks)]
    for at in range(blocks):
        for of in range(at + 1):
            mask = allowed_here(cols_ref, row_ref, at, of, False)
            t_row = row_ref[0, :, pl.ds(at * BLOCK, BLOCK)]
            s_col = cols_ref[0, pl.ds(of * BLOCK, BLOCK), 0:1]
            mask_t = s_col == t_row
            if at == of:
                shape = (BLOCK, BLOCK)
                mask_t = jnp.logical_and(
                    mask_t, lax.broadcasted_iota(jnp.int32, shape, 0) < lax.broadcasted_iota(jnp.int32, shape, 1)
                )
            gap = jnp.exp(log_decay * (BLOCK * (at - of - 1))) if at > of + 1 else None
            keys = near[of] if of == at else cut(far[of] if gap is None else far[of] * gap)
            for head in range(2):
                q_hl = high_low(queries[at], first, head)
                g_hl = high_low(grads[at], first, head)
                k_hl = high_low(keys, first, head)
                v_hl = high_low(values[of], first, head)
                scores_t = dot_nt(twice(k_hl), doubled(queries[at], first, head))
                s_h, s_l = split(jnp.where(mask_t, scores_t, 0.0))
                d_value[of][head] = d_value[of][head] + dot(s_h, g_hl) + dot(s_l, g_hl)
                d_scores = dot_nt(twice(g_hl), doubled(values[of], first, head))
                s_h, s_l = split(jnp.where(mask, d_scores, 0.0))
                d_query[at][head] = d_query[at][head] + dot(s_h, k_hl) + dot(s_l, k_hl)
                d_scores_t = dot_nt(twice(v_hl), doubled(grads[at], first, head))
                s_h, s_l = split(jnp.where(mask_t, d_scores_t, 0.0))
                d_key = dot(s_h, q_hl) + dot(s_l, q_hl)
                if of == at:
                    d_near[of][head] = d_key
                else:
                    if gap is not None:
                        d_key = d_key * gap
                    d_far[of][head] = d_far[of][head] + d_key
    d_decay = jnp.zeros((1, PAIR), f32)
    d_boost = jnp.zeros((1, PAIR), f32)
    for at in range(blocks):
        here = pl.ds(at * BLOCK, BLOCK)
        recept, keys, value, grad = recept_ref[0, here], keys_ref[0, here], values_ref[0, here], grad_ref[0, here]
        fresh = cols_ref[0, here, 2:3]
        d_in = folded(d_query[at], first) * fall
        d_state = times_state_t(grad, square) * (fall * jnp.exp(log_decay * (BLOCK * at)) * fresh)
        d_here = folded(d_near[at], first) * rise
        d_later = folded(d_far[at], first) * (rise * whole)
        boost = boost_ref[...]
        present = head_sum(recept * boost * keys, ones)
        d_present = head_sum(grad * value, ones)
        d_recept_ref[0, here] = d_in + d_state + boost * keys * d_present
        d_keys_ref[0, here] = d_here + d_later + boost * recept * d_present
        d_values_ref[0, here] = folded(d_value[at], first) + present * grad
        d_boost = d_boost + jnp.sum(recept * keys * d_present, axis=0, keepdims=True)
        d_decay = d_decay + jnp.sum(
            recept * (step * d_in + (step + float(BLOCK * at)) * d_state)
            + keys * ((BLOCK - 1.0 - step) * d_later - (step + 1.0) * d_here),
            axis=0,
            keepdims=True,
        )
    d_decay_ref[0] = d_decay
    d_boost_ref[0] = d_boost


def project_back_kernel(
    x_ref, before_ref, cols_ref, gain_ref, bias_ref, d_attended_ref,
    d_recept_ref, d_keys_ref, d_values_ref, d_valve_ref, keys_ref, values_ref, out_state_ref, decay_ref,
    mix_r, mix_k, mix_v, mix_g, w_r, w_k, w_v, w_g,
    d_x_ref, d_row_ref, d_gain_ref, d_bias_ref, d_decay_ref,
    dm_r, dm_k, dm_v, dm_g, dw_r, dw_k, dw_v, dw_g,
):
    length, width = x_ref.shape[1:]

    @pl.when(pl.program_id(0) == 0)
    def _():
        for ref in (d_gain_ref, d_bias_ref, d_decay_ref, dm_r, dm_k, dm_v, dm_g, dw_r, dw_k, dw_v, dw_g):
            ref[...] = jnp.zeros_like(ref)

    last = cols_ref[0, :, 3:4]
    steps = lax.broadcasted_iota(jnp.int32, (length, PAIR), 0).astype(f32)
    keys_part, values_part = [], []
    for pair in range(width // PAIR):
        lanes = slice(pair * PAIR, (pair + 1) * PAIR)
        keys = keys_ref[0, :, lanes]
        tail = jnp.exp(decay_ref[:, lanes] * (length - 1.0 - steps)) * last
        square = widen(out_state_ref[0, pair])
        d_keys = times_state_t(values_ref[0, :, lanes], square) * tail
        d_decay_ref[:, lanes] += jnp.sum((length - 1.0 - steps) * keys * d_keys, axis=0, keepdims=True)
        keys_part.append(d_keys_ref[0, :, lanes] + d_keys)
        values_part.append(d_values_ref[0, :, lanes] + times_state(keys * tail, square))
    d_keys = jnp.concatenate(keys_part, axis=1)
    d_values = jnp.concatenate(values_part, axis=1)
    gain, bias, keep = gain_ref[...], bias_ref[...], cols_ref[0, :, 1:2]
    hat, scale = standard(x_ref[0].astype(f32))
    normal = hat * gain + bias
    before = standard(before_ref[0])[0] * gain + bias
    earlier = shifted(normal, before, keep)
    difference = normal - earlier
    direct = jnp.zeros((length, width), f32)
    passed = jnp.zeros((length, width), f32)
    for grad, mix_ref, weight, d_mix, d_weight in (
        (d_recept_ref[0], mix_r, w_r, dm_r, dw_r),
        (d_keys, mix_k, w_k, dm_k, dw_k),
        (d_values, mix_v, w_v, dm_v, dw_v),
        (d_valve_ref[0], mix_g, w_g, dm_g, dw_g),
    ):
        mix = mix_ref[...]
        gh, gl = split(grad)
        mh, ml = split(earlier + mix * difference)
        d_weight[...] += dot_tn(mh, gh) + dot_tn(ml, gh) + dot_tn(mh, gl)
        d_mixed = dot_nt(gh, weight[...]) + dot_nt(gl, weight[...])
        d_mix[...] += jnp.sum(d_mixed * difference, axis=0, keepdims=True)
        direct = direct + mix * d_mixed
        passed = passed + (d_mixed - mix * d_mixed)
    passed = passed * keep
    d_row_ref[0] = passed[0:1]
    rows = lax.broadcasted_iota(jnp.int32, (length, width), 0)
    d_normal = direct + jnp.where(rows == length - 1, 0.0, pltpu.roll(passed, length - 1, 0))
    d_gain_ref[...] += jnp.sum(d_normal * hat, axis=0, keepdims=True)
    d_bias_ref[...] += jnp.sum(d_normal, axis=0, keepdims=True)
    d_x_ref[0] = d_attended_ref[0] + standard_back(d_normal * gain, hat, scale)


def call(kernel, grid, ins, outs, name, scratch=(), flops=0, transcendentals=0):
    bytes_accessed = sum(a.size * a.dtype.itemsize for a, _, _ in ins)
    for shape, dtype, _, _ in outs:
        size = jnp.dtype(dtype).itemsize
        for extent in shape:
            size *= extent
        bytes_accessed += size

    def spec(block, index):
        steady = index is None
        at = (lambda *_: (0,) * len(block)) if steady else index
        if steady:
            return pl.BlockSpec(block, at, pipeline_mode=pl.Buffered(1))
        return pl.BlockSpec(block, at)

    return pl.pallas_call(
        kernel,
        grid=grid,
        in_specs=[spec(block, index) for _, block, index in ins],
        out_specs=[spec(block, index) for _, _, block, index in outs],
        out_shape=[jax.ShapeDtypeStruct(shape, dtype) for shape, dtype, _, _ in outs],
        scratch_shapes=list(scratch),
        compiler_params=pltpu.CompilerParams(
            dimension_semantics=("arbitrary",) * len(grid), vmem_limit_bytes=VMEM_LIMIT
        ),
        cost_estimate=pl.CostEstimate(
            flops=flops, bytes_accessed=bytes_accessed, transcendentals=transcendentals
        ),
        name=name,
    )(*[a for a, _, _ in ins])


def moved(value, steps):
    count = lax.axis_size("seq")
    low, high = max(0, -steps), min(count, count - steps)
    return lax.ppermute(value, "seq", [(source, source + steps) for source in range(low, high)])


def reach(count):
    factors, window, needed = [], 1, {32: 16, 128: 32}.get(count, count)
    while window < needed:
        factor = min(4, needed // window)
        factors.append(factor)
        window *= factor
    return factors


def carried(value, log_state, bounds, length, sign):
    count, mine = lax.axis_size("seq"), lax.axis_index("seq")

    def segment(device):
        return jnp.sum((device * length - 1 >= bounds).astype(jnp.int32), axis=1)

    here = segment(mine) if sign > 0 else segment(mine + 1)
    total, window = value, 1
    for turn, factor in enumerate(reach(count)):
        fresh = None if turn == 0 else total
        for piece in range(1, factor + 1 if turn == 0 else factor):
            hops = piece * window
            crossed = hops - 1 if turn == 0 else hops
            got = moved(total, sign * hops)
            if turn == 0:
                there = segment(mine - hops + 1) if sign > 0 else segment(mine + hops)
            else:
                there = segment(mine - hops) if sign > 0 else segment(mine + 1 + hops)
            factor_here = (there == here).astype(f32)[:, None, None, None] * jnp.exp(log_state * float(length * crossed))[None]
            part = got * factor_here
            fresh = part if fresh is None else fresh + part
        total, window = fresh, window * factor
    return total


def local(
    incoming_hidden,
    packed_run_lengths,
    prior_standardize_factor,
    prior_standardize_addend,
    respond_interpolant,
    address_interpolant,
    content_interpolant,
    valve_interpolant,
    respond_transform,
    address_transform,
    content_transform,
    valve_transform,
    damping_rates,
    immediate_boost,
    cluster_normal_factor,
    cluster_normal_shift_term,
    readout_transform,
    posterior_standardize_factor,
    posterior_standardize_addend,
    dense_address_interpolant,
    dense_respond_interpolant,
    dense_address_transform,
    dense_content_transform,
    dense_respond_transform,
    objective_adjoint,
):
    batches, length, width = incoming_hidden.shape
    hidden_width = dense_address_transform.shape[1]
    pairs = width // PAIR
    offset = lax.axis_index("seq") * length
    lengths = packed_run_lengths
    earlier_than = jnp.arange(lengths.shape[1])[:, None] < jnp.arange(lengths.shape[1])[None, :]
    bounds = jnp.sum(jnp.where(earlier_than[None], lengths[:, :, None], 0), axis=1)
    positions = offset + jnp.arange(length, dtype=jnp.int32)

    def segments(at):
        return jnp.sum((at[None, :, None] >= bounds[:, None, :]).astype(jnp.int32), axis=2)

    segment = segments(positions)
    starts = jnp.any(positions[None, :, None] == bounds[:, None, :], axis=2)
    fresh = segment == segments(offset[None] - 1)
    last = segment == segments(offset[None] + length - 1)
    zeros = jnp.zeros((batches, length), f32)
    cols = jnp.stack(
        [segment.astype(f32), 1.0 - starts.astype(f32), fresh.astype(f32), last.astype(f32)] + [zeros] * 4, axis=2
    )
    row = segment.astype(f32)[:, None, :]
    log_decay = -jnp.exp(damping_rates)
    by_head = log_decay.reshape(pairs, 2, LANE_FEATURES)
    log_state = jnp.repeat(by_head.transpose(0, 2, 1), LANE_FEATURES, axis=2)

    def vector(v):
        return (v.reshape(1, width), (1, width), None)

    def table(w):
        return (w, w.shape, None)

    def rows_of(a):
        return (a, (1,) + a.shape[1:], lambda b: (b,) + (0,) * (a.ndim - 1))

    def rows_out(shape, dtype=f32):
        return (shape, dtype, (1,) + tuple(shape[1:]), lambda b: (b,) + (0,) * (len(shape) - 1))

    def sum_out(*shape):
        return (shape, f32, shape, None)

    tokens = (batches, length, width)
    square_flops = 2 * batches * length * width * width
    before = moved(incoming_hidden[:, -1, :].astype(f32), 1)[:, None, :]
    common = [rows_of(incoming_hidden), rows_of(before), rows_of(cols), vector(prior_standardize_factor), vector(prior_standardize_addend)]

    def project(mixes, weights, name):
        return call(
            functools.partial(project_kernel, len(mixes)),
            (batches,),
            common + [vector(m) for m in mixes] + [table(w) for w in weights],
            [rows_out(tokens)] * len(mixes),
            name,
            flops=2 * len(mixes) * square_flops,
        )

    keys, values = project(
        [address_interpolant, content_interpolant], [address_transform, content_transform], "project_keys"
    )
    by_pair = lambda a: (a, (1, length, PAIR), lambda b, p: (b, 0, p))
    pair_vector = lambda v: (v.reshape(1, width), (1, PAIR), lambda b, p: (0, p))
    pair_cols = (cols, (1, length, cols.shape[2]), lambda b, p: (b, 0, 0))
    pair_row = (row, (1, 1, length), lambda b, p: (b, 0, 0))
    pair_state = lambda s: (s, (1, 1, LANE_FEATURES, PAIR), lambda b, p: (b, p, 0, 0))
    pair_out = (tokens, f32, (1, length, PAIR), lambda b, p: (b, 0, p))
    states = (batches, pairs, LANE_FEATURES, PAIR)
    end_state = call(
        end_state_kernel,
        (batches, pairs),
        [by_pair(keys), by_pair(values), pair_cols, pair_vector(log_decay)],
        [(states, f32, (1, 1, LANE_FEATURES, PAIR), lambda b, p: (b, p, 0, 0))],
        "end_state",
        flops=3 * 2 * batches * length * width * PAIR,
    )[0]
    state = carried(end_state, log_state, bounds, length, 1)
    recept, valve = project(
        [respond_interpolant, valve_interpolant], [respond_transform, valve_transform], "project_recept"
    )
    mixed = call(
        mix_kernel,
        (batches, pairs),
        [by_pair(recept), by_pair(keys), by_pair(values), pair_cols, pair_row, pair_vector(log_decay), pair_vector(immediate_boost)],
        [pair_out],
        "mix",
        flops=3 * 2 * batches * length * length * width * 2,
    )[0]
    wkv, attended, second = call(
        readout_kernel,
        (batches,),
        [
            rows_of(mixed), rows_of(recept), rows_of(state), rows_of(valve), rows_of(cols), vector(log_decay),
            rows_of(incoming_hidden), vector(cluster_normal_factor), vector(cluster_normal_shift_term),
            table(readout_transform), vector(posterior_standardize_factor), vector(posterior_standardize_addend),
        ],
        [rows_out(tokens)] * 3,
        "readout",
        flops=2 * square_flops,
    )
    second_row = moved(second[:, -1, :], 1)[:, None, :]
    tiles = length // BLOCK
    tile_rows = lambda a: (a, (1, BLOCK, a.shape[2]), lambda b, i: (b, tiles - 1 - i, 0))
    ahead = (second, (1, 8, width), lambda b, i: (b, jnp.maximum((tiles - 1 - i) * (BLOCK // 8) - 1, 0), 0))
    row_in = lambda a: (a, (1, 1, width), lambda b, i: (b, 0, 0))
    tile_out = lambda dtype: (tokens, dtype, (1, BLOCK, width), lambda b, i: (b, tiles - 1 - i, 0))
    (
        block, d_second, d_second_row, grad_expand, grad_shrink, grad_filter, grad_mix_expand, grad_mix_filter,
    ) = call(
        channel_kernel,
        (batches, tiles),
        [
            tile_rows(second), ahead, row_in(second_row), tile_rows(attended), tile_rows(objective_adjoint),
            tile_rows(cols), vector(dense_address_interpolant), vector(dense_respond_interpolant),
            table(dense_address_transform), table(dense_content_transform), table(dense_respond_transform),
        ],
        [
            tile_out(bf16), tile_out(f32), ((batches, 1, width), f32, (1, 1, width), lambda b, i: (b, 0, 0)),
            sum_out(width, hidden_width), sum_out(hidden_width, width), sum_out(width, width),
            sum_out(1, width), sum_out(1, width),
        ],
        "channel",
        scratch=[pltpu.VMEM((BLOCK, hidden_width), f32), pltpu.VMEM((1, width), f32)],
        flops=7 * 2 * batches * length * width * (2 * hidden_width + width),
    )
    back_second = moved(d_second_row[:, 0, :], -1)[:, None, :]
    (
        d_attended, d_wkv, d_valve, carry, grad_output, grad_group_gain, grad_group_bias, grad_second_gain, grad_second_bias,
    ) = call(
        attention_back_kernel,
        (batches,),
        [
            rows_of(d_second), rows_of(back_second), rows_of(attended), rows_of(objective_adjoint), rows_of(wkv),
            rows_of(valve), rows_of(recept), rows_of(cols), vector(log_decay), vector(cluster_normal_factor),
            vector(cluster_normal_shift_term), table(readout_transform), vector(posterior_standardize_factor),
        ],
        [rows_out(tokens), rows_out(tokens), rows_out(tokens), rows_out(states), sum_out(width, width)]
        + [sum_out(1, width)] * 4,
        "attention_back",
        flops=5 * square_flops,
    )
    out_state = carried(carry, log_state, bounds, length, -1)
    by_batch = lambda: ((batches, 1, width), f32, (1, 1, PAIR), lambda b, p: (b, 0, p))
    d_recept, d_keys, d_values, decay_part, boost_part = call(
        mix_back_kernel,
        (batches, pairs),
        [
            by_pair(recept), by_pair(keys), by_pair(values), by_pair(d_wkv), pair_state(state), pair_cols, pair_row,
            pair_vector(log_decay), pair_vector(immediate_boost),
        ],
        [pair_out, pair_out, pair_out, by_batch(), by_batch()],
        "mix_back",
        flops=9 * 2 * batches * length * length * width * 2,
    )
    (
        d_x, d_first_row, grad_first_gain, grad_first_bias, decay_end,
        grad_mix_recept, grad_mix_keys, grad_mix_values, grad_mix_gate,
        grad_recept, grad_keys, grad_values, grad_gate_w,
    ) = call(
        project_back_kernel,
        (batches,),
        common
        + [
            rows_of(d_attended), rows_of(d_recept), rows_of(d_keys), rows_of(d_values), rows_of(d_valve),
            rows_of(keys), rows_of(values), rows_of(out_state), vector(log_decay),
        ]
        + [vector(m) for m in (respond_interpolant, address_interpolant, content_interpolant, valve_interpolant)]
        + [table(w) for w in (respond_transform, address_transform, content_transform, valve_transform)],
        [rows_out(tokens), rows_out((batches, 1, width))] + [sum_out(1, width)] * 7 + [sum_out(width, width)] * 4,
        "project_back",
        flops=5 * 4 * square_flops,
    )
    back_first = moved(d_first_row[:, 0, :], -1)
    hat, scale = standard(incoming_hidden[:, -1, :].astype(f32))
    grad_first_gain = grad_first_gain[0] + jnp.sum(back_first * hat, axis=0)
    grad_first_bias = grad_first_bias[0] + jnp.sum(back_first, axis=0)
    grad_tokens = d_x.at[:, -1, :].add(standard_back(back_first * prior_standardize_factor, hat, scale))
    whole = (fresh[:, -1].astype(f32)[:, None, None, None] * jnp.exp(log_state * float(length))[None]) * state * out_state
    per_channel = jnp.sum(whole.reshape(batches, pairs, LANE_FEATURES, 2, LANE_FEATURES), axis=(0, 4))
    per_channel = per_channel.transpose(0, 2, 1).reshape(width) * float(length)
    grad_decay = (jnp.sum(decay_part[:, 0], axis=0) + decay_end[0] + per_channel) * log_decay
    grad_boost = jnp.sum(boost_part[:, 0], axis=0)
    summed = lax.psum(
        (
            grad_first_gain, grad_first_bias, grad_mix_recept[0], grad_mix_keys[0], grad_mix_values[0], grad_mix_gate[0],
            grad_recept, grad_keys, grad_values, grad_gate_w, grad_decay, grad_boost, grad_group_gain[0],
            grad_group_bias[0], grad_output, grad_second_gain[0], grad_second_bias[0], grad_mix_expand[0],
            grad_mix_filter[0], grad_expand, grad_shrink, grad_filter,
        ),
        "seq",
    )
    return (block, grad_tokens) + tuple(summed)


def solution(mesh):
    rows = P(None, "seq", None)
    return jax.shard_map(
        local,
        mesh=mesh,
        in_specs=(rows,) + (P(),) * 23 + (rows,),
        out_specs=(rows, rows) + (P(),) * 22,
        check_vma=False,
    )
```

```python
import functools

import jax
import jax.numpy as jnp
from jax import lax
from jax.experimental import pallas as pl
from jax.experimental.pallas import tpu as pltpu
from jax.sharding import PartitionSpec as P

LANE_FEATURES = 64
PAIR = 2 * LANE_FEATURES
BLOCK = 256
f32 = jnp.float32
bf16 = jnp.bfloat16
VMEM_LIMIT = 60 * 1024 * 1024
MESH = pl.DeviceIdType.MESH


def split(x):
    high = x.astype(bf16)
    return high, (x - high.astype(f32)).astype(bf16)


def dot(a, b):
    return lax.dot_general(a, b, (((1,), (0,)), ((), ())), preferred_element_type=f32)


def dot_nt(a, b):
    return lax.dot_general(a, b, (((1,), (1,)), ((), ())), preferred_element_type=f32)


def dot_tn(a, b):
    return lax.dot_general(a, b, (((0,), (0,)), ((), ())), preferred_element_type=f32)


def times_weight(x, w):
    high, low = split(x)
    return dot(high, w) + dot(low, w)


def times_weight_t(x, w):
    high, low = split(x)
    return dot_nt(high, w) + dot_nt(low, w)


def outer_sum(a, b):
    ah, al = split(a)
    bh, bl = split(b)
    return dot_tn(ah, bh) + dot_tn(al, bh) + dot_tn(ah, bl)


def standard(x, epsilon=1e-05):
    centred = x - jnp.mean(x, axis=-1, keepdims=True)
    scale = lax.rsqrt(jnp.mean(centred * centred, axis=-1, keepdims=True) + epsilon)
    return centred * scale, scale


def standard_back(grad, normal, scale):
    return scale * (
        grad
        - jnp.mean(grad, axis=-1, keepdims=True)
        - normal * jnp.mean(grad * normal, axis=-1, keepdims=True)
    )


def first_lanes(rows):
    return lax.broadcasted_iota(jnp.int32, (rows, PAIR), 1) < LANE_FEATURES


def head_ones(scale):
    row = lax.broadcasted_iota(jnp.int32, (2 * PAIR, PAIR), 0) // LANE_FEATURES % 2
    col = lax.broadcasted_iota(jnp.int32, (2 * PAIR, PAIR), 1) // LANE_FEATURES
    return jnp.where(row == col, scale, 0.0).astype(bf16)


def head_sum(x, ones):
    return dot(jnp.concatenate(split(x), axis=1), ones)


def widen(state):
    first = first_lanes(LANE_FEATURES)
    return jnp.concatenate([jnp.where(first, state, 0.0), jnp.where(first, 0.0, state)], axis=0)


def compact(square):
    first = first_lanes(LANE_FEATURES)
    return jnp.where(first, square[:LANE_FEATURES], square[LANE_FEATURES:])


def times_state(x, square):
    xh, xl = split(x)
    sh, sl = split(square)
    return dot(jnp.concatenate([xh, xl], axis=1), jnp.concatenate([sh, sh], axis=0)) + dot(xh, sl)


def times_state_t(x, square):
    xh, xl = split(x)
    sh, sl = split(square)
    return dot_nt(jnp.concatenate([xh, xl], axis=1), jnp.concatenate([sh, sh], axis=1)) + dot_nt(xh, sl)


def cut(x):
    high = x.astype(bf16).astype(f32)
    low = x - high
    return high, low, pltpu.roll(high, LANE_FEATURES, 1), pltpu.roll(low, LANE_FEATURES, 1)


def high_low(pieces, first, head):
    high, low, high_r, low_r = pieces
    return (jnp.where(first, high, low_r) if head == 0 else jnp.where(first, high_r, low)).astype(bf16)


def doubled(pieces, first, head):
    high, low, high_r, low_r = pieces
    if head == 0:
        both = (jnp.where(first, high, high_r), jnp.where(first, low, low_r))
    else:
        both = (jnp.where(first, high_r, high), jnp.where(first, low_r, low))
    return jnp.concatenate([part.astype(bf16) for part in both], axis=1)


def twice(x):
    return jnp.concatenate([x, x], axis=1)


def folded(parts, first):
    sums = [part + pltpu.roll(part, LANE_FEATURES, 1) for part in parts]
    return jnp.where(first, sums[0], sums[1])


def decays(log_decay):
    step = lax.broadcasted_iota(jnp.int32, (BLOCK, PAIR), 0).astype(f32)
    return step, jnp.exp(log_decay * step), jnp.exp(-log_decay * (step + 1.0)), jnp.exp(log_decay * BLOCK)


def shifted(normal, row_before, keep):
    rows = lax.broadcasted_iota(jnp.int32, normal.shape, 0)
    return jnp.where(rows == 0, row_before, pltpu.roll(normal, 1, 0)) * keep


GAIN, BIAS, MIX_R, MIX_K, MIX_V, MIX_G, DECAY, BOOST, GROUP_GAIN, GROUP_SHIFT, GAIN2, BIAS2, MIX_E, MIX_F = range(14)


def vec(ref, which, lanes=slice(None)):
    return ref[which : which + 1, lanes]


def bounds_of(lengths_ref, batch):
    at, bounds = jnp.int32(0), []
    for j in range(lengths_ref.shape[1]):
        bounds.append(at)
        at = at + lengths_ref[batch, j]
    return bounds


def segment_of(bounds, position):
    return sum([(position >= bound).astype(jnp.int32) for bound in bounds])


def tokens_kernel(lengths_ref, cols_ref, row_ref):
    batches, length, columns = cols_ref.shape
    offset = lax.axis_index("seq") * length
    for batch in range(batches):
        bounds = bounds_of(lengths_ref, batch)
        place = offset + lax.broadcasted_iota(jnp.int32, (length, columns), 0)
        segment = segment_of(bounds, place)
        starts = functools.reduce(jnp.logical_or, [place == bound for bound in bounds])
        column = lax.broadcasted_iota(jnp.int32, (length, columns), 1)
        fresh = segment == segment_of(bounds, offset - 1)
        last = segment == segment_of(bounds, offset + length - 1)
        flag = jnp.where(column == 1, jnp.where(starts, 0, 1), jnp.where(column == 2, jnp.where(fresh, 1, 0), jnp.where(last, 1, 0)))
        cols_ref[batch] = jnp.where(column == 0, segment, flag).astype(f32)
        row_ref[batch] = segment_of(bounds, offset + lax.broadcasted_iota(jnp.int32, (1, length), 1)).astype(f32)


def project_kernel(mixes, states, x_ref, before_ref, cols_ref, vec_ref, *refs):
    count = len(mixes)
    weights, outs = refs[:count], refs[count : 2 * count]
    gain, bias = vec(vec_ref, GAIN), vec(vec_ref, BIAS)
    normal = standard(x_ref[0].astype(f32))[0] * gain + bias
    before = standard(before_ref[0])[0] * gain + bias
    earlier = shifted(normal, before, cols_ref[0, :, 1:2])
    difference = normal - earlier
    for mix, weight, out in zip(mixes, weights, outs):
        out[0] = times_weight(earlier + vec(vec_ref, mix) * difference, weight[...])
    if states:
        length, width = normal.shape
        keys, values, end_ref = outs[0], outs[1], refs[2 * count]
        rows = lax.broadcasted_iota(jnp.int32, (length, PAIR), 0).astype(f32)
        for pair in range(width // PAIR):
            lanes = slice(pair * PAIR, (pair + 1) * PAIR)
            tail = jnp.exp(vec(vec_ref, DECAY, lanes) * (length - 1.0 - rows)) * cols_ref[0, :, 3:4]
            end_ref[0, pair] = compact(outer_sum(keys[0, :, lanes] * tail, values[0, :, lanes]))


def allowed_here(cols_ref, row_ref, at, of, across):
    t_col = cols_ref[0, pl.ds(at * BLOCK, BLOCK), 0:1]
    s_row = row_ref[0, :, pl.ds(of * BLOCK, BLOCK)]
    mask = t_col == s_row
    if at == of:
        shape = (BLOCK, BLOCK)
        low, high = (1, 0) if not across else (0, 1)
        mask = jnp.logical_and(
            mask,
            lax.broadcasted_iota(jnp.int32, shape, low) < lax.broadcasted_iota(jnp.int32, shape, high),
        )
    return mask


def mix_kernel(recept_ref, keys_ref, values_ref, cols_ref, row_ref, vec_ref, out_ref):
    length = recept_ref.shape[1]
    log_decay, boost = vec(vec_ref, DECAY), vec(vec_ref, BOOST)
    first = first_lanes(BLOCK)
    step, fall, rise, whole = decays(log_decay)
    ones = head_ones(1.0)
    queries, near, far, values = [], [], [], []
    for at in range(length // BLOCK):
        here = pl.ds(at * BLOCK, BLOCK)
        queries.append(cut(recept_ref[0, here] * fall))
        raised = keys_ref[0, here] * rise
        near.append(cut(raised))
        far.append(raised * whole)
        values.append(cut(values_ref[0, here]))
    for at in range(length // BLOCK):
        here = pl.ds(at * BLOCK, BLOCK)
        totals = [jnp.zeros((BLOCK, PAIR), f32)] * 2
        for of in range(at + 1):
            mask = allowed_here(cols_ref, row_ref, at, of, False)
            gap = jnp.exp(log_decay * (BLOCK * (at - of - 1))) if at > of + 1 else None
            keys = near[of] if of == at else cut(far[of] if gap is None else far[of] * gap)
            for head in range(2):
                scores = dot_nt(twice(high_low(queries[at], first, head)), doubled(keys, first, head))
                sh, sl = split(jnp.where(mask, scores, 0.0))
                held = high_low(values[of], first, head)
                totals[head] = totals[head] + dot(sh, held) + dot(sl, held)
        present = head_sum(recept_ref[0, here] * boost * keys_ref[0, here], ones)
        out_ref[0, here] = folded(totals, first) + present * values_ref[0, here]


def readout_kernel(
    mixed_ref, recept_ref, state_ref, valve_ref, cols_ref, vec_ref, x_ref, weight_ref,
    wkv_ref, attended_ref, second_ref, last_ref,
):
    length, width = mixed_ref.shape[1:]
    rows = lax.broadcasted_iota(jnp.int32, (length, PAIR), 0).astype(f32)
    ones = head_ones(1.0 / LANE_FEATURES)
    fresh = cols_ref[0, :, 2:3]
    gated = []
    for pair in range(width // PAIR):
        lanes = slice(pair * PAIR, (pair + 1) * PAIR)
        query = recept_ref[0, :, lanes] * jnp.exp(vec(vec_ref, DECAY, lanes) * rows) * fresh
        wkv = mixed_ref[0, :, lanes] + times_state(query, widen(state_ref[0, pair]))
        wkv_ref[0, :, lanes] = wkv
        centred = wkv - head_sum(wkv, ones)
        normal = centred * lax.rsqrt(head_sum(centred * centred, ones) + 0.00064)
        grouped = normal * vec(vec_ref, GROUP_GAIN, lanes) + vec(vec_ref, GROUP_SHIFT, lanes)
        gated.append(grouped * jax.nn.silu(valve_ref[0, :, lanes]))
    attended = x_ref[0].astype(f32) + times_weight(jnp.concatenate(gated, axis=1), weight_ref[...])
    attended_ref[0] = attended
    second = standard(attended)[0] * vec(vec_ref, GAIN2) + vec(vec_ref, BIAS2)
    second_ref[0] = second
    last_ref[0] = second[length - 1 :]


def pieces_of(total):
    cuts, at = [], 0
    while at < total:
        size = min(768, total - at)
        cuts.append((at, size))
        at += size
    return cuts


def channel_kernel(
    second_ref, ahead_ref, received_ref, attended_ref, grad_ref, cols_ref, vec_ref,
    expand_ref, shrink_ref, filter_ref,
    block_ref, d_second_ref, d_row_ref, d_expand_ref, d_shrink_ref, d_filter_ref, d_vec_ref,
    hidden_ref, carry_ref,
):
    tiles = pl.num_programs(1)
    batch, turn = pl.program_id(0), pl.program_id(1)
    tile = tiles - 1 - turn
    start = jnp.logical_and(batch == 0, turn == 0)

    @pl.when(start)
    def _():
        d_expand_ref[...] = jnp.zeros_like(d_expand_ref)
        d_shrink_ref[...] = jnp.zeros_like(d_shrink_ref)
        d_filter_ref[...] = jnp.zeros_like(d_filter_ref)
        d_vec_ref[...] = jnp.zeros_like(d_vec_ref)

    keep = cols_ref[0, :, 1:2]
    second = second_ref[0]
    before = jnp.where(tile == 0, received_ref[0], ahead_ref[0, 7:8])
    earlier = shifted(second, before, keep)
    difference = second - earlier
    mix_e, mix_f = vec(vec_ref, MIX_E), vec(vec_ref, MIX_F)
    inner = earlier + mix_e * difference
    inner_h, inner_l = split(inner)
    side = earlier + mix_f * difference
    side_h, side_l = split(side)
    width = hidden_ref.shape[1]
    total = jnp.zeros(second.shape, f32)
    for at, size in pieces_of(width):
        lanes = slice(at, at + size)
        raw = jnp.maximum(dot(inner_h, expand_ref[:, lanes]) + dot(inner_l, expand_ref[:, lanes]), 0.0)
        hidden_ref[:, lanes] = raw
        total = total + times_weight(raw * raw, shrink_ref[lanes, :])
    gate = jax.nn.sigmoid(dot(side_h, filter_ref[...]) + dot(side_l, filter_ref[...]))
    grad = grad_ref[0].astype(f32)
    block_ref[0] = (attended_ref[0] + gate * total).astype(bf16)
    d_total = grad * gate
    d_side_raw = grad * total * (gate * (1.0 - gate))
    dt_h, dt_l = split(d_total)
    ds_h, ds_l = split(d_side_raw)
    d_filter_ref[...] += dot_tn(side_h, ds_h) + dot_tn(side_l, ds_h) + dot_tn(side_h, ds_l)
    d_side = dot_nt(ds_h, filter_ref[...]) + dot_nt(ds_l, filter_ref[...])
    d_inner = jnp.zeros(second.shape, f32)
    for at, size in pieces_of(width):
        lanes = slice(at, at + size)
        raw = hidden_ref[:, lanes]
        hid_h, hid_l = split(raw * raw)
        d_hidden = dot_nt(dt_h, shrink_ref[lanes, :]) + dot_nt(dt_l, shrink_ref[lanes, :])
        dr_h, dr_l = split(d_hidden * (2.0 * raw))
        d_shrink_ref[lanes, :] += dot_tn(hid_h, dt_h) + dot_tn(hid_l, dt_h) + dot_tn(hid_h, dt_l)
        d_expand_ref[:, lanes] += dot_tn(inner_h, dr_h) + dot_tn(inner_l, dr_h) + dot_tn(inner_h, dr_l)
        d_inner = d_inner + dot_nt(dr_h, expand_ref[:, lanes]) + dot_nt(dr_l, expand_ref[:, lanes])
    d_vec_ref[0:1] += jnp.sum(d_inner * difference, axis=0, keepdims=True)
    d_vec_ref[1:2] += jnp.sum(d_side * difference, axis=0, keepdims=True)
    direct = mix_e * d_inner + mix_f * d_side
    passed = (d_inner + d_side - direct) * keep
    rows = lax.broadcasted_iota(jnp.int32, second.shape, 0)
    above = pltpu.roll(passed, second.shape[0] - 1, 0)
    outside = jnp.where(turn == 0, 0.0, carry_ref[...])
    d_second_ref[0] = direct + jnp.where(rows == second.shape[0] - 1, outside, above)
    carry_ref[...] = passed[0:1]
    d_row_ref[0] = passed[0:1]


def attention_back_kernel(
    d_second_ref, back_ref, attended_ref, grad_ref, wkv_ref, valve_ref, recept_ref, cols_ref, vec_ref, weight_ref,
    d_attended_ref, d_wkv_ref, d_valve_ref, carry_ref, d_weight_ref, d_vec_ref,
):
    length, width = attended_ref.shape[1:]

    @pl.when(pl.program_id(0) == 0)
    def _():
        for ref in (d_weight_ref, d_vec_ref):
            ref[...] = jnp.zeros_like(ref)

    rows = lax.broadcasted_iota(jnp.int32, (length, width), 0)
    d_second = d_second_ref[0] + jnp.where(rows == length - 1, back_ref[0], 0.0)
    normal2, scale2 = standard(attended_ref[0])
    d_vec_ref[2:3] += jnp.sum(d_second * normal2, axis=0, keepdims=True)
    d_vec_ref[3:4] += jnp.sum(d_second, axis=0, keepdims=True)
    d_attended = grad_ref[0].astype(f32) + standard_back(d_second * vec(vec_ref, GAIN2), normal2, scale2)
    d_attended_ref[0] = d_attended
    d_gated = times_weight_t(d_attended, weight_ref[...])
    steps = lax.broadcasted_iota(jnp.int32, (length, PAIR), 0).astype(f32)
    ones = head_ones(1.0 / LANE_FEATURES)
    fresh = cols_ref[0, :, 2:3]
    gated = []
    for pair in range(width // PAIR):
        lanes = slice(pair * PAIR, (pair + 1) * PAIR)
        wkv = wkv_ref[0, :, lanes]
        centred = wkv - head_sum(wkv, ones)
        scale = lax.rsqrt(head_sum(centred * centred, ones) + 0.00064)
        normal = centred * scale
        grouped = normal * vec(vec_ref, GROUP_GAIN, lanes) + vec(vec_ref, GROUP_SHIFT, lanes)
        valve = valve_ref[0, :, lanes]
        sigmoid = jax.nn.sigmoid(valve)
        gate = valve * sigmoid
        gated.append(grouped * gate)
        d_here = d_gated[:, lanes]
        d_valve_ref[0, :, lanes] = d_here * grouped * (sigmoid * (1.0 + valve * (1.0 - sigmoid)))
        d_grouped = d_here * gate
        d_vec_ref[0:1, lanes] += jnp.sum(d_grouped * normal, axis=0, keepdims=True)
        d_vec_ref[1:2, lanes] += jnp.sum(d_grouped, axis=0, keepdims=True)
        d_normal = d_grouped * vec(vec_ref, GROUP_GAIN, lanes)
        d_wkv = scale * (d_normal - head_sum(d_normal, ones) - normal * head_sum(d_normal * normal, ones))
        d_wkv_ref[0, :, lanes] = d_wkv
        query = recept_ref[0, :, lanes] * jnp.exp(vec(vec_ref, DECAY, lanes) * steps) * fresh
        carry_ref[0, pair] = compact(outer_sum(query, d_wkv))
    d_weight_ref[...] += outer_sum(jnp.concatenate(gated, axis=1), d_attended)


def mix_back_kernel(
    recept_ref, keys_ref, values_ref, grad_ref, state_ref, cols_ref, row_ref, vec_ref,
    d_recept_ref, d_keys_ref, d_values_ref, d_vec_ref,
):
    length = recept_ref.shape[1]
    blocks = length // BLOCK
    first = first_lanes(BLOCK)
    log_decay, boost = vec(vec_ref, DECAY), vec(vec_ref, BOOST)
    step, fall, rise, whole = decays(log_decay)
    ones = head_ones(1.0)
    square = widen(state_ref[0, 0])
    queries, near, far, values, grads = [], [], [], [], []
    for at in range(blocks):
        here = pl.ds(at * BLOCK, BLOCK)
        queries.append(cut(recept_ref[0, here] * fall))
        raised = keys_ref[0, here] * rise
        near.append(cut(raised))
        far.append(raised * whole)
        values.append(cut(values_ref[0, here]))
        grads.append(cut(grad_ref[0, here]))
    zero = jnp.zeros((BLOCK, PAIR), f32)
    d_query = [[zero, zero] for _ in range(blocks)]
    d_value = [[zero, zero] for _ in range(blocks)]
    d_near = [[zero, zero] for _ in range(blocks)]
    d_far = [[zero, zero] for _ in range(blocks)]
    for at in range(blocks):
        for of in range(at + 1):
            mask = allowed_here(cols_ref, row_ref, at, of, False)
            t_row = row_ref[0, :, pl.ds(at * BLOCK, BLOCK)]
            s_col = cols_ref[0, pl.ds(of * BLOCK, BLOCK), 0:1]
            mask_t = s_col == t_row
            if at == of:
                shape = (BLOCK, BLOCK)
                mask_t = jnp.logical_and(
                    mask_t, lax.broadcasted_iota(jnp.int32, shape, 0) < lax.broadcasted_iota(jnp.int32, shape, 1)
                )
            gap = jnp.exp(log_decay * (BLOCK * (at - of - 1))) if at > of + 1 else None
            keys = near[of] if of == at else cut(far[of] if gap is None else far[of] * gap)
            for head in range(2):
                q_hl = high_low(queries[at], first, head)
                g_hl = high_low(grads[at], first, head)
                k_hl = high_low(keys, first, head)
                v_hl = high_low(values[of], first, head)
                scores_t = dot_nt(twice(k_hl), doubled(queries[at], first, head))
                s_h, s_l = split(jnp.where(mask_t, scores_t, 0.0))
                d_value[of][head] = d_value[of][head] + dot(s_h, g_hl) + dot(s_l, g_hl)
                d_scores = dot_nt(twice(g_hl), doubled(values[of], first, head))
                s_h, s_l = split(jnp.where(mask, d_scores, 0.0))
                d_query[at][head] = d_query[at][head] + dot(s_h, k_hl) + dot(s_l, k_hl)
                d_scores_t = dot_nt(twice(v_hl), doubled(grads[at], first, head))
                s_h, s_l = split(jnp.where(mask_t, d_scores_t, 0.0))
                d_key = dot(s_h, q_hl) + dot(s_l, q_hl)
                if of == at:
                    d_near[of][head] = d_key
                else:
                    if gap is not None:
                        d_key = d_key * gap
                    d_far[of][head] = d_far[of][head] + d_key
    d_decay = jnp.zeros((1, PAIR), f32)
    d_boost = jnp.zeros((1, PAIR), f32)
    for at in range(blocks):
        here = pl.ds(at * BLOCK, BLOCK)
        recept, keys, value, grad = recept_ref[0, here], keys_ref[0, here], values_ref[0, here], grad_ref[0, here]
        fresh = cols_ref[0, here, 2:3]
        d_in = folded(d_query[at], first) * fall
        d_state = times_state_t(grad, square) * (fall * jnp.exp(log_decay * (BLOCK * at)) * fresh)
        d_here = folded(d_near[at], first) * rise
        d_later = folded(d_far[at], first) * (rise * whole)
        present = head_sum(recept * boost * keys, ones)
        d_present = head_sum(grad * value, ones)
        d_recept_ref[0, here] = d_in + d_state + boost * keys * d_present
        d_keys_ref[0, here] = d_here + d_later + boost * recept * d_present
        d_values_ref[0, here] = folded(d_value[at], first) + present * grad
        d_boost = d_boost + jnp.sum(recept * keys * d_present, axis=0, keepdims=True)
        d_decay = d_decay + jnp.sum(
            recept * (step * d_in + (step + float(BLOCK * at)) * d_state)
            + keys * ((BLOCK - 1.0 - step) * d_later - (step + 1.0) * d_here),
            axis=0,
            keepdims=True,
        )
    d_vec_ref[0, 0:1] = d_decay
    d_vec_ref[0, 1:2] = d_boost


def project_back_kernel(
    x_ref, before_ref, cols_ref, vec_ref, d_attended_ref,
    d_recept_ref, d_keys_ref, d_values_ref, d_valve_ref, keys_ref, values_ref, state_ref, out_state_ref,
    mix_vec_ref, attention_vec_ref, channel_vec_ref, w_r, w_k, w_v, w_g,
    d_x_ref, d_row_ref, packed_ref, dw_r, dw_k, dw_v, dw_g,
    earlier_ref, difference_ref, direct_ref, passed_ref,
):
    length, width = x_ref.shape[1:]
    turn = pl.program_id(1)
    gain, bias = vec(vec_ref, GAIN), vec(vec_ref, BIAS)
    steps = lax.broadcasted_iota(jnp.int32, (length, PAIR), 0).astype(f32)
    pairs = [(pair, slice(pair * PAIR, (pair + 1) * PAIR)) for pair in range(width // PAIR)]

    @pl.when(jnp.logical_and(pl.program_id(0) == 0, turn == 0))
    def _():
        for ref in (packed_ref, dw_r, dw_k, dw_v, dw_g):
            ref[...] = jnp.zeros_like(ref)
        packed_ref[GROUP_GAIN : BIAS2 + 1] = attention_vec_ref[...]
        packed_ref[MIX_E : MIX_F + 1] = channel_vec_ref[...]

    def tail_of(lanes):
        return jnp.exp(vec(vec_ref, DECAY, lanes) * (length - 1.0 - steps)) * cols_ref[0, :, 3:4]

    def through(grad, which, weight, d_weight, first=False):
        mix, difference = vec(vec_ref, which), difference_ref[...]
        gh, gl = split(grad)
        mh, ml = split(earlier_ref[...] + mix * difference)
        d_weight[...] += dot_tn(mh, gh) + dot_tn(ml, gh) + dot_tn(mh, gl)
        d_mixed = dot_nt(gh, weight[...]) + dot_nt(gl, weight[...])
        packed_ref[which : which + 1] += jnp.sum(d_mixed * difference, axis=0, keepdims=True)
        direct, passed = mix * d_mixed, d_mixed - mix * d_mixed
        direct_ref[...] = direct if first else direct_ref[...] + direct
        passed_ref[...] = passed if first else passed_ref[...] + passed

    @pl.when(turn == 0)
    def _():
        normal = standard(x_ref[0].astype(f32))[0] * gain + bias
        before = standard(before_ref[0])[0] * gain + bias
        earlier = shifted(normal, before, cols_ref[0, :, 1:2])
        earlier_ref[...] = earlier
        difference_ref[...] = normal - earlier
        through(d_recept_ref[0], MIX_R, w_r, dw_r, True)
        packed_ref[DECAY : BOOST + 1] += mix_vec_ref[0]

    @pl.when(turn == 1)
    def _():
        through(d_valve_ref[0], MIX_G, w_g, dw_g)

    @pl.when(turn == 2)
    def _():
        parts = []
        for pair, lanes in pairs:
            d_keys = times_state_t(values_ref[0, :, lanes], widen(out_state_ref[0, pair])) * tail_of(lanes)
            later = (length - 1.0 - steps) * keys_ref[0, :, lanes] * d_keys
            both = widen(state_ref[0, pair]) * widen(out_state_ref[0, pair])
            ones = jnp.ones((8, PAIR), bf16)
            kept = sum([dot_nt(ones, part)[0:1] for part in split(both)])
            kept = kept * jnp.exp(vec(vec_ref, DECAY, lanes) * length) * (float(length) * cols_ref[0, length - 1 :, 2:3])
            packed_ref[DECAY : DECAY + 1, lanes] += jnp.sum(later, axis=0, keepdims=True) + kept
            parts.append(d_keys_ref[0, :, lanes] + d_keys)
        through(jnp.concatenate(parts, axis=1), MIX_K, w_k, dw_k)

    @pl.when(turn == 3)
    def _():
        parts = []
        for pair, lanes in pairs:
            ended = times_state(keys_ref[0, :, lanes] * tail_of(lanes), widen(out_state_ref[0, pair]))
            parts.append(d_values_ref[0, :, lanes] + ended)
        through(jnp.concatenate(parts, axis=1), MIX_V, w_v, dw_v)
        passed = passed_ref[...] * cols_ref[0, :, 1:2]
        rows = lax.broadcasted_iota(jnp.int32, (length, width), 0)
        d_normal = direct_ref[...] + jnp.where(rows == length - 1, 0.0, pltpu.roll(passed, length - 1, 0))
        hat, scale = standard(x_ref[0].astype(f32))
        hat_before, scale_before = standard(before_ref[0])
        out = passed[0:1]
        packed_ref[GAIN : GAIN + 1] += jnp.sum(d_normal * hat, axis=0, keepdims=True) + out * hat_before
        packed_ref[BIAS : BIAS + 1] += jnp.sum(d_normal, axis=0, keepdims=True) + out
        d_x_ref[0] = d_attended_ref[0] + standard_back(d_normal * gain, hat, scale)
        d_row_ref[0] = standard_back(out * gain, hat_before, scale_before)

        @pl.when(pl.program_id(0) == pl.num_programs(0) - 1)
        def _():
            packed_ref[DECAY : DECAY + 1] = packed_ref[DECAY : DECAY + 1] * vec(vec_ref, DECAY)


def call(kernel, grid, ins, outs, name, scratch=(), flops=0, hosts=(), collective_id=None):
    bytes_accessed = sum(a.size * a.dtype.itemsize for a, _, _ in ins)
    for shape, dtype, _, _ in outs:
        size = jnp.dtype(dtype).itemsize
        for extent in shape:
            size *= extent
        bytes_accessed += size

    def spec(block, index):
        if block == "smem":
            return pl.BlockSpec(memory_space=pltpu.SMEM)
        if block == "any":
            return pl.BlockSpec(memory_space=pl.ANY)
        if index is None:
            return pl.BlockSpec(block, lambda *_: (0,) * len(block), pipeline_mode=pl.Buffered(1))
        return pl.BlockSpec(block, index)

    ins, outs, scratch = list(ins), list(outs), list(scratch)
    own, places, aliases = (len(ins), len(outs), len(scratch)), [], {}
    for exchange, _ in hosts:
        more_in, more_out, alias = exchange.operands()
        aliases.update({len(ins) + i: len(outs) + j for i, j in alias})
        place = [len(ins), len(outs), len(scratch)]
        ins, outs, scratch = ins + more_in, outs + more_out, scratch + exchange.scratch()
        places.append([slice(a, b) for a, b in zip(place, (len(ins), len(outs), len(scratch)))])
    steps = 1
    for extent in grid:
        steps *= extent

    def body(*refs):
        in_refs, out_refs, scratch_refs = refs[: len(ins)], refs[len(ins) : len(ins) + len(outs)], refs[len(ins) + len(outs) :]
        step = pl.program_id(0)
        for axis in range(1, len(grid)):
            step = step * grid[axis] + pl.program_id(axis)
        for (exchange, _), (i, o, t) in zip(hosts, places):
            exchange.bind(in_refs[i], out_refs[o], scratch_refs[t])

        def enter():
            barrier = pltpu.get_barrier_semaphore()
            partners = [partner for exchange, _ in hosts for partner in exchange.partners()]
            for partner in partners:
                pl.semaphore_signal(barrier, inc=1, device_id=(partner,), device_id_type=MESH)
            pl.semaphore_wait(barrier, len(partners))
            for exchange, _ in hosts:
                exchange.start()

        def advance(turn):
            for exchange, ends in hosts:
                due = [slot for slot in range(exchange.slots) if min(ends[slot], steps) == turn]
                if due:

                    @pl.when(step == min(turn, steps - 1))
                    def _():
                        for slot in due:
                            exchange.run(slot)

        if hosts:
            pl.when(step == 0)(enter)
        for turn in range(steps):
            advance(turn)
        kernel(*in_refs[: own[0]], *out_refs[: own[1]], *scratch_refs[: own[2]])
        advance(steps)

    params = {"collective_id": collective_id, "has_side_effects": True} if hosts else {}
    return pl.pallas_call(
        body,
        grid=grid,
        in_specs=[spec(block, index) for _, block, index in ins],
        out_specs=[spec(block, index) for _, _, block, index in outs],
        out_shape=[jax.ShapeDtypeStruct(shape, dtype) for shape, dtype, _, _ in outs],
        input_output_aliases=aliases,
        scratch_shapes=scratch,
        compiler_params=pltpu.CompilerParams(
            dimension_semantics=("arbitrary",) * len(grid), vmem_limit_bytes=VMEM_LIMIT, **params
        ),
        cost_estimate=pl.CostEstimate(flops=flops, bytes_accessed=bytes_accessed, transcendentals=0),
        name=name,
    )(*[a for a, _, _ in ins])


def moved(value, steps):
    count = lax.axis_size("seq")
    low, high = max(0, -steps), min(count, count - steps)
    return lax.ppermute(value, "seq", [(source, source + steps) for source in range(low, high)])


def reach(count):
    window, needed, hops = 2, {32: 16, 128: 32}.get(count, count) // 2, []
    while window < needed:
        hops.append(window)
        window *= 2
    return hops


class Carrier:
    def __init__(self, parts, lengths, vectors, length, sign, begin=0, end=None):
        self.count = lax.axis_size("seq")
        self.parts, self.lengths, self.vectors, self.length, self.sign = parts, lengths, vectors, length, sign
        self.hops = [[1, 2]] + [[hop] for hop in reach(self.count)]
        self.whole = len(self.hops) + 2
        self.begin, self.end = begin, self.whole if end is None else end
        self.slots = self.end - self.begin
        batches, pairs = parts[0].shape[:2]
        self.half = pairs // 2 if begin == 0 else pairs
        self.shape = (batches, self.half) + parts[0].shape[2:]

    def operands(self):
        shape = self.shape
        full = (shape[0], 2 * self.half) + shape[2:]
        outs = [(full, f32, full, None)] if self.end == self.whole else [(shape, f32, shape, None)] * 2
        ins = [(part, part.shape, None) for part in self.parts]
        return ins + [(self.vectors, self.vectors.shape, None), (self.lengths, "smem", None)], outs, []

    def scratch(self):
        return [
            pltpu.VMEM((self.slots, 2) + self.shape, f32),
            pltpu.VMEM((self.slots + 1,) + self.shape, f32),
            pltpu.VMEM((2,) + self.shape, f32),
            pltpu.SemaphoreType.DMA((self.slots, 2)),
            pltpu.SemaphoreType.DMA((self.slots, 2)),
        ]

    def bind(self, ins, outs, scratch):
        *self.part_refs, self.vec_ref, self.lengths_ref = ins
        self.out_refs = outs
        self.landed, self.totals, self.kept, self.send_sems, self.recv_sems = scratch
        self.mine = lax.axis_index("seq")
        self.core, self.chip = self.mine % 2, self.mine // 2
        self.sibling = self.mine + 1 - 2 * self.core

    def chip_at(self, hop):
        chips = self.count // 2
        return (self.chip + hop + chips) % chips * 2 + self.core

    def partners(self):
        out = []
        for slot in range(self.begin, self.end):
            if slot in (0, self.whole - 1):
                out.append(self.sibling)
            else:
                out += [self.chip_at(sign * hop) for hop in self.hops[slot - 1] for sign in (1, -1)]
        return out

    def first_part(self):
        return self.kept.at[0] if self.begin == 0 else self.part_refs[1]

    def total(self, slot):
        return self.part_refs[0] if slot == self.begin and slot > 0 else self.totals.at[slot - self.begin]

    def copies(self, slot):
        at = slot - self.begin
        if slot == 0:
            away = self.part_refs[0].at[:, pl.ds((1 - self.core) * self.half, self.half)]
            moves = [(away, self.landed.at[at, 0], self.sibling)]
        elif slot == self.whole - 1:
            moves = [(self.kept.at[1], self.landed.at[at, 0], self.sibling)]
        else:
            moves = [
                (self.total(slot), self.landed.at[at, i], self.chip_at(self.sign * hop))
                for i, hop in enumerate(self.hops[slot - 1])
            ]
        return [
            pltpu.make_async_remote_copy(
                src_ref=source, dst_ref=target, send_sem=self.send_sems.at[at, i], recv_sem=self.recv_sems.at[at, i],
                device_id=(device,), device_id_type=MESH,
            )
            for i, (source, target, device) in enumerate(moves)
        ]

    def start(self):
        self.open(self.begin)

    def open(self, slot):
        if slot == self.whole - 1:
            self.finish()
        for copy in self.copies(slot):
            copy.start()

    def fade(self, pair, devices):
        lane = lax.broadcasted_iota(jnp.int32, (LANE_FEATURES, PAIR), 1)
        row = lax.broadcasted_iota(jnp.int32, (LANE_FEATURES, PAIR), 0)
        at = pl.multiple_of((self.core * self.half + pair) * PAIR, PAIR)
        decay = self.vec_ref[DECAY : DECAY + 1, pl.ds(at, PAIR)] * float(self.length * devices)
        heads = [
            jnp.sum(jnp.where(lane == row + head * LANE_FEATURES, decay, 0.0), axis=1, keepdims=True) for head in range(2)
        ]
        return jnp.exp(jnp.where(first_lanes(LANE_FEATURES), heads[0], heads[1]))

    def same(self, batch, bound, other):
        bounds = bounds_of(self.lengths_ref, batch)
        ends = [segment_of(bounds, (device + 1) * self.length - 1) for device in (bound, other)]
        return jnp.where(ends[0] == ends[1], 1.0, 0.0).astype(f32)

    def edges(self):
        middle = 2 * self.chip
        return middle - self.sign, middle, middle + self.sign

    def run(self, slot):
        slot = slot + self.begin
        at = slot - self.begin
        for copy in self.copies(slot):
            copy.wait()
        batches = self.shape[0]
        entry, middle, leaving = self.edges()
        if slot == 0:
            flags = [self.same(batch, middle, leaving) for batch in range(batches)]
            is_first = self.core == (0 if self.sign > 0 else 1)
            for pair in range(self.half):
                fade = self.fade(pair, 1)
                for batch in range(batches):
                    own = self.part_refs[0][batch, self.core * self.half + pair]
                    other = self.landed[at, 0, batch, pair]
                    ahead, behind = jnp.where(is_first, own, other), jnp.where(is_first, other, own)
                    self.kept[0, batch, pair] = ahead
                    self.totals[at + 1, batch, pair] = ahead * fade * flags[batch] + behind
        elif slot < self.whole - 1:
            hops = self.hops[slot - 1]
            chips = self.count // 2
            flags = []
            for hop in hops:
                there = self.chip - self.sign * hop
                exists = jnp.where(jnp.logical_and(there >= 0, there < chips), 1.0, 0.0).astype(f32)
                crossed = hop - 1 if slot == 1 else hop
                flags.append([exists * self.same(batch, entry - 2 * self.sign * crossed, entry) for batch in range(batches)])
            for pair in range(self.half):
                fade = self.fade(pair, 2 if slot == 1 else 2 * hops[0])
                for batch in range(batches):
                    if slot == 1:
                        near, far = self.landed[at, 0, batch, pair], self.landed[at, 1, batch, pair]
                        here = near * flags[0][batch] + far * fade * flags[1][batch]
                    else:
                        here = self.total(slot)[batch, pair] + self.landed[at, 0, batch, pair] * fade * flags[0][batch]
                    self.totals[at + 1, batch, pair] = here
        else:
            for pair in range(self.half):
                for batch in range(batches):
                    self.out_refs[0][batch, (1 - self.core) * self.half + pair] = self.landed[at, 0, batch, pair]
        if slot + 1 < self.end:
            self.open(slot + 1)
        elif self.end < self.whole:
            self.out_refs[0][...] = self.totals[at + 1]
            self.out_refs[1][...] = self.first_part()[...]

    def finish(self):
        entry, middle, _ = self.edges()
        total, first_part = self.total(self.whole - 1), self.first_part()
        is_first = self.core == (0 if self.sign > 0 else 1)
        flags = [self.same(batch, entry, middle) for batch in range(self.shape[0])]
        for pair in range(self.half):
            fade = self.fade(pair, 1)
            for batch in range(self.shape[0]):
                first = total[batch, pair]
                second = first * fade * flags[batch] + first_part[batch, pair]
                self.out_refs[0][batch, self.core * self.half + pair] = jnp.where(is_first, first, second)
                self.kept[1, batch, pair] = jnp.where(is_first, second, first)


def bit_orders(count):
    bits = count.bit_length() - 1
    if bits == 5:
        return [(0, 1, 2, 3, 4), (0, 2, 3, 1, 4), (0, 3, 1, 2, 4)]
    chip = list(range(1, bits))
    third = max(1, len(chip) // 3)
    return [tuple([0] + chip[k * third :] + chip[: k * third]) for k in range(3)]


class Unit:
    def __init__(self, array, first, rows, width, order, group, begin, end):
        self.array, self.first, self.rows, self.width, self.group = array, first, rows, width, group
        self.steps, size, landing = [], rows, 0
        bits = self.bits = len(order)
        for k, bit in enumerate(order):
            halved = size % 16 == 0
            sent = size // 2 if halved else size
            self.steps.append((bit, halved, sent, landing))
            if begin <= k < end:
                landing += sent
            size = sent
        phases = [p for p in range(2 * bits) if p < bits or self.steps[2 * bits - 1 - p][1]]
        self.phases = [p for p in phases if begin <= p < end]
        self.sums = [p for p in self.phases if p < bits]
        self.landing = landing
        self.held = self.steps[self.sums[0]][2] if self.sums else 0
        self.stages = len(self.phases)


def add_rows(target, at, source, source_at, rows):
    block = next(b for b in (64, 56, 48, 32, 24, 16, 8) if rows % b == 0)

    def step(i, _):
        here = pl.ds(pl.multiple_of(at + i * block, 8), block)
        target[here] = target[here] + source[pl.ds(pl.multiple_of(source_at + i * block, 8), block)]
        return 0

    lax.fori_loop(0, rows // block, step, 0)


def rows8(at, size):
    return pl.ds(pl.multiple_of(at, 8), size)


class Summer:
    def __init__(self, arrays, layout):
        self.count, self.arrays, self.units = lax.axis_size("seq"), arrays, []
        orders = bit_orders(self.count)
        for array, first, rows, parts, group, turn, begin, end in layout:
            size = rows // parts
            for part in range(parts):
                order, width = orders[(turn + part) % 3], arrays[array].shape[1]
                self.units.append(Unit(array, first + part * size, size, width, order, group, begin, end))
        self.groups = sorted({unit.group for unit in self.units})
        self.stages = max(unit.stages for unit in self.units)
        self.slots = self.stages + len(self.groups) - 1

    def operands(self):
        arrays = self.arrays
        return (
            [(a, "any", None) for a in arrays],
            [(a.shape, a.dtype, "any", None) for a in arrays],
            [(i, i) for i in range(len(arrays))],
        )

    def scratch(self):
        return (
            [pltpu.VMEM((max(8, unit.held), unit.width), f32) for unit in self.units]
            + [pltpu.VMEM((max(8, unit.landing), unit.width), f32) for unit in self.units]
            + [
                pltpu.SemaphoreType.DMA((len(self.units), self.stages)),
                pltpu.SemaphoreType.DMA((len(self.units), self.stages)),
                pltpu.SemaphoreType.DMA((len(self.units), 2)),
                pltpu.SemaphoreType.REGULAR((len(self.units),)),
            ]
        )

    def bind(self, ins, outs, scratch):
        size = len(self.units)
        self.refs, self.held, self.landed = outs, scratch[:size], scratch[size : 2 * size]
        self.send_sems, self.recv_sems, self.local_sems, self.free_sems = scratch[2 * size :]
        mine = lax.axis_index("seq")
        bits = self.count.bit_length() - 1
        self.bit = [mine // (1 << k) % 2 for k in range(bits)]
        self.partner = [mine + (1 - 2 * self.bit[k]) * (1 << k) for k in range(bits)]
        self.offsets = []
        for unit in self.units:
            at, seen = 0, [0]
            for which, halved, sent, _ in unit.steps:
                at = at + self.bit[which] * sent if halved else at
                seen.append(at)
            self.offsets.append(seen)

    def partners(self):
        used = sorted({unit.steps[min(p, 2 * unit.bits - 1 - p)][0] for unit in self.units for p in unit.phases})
        return [self.partner[k] for k in used]

    def start(self):
        for group in self.groups:
            for u, unit in enumerate(self.units):
                if unit.group == group:
                    self.begin(u, 0)

    def own(self, u, step):
        unit = self.units[u]
        return self.refs[unit.array].at[rows8(unit.first + self.offsets[u][step + 1], unit.steps[step][2])]

    def copies(self, u, stage):
        unit, seen, here = self.units[u], self.offsets[u], self.refs[self.units[u].array]
        phase, out = unit.phases[stage], []
        if phase < unit.bits:
            which, halved, sent, landing = unit.steps[phase]
            away = seen[phase] + (1 - self.bit[which]) * sent if halved else seen[phase]
            target = self.landed[u].at[pl.ds(landing, sent)]
            if stage == 0:
                source = here.at[rows8(unit.first + away, sent)]
                out.append(pltpu.make_async_copy(self.own(u, phase), self.held[u], self.local_sems.at[u, 0]))
            else:
                source = self.held[u].at[rows8(away - seen[unit.sums[0] + 1], sent)]
        else:
            step = 2 * unit.bits - 1 - phase
            which, _, sent, _ = unit.steps[step]
            source = target = self.own(u, step)
            if unit.sums and stage == len(unit.sums):
                source = self.held[u].at[rows8(seen[step + 1] - seen[unit.sums[0] + 1], sent)]
        return out + [
            pltpu.make_async_remote_copy(
                src_ref=source, dst_ref=target, send_sem=self.send_sems.at[u, stage],
                recv_sem=self.recv_sems.at[u, stage], device_id=(self.partner[which],), device_id_type=MESH,
            )
        ]

    def store(self, u):
        unit, seen = self.units[u], self.offsets[u]
        step = unit.sums[-1]
        source = self.held[u].at[rows8(seen[step + 1] - seen[unit.sums[0] + 1], unit.steps[step][2])]
        return pltpu.make_async_copy(source, self.own(u, step), self.local_sems.at[u, 1])

    def returns(self, u):
        unit = self.units[u]
        back = 2 * unit.bits - 1 - unit.phases[0]
        return unit.phases.index(back) if unit.sums and back in unit.phases else None

    def begin(self, u, stage):
        if stage == self.returns(u):
            pl.semaphore_wait(self.free_sems.at[u], 1)
        for copy in self.copies(u, stage):
            copy.start()

    def end(self, u, stage):
        unit, seen = self.units[u], self.offsets[u]
        for copy in self.copies(u, stage):
            copy.wait()
        phase, sums = unit.phases[stage], len(unit.sums)
        if stage == 0 and self.returns(u) is not None:
            partner = self.partner[unit.steps[phase][0]]
            pl.semaphore_signal(self.free_sems.at[u], inc=1, device_id=(partner,), device_id_type=MESH)
        if phase < unit.bits:
            _, _, sent, landing = unit.steps[phase]
            add_rows(self.held[u], seen[phase + 1] - seen[unit.sums[0] + 1], self.landed[u], landing, sent)
            if stage == sums - 1:
                self.store(u).start()
                if unit.stages == sums:
                    self.store(u).wait()
        elif sums and stage == sums:
            self.store(u).wait()

    def run(self, slot):
        for place, group in enumerate(self.groups):
            for u, unit in enumerate(self.units):
                stage = slot - place
                if unit.group != group:
                    continue
                if unit.phases[0] >= unit.bits and unit.phases[-1] == 2 * unit.bits - 1 and stage >= unit.stages - 1:
                    stage = unit.stages - 1 if slot == self.slots - 1 else -1
                if 0 <= stage < unit.stages:
                    self.end(u, stage)
                    if stage + 1 < unit.stages:
                        self.begin(u, stage + 1)


def nothing():
    pass


def summed_over_devices(arrays, layout, collective_id):
    summer = Summer(arrays, layout)
    return call(nothing, (1,), [], [], "sum_over_devices", hosts=[(summer, [1] * summer.slots)], collective_id=collective_id)


def local(
    incoming_hidden,
    packed_run_lengths,
    prior_standardize_factor,
    prior_standardize_addend,
    respond_interpolant,
    address_interpolant,
    content_interpolant,
    valve_interpolant,
    respond_transform,
    address_transform,
    content_transform,
    valve_transform,
    damping_rates,
    immediate_boost,
    cluster_normal_factor,
    cluster_normal_shift_term,
    readout_transform,
    posterior_standardize_factor,
    posterior_standardize_addend,
    dense_address_interpolant,
    dense_respond_interpolant,
    dense_address_transform,
    dense_content_transform,
    dense_respond_transform,
    objective_adjoint,
):
    batches, length, width = incoming_hidden.shape
    hidden_width = dense_address_transform.shape[1]
    pairs = width // PAIR
    depth = lax.axis_size("seq").bit_length() - 1
    lengths = packed_run_lengths
    vectors = jnp.stack(
        [
            prior_standardize_factor, prior_standardize_addend, respond_interpolant, address_interpolant,
            content_interpolant, valve_interpolant, -jnp.exp(damping_rates), immediate_boost, cluster_normal_factor,
            cluster_normal_shift_term, posterior_standardize_factor, posterior_standardize_addend,
            dense_address_interpolant, dense_respond_interpolant,
        ]
        + [jnp.zeros_like(damping_rates)] * 2
    )

    def table(w):
        return (w, w.shape, None)

    def rows_of(a):
        return (a, (1,) + a.shape[1:], lambda b, *_: (b,) + (0,) * (a.ndim - 1))

    def rows_out(shape, dtype=f32):
        return (shape, dtype, (1,) + tuple(shape[1:]), lambda b, *_: (b,) + (0,) * (len(shape) - 1))

    def sum_out(*shape):
        return (shape, f32, shape, None)

    tokens, states, one_row = (batches, length, width), (batches, pairs, LANE_FEATURES, PAIR), (batches, 1, width)
    square_flops = 2 * batches * length * width * width
    before = moved(incoming_hidden[:, -1, :].astype(f32), 1)[:, None, :]
    cols, row = call(
        tokens_kernel, (1,), [(lengths, "smem", None)], [sum_out(batches, length, 8), sum_out(batches, 1, length)], "tokens"
    )
    common = [rows_of(incoming_hidden), rows_of(before), rows_of(cols), table(vectors)]
    keys, values, end_state = call(
        functools.partial(project_kernel, (MIX_K, MIX_V), True),
        (batches,),
        common + [table(address_transform), table(content_transform)],
        [rows_out(tokens)] * 2 + [rows_out(states)],
        "project_keys",
        flops=4 * square_flops,
    )
    nearest = Carrier([end_state], lengths, vectors, length, 1, 0, 2)
    recept, valve, *near_state = call(
        functools.partial(project_kernel, (MIX_R, MIX_G), False),
        (batches,),
        common + [table(respond_transform), table(valve_transform)],
        [rows_out(tokens)] * 2,
        "project_recept",
        flops=4 * square_flops,
        hosts=[(nearest, [batches // 2, batches])],
        collective_id=1,
    )
    by_pair = lambda a: (a, (1, length, PAIR), lambda b, p: (b, 0, p))
    pair_vectors = (vectors, (vectors.shape[0], PAIR), lambda b, p: (0, p))
    pair_state = lambda s: (s, (1, 1, LANE_FEATURES, PAIR), lambda b, p: (b, p, 0, 0))
    pair_out = (tokens, f32, (1, length, PAIR), lambda b, p: (b, 0, p))
    further = Carrier(near_state, lengths, vectors, length, 1, 2)
    steps = batches * pairs
    mixed, state = call(
        mix_kernel,
        (batches, pairs),
        [by_pair(recept), by_pair(keys), by_pair(values), rows_of(cols), rows_of(row), pair_vectors],
        [pair_out],
        "mix",
        flops=3 * 2 * batches * length * length * width * 2,
        hosts=[(further, [(i + 1) * steps // further.slots for i in range(further.slots)])],
        collective_id=2,
    )
    wkv, attended, second, second_row = call(
        readout_kernel,
        (batches,),
        [
            rows_of(mixed), rows_of(recept), rows_of(state), rows_of(valve), rows_of(cols), table(vectors),
            rows_of(incoming_hidden), table(readout_transform),
        ],
        [rows_out(tokens)] * 3 + [rows_out(one_row)],
        "readout",
        flops=2 * square_flops,
    )
    second_row = moved(second_row[:, 0, :], 1)[:, None, :]
    tiles = length // BLOCK
    tile_rows = lambda a: (a, (1, BLOCK, a.shape[2]), lambda b, i: (b, tiles - 1 - i, 0))
    ahead = (second, (1, 8, width), lambda b, i: (b, jnp.maximum((tiles - 1 - i) * (BLOCK // 8) - 1, 0), 0))
    tile_out = lambda dtype: (tokens, dtype, (1, BLOCK, width), lambda b, i: (b, tiles - 1 - i, 0))
    block, d_second, d_second_row, grad_expand, grad_shrink, grad_filter, channel_vectors = call(
        channel_kernel,
        (batches, tiles),
        [
            tile_rows(second), ahead, rows_of(second_row), tile_rows(attended), tile_rows(objective_adjoint),
            tile_rows(cols), table(vectors),
            table(dense_address_transform), table(dense_content_transform), table(dense_respond_transform),
        ],
        [
            tile_out(bf16), tile_out(f32), rows_out(one_row),
            sum_out(width, hidden_width), sum_out(hidden_width, width), sum_out(width, width), sum_out(2, width),
        ],
        "channel",
        scratch=[pltpu.VMEM((BLOCK, hidden_width), f32), pltpu.VMEM((1, width), f32)],
        flops=7 * 2 * batches * length * width * (2 * hidden_width + width),
    )
    channel_grads = [grad_expand, grad_shrink, grad_filter]

    def channel_phases(begin, end, group=0):
        return [(i, 0, a.shape[0], 3, group, 0, begin, end) for i, a in enumerate(channel_grads)]

    back_second = moved(d_second_row[:, 0, :], -1)[:, None, :]
    d_attended, d_wkv, d_valve, carry, grad_output, attention_vectors, *channel_grads = call(
        attention_back_kernel,
        (batches,),
        [
            rows_of(d_second), rows_of(back_second), rows_of(attended), rows_of(objective_adjoint), rows_of(wkv),
            rows_of(valve), rows_of(recept), rows_of(cols), table(vectors), table(readout_transform),
        ],
        [rows_out(tokens)] * 3 + [rows_out(states), sum_out(width, width), sum_out(4, width)],
        "attention_back",
        flops=5 * square_flops,
        hosts=[(Summer(channel_grads, channel_phases(0, 1)), [batches])],
        collective_id=3,
    )
    arriving = Carrier([carry], lengths, vectors, length, -1)
    d_recept, d_keys, d_values, mix_vectors, out_state, *channel_grads = call(
        mix_back_kernel,
        (batches, pairs),
        [
            by_pair(recept), by_pair(keys), by_pair(values), by_pair(d_wkv), pair_state(state), rows_of(cols), rows_of(row),
            pair_vectors,
        ],
        [pair_out] * 3 + [((batches, 2, width), f32, (1, 2, PAIR), lambda b, p: (b, 0, p))],
        "mix_back",
        flops=9 * 2 * batches * length * length * width * 2,
        hosts=[
            (arriving, [(i + 1) * steps // arriving.slots for i in range(arriving.slots)]),
            (Summer(channel_grads, channel_phases(1, depth - 1)), [(7 * steps) // 12, (10 * steps) // 12] + [steps] * (depth - 4)),
        ],
        collective_id=4,
    )
    fading = [2, 4, 6] + [8] * (2 * depth)
    wide = lambda: pltpu.VMEM((length, width), f32)
    d_x, d_first_row, packed, grad_recept, grad_keys, grad_values, grad_gate_w, *channel_grads = call(
        project_back_kernel,
        (batches, 4),
        common
        + [
            rows_of(d_attended), rows_of(d_recept), rows_of(d_keys), rows_of(d_values), rows_of(d_valve),
            rows_of(keys), rows_of(values), rows_of(state), rows_of(out_state), rows_of(mix_vectors),
            table(attention_vectors), table(channel_vectors),
        ]
        + [table(w) for w in (respond_transform, address_transform, content_transform, valve_transform)],
        [rows_out(tokens), rows_out(one_row), sum_out(*vectors.shape)] + [sum_out(width, width)] * 4,
        "project_back",
        scratch=[wide(), wide(), wide(), wide()],
        flops=5 * 4 * square_flops,
        hosts=[(Summer(channel_grads, channel_phases(depth - 1, 2 * depth - 2)), fading)],
        collective_id=5,
    )
    layout = channel_phases(2 * depth - 2, 2 * depth) + [(8, 0, packed.shape[0], 1, 1, 0, 0, 2 * depth)]
    layout += [(3 + i, 0, width, 3, 1 + i, 0, 0, 2 * depth) for i in range(5)]
    w_expand, w_shrink, w_filter, w_output, w_recept, w_keys, w_values, w_gate, vectors = summed_over_devices(
        channel_grads + [grad_output, grad_recept, grad_keys, grad_values, grad_gate_w, packed], layout, 0
    )
    grad_tokens = d_x.at[:, -1, :].add(moved(d_first_row[:, 0, :], -1))
    return (
        block, grad_tokens, *[vectors[i] for i in range(6)], w_recept, w_keys, w_values, w_gate,
        vectors[6], vectors[7], vectors[8], vectors[9], w_output, vectors[10], vectors[11], vectors[12], vectors[13],
        w_expand, w_shrink, w_filter,
    )


def solution(mesh):
    rows = P(None, "seq", None)
    return jax.shard_map(
        local,
        mesh=mesh,
        in_specs=(rows,) + (P(),) * 23 + (rows,),
        out_specs=(rows, rows) + (P(),) * 22,
        check_vma=False,
    )
```

```python
import functools

import jax
import jax.numpy as jnp
from jax import lax
from jax.experimental import pallas as pl
from jax.experimental.pallas import tpu as pltpu
from jax.sharding import PartitionSpec as P

LANE_FEATURES = 64
PAIR = 2 * LANE_FEATURES
BLOCK = 256
f32 = jnp.float32
bf16 = jnp.bfloat16
VMEM_LIMIT = 60 * 1024 * 1024
MESH = pl.DeviceIdType.MESH


def nothing():
    pass


def split(x):
    high = x.astype(bf16)
    return high, (x - high.astype(f32)).astype(bf16)


def dot(a, b):
    return lax.dot_general(a, b, (((1,), (0,)), ((), ())), preferred_element_type=f32)


def dot_nt(a, b):
    return lax.dot_general(a, b, (((1,), (1,)), ((), ())), preferred_element_type=f32)


def dot_tn(a, b):
    return lax.dot_general(a, b, (((0,), (0,)), ((), ())), preferred_element_type=f32)


def times_weight(x, w):
    high, low = split(x)
    return dot(high, w) + dot(low, w)


def times_weight_t(x, w):
    high, low = split(x)
    return dot_nt(high, w) + dot_nt(low, w)


def outer_sum(a, b):
    ah, al = split(a)
    bh, bl = split(b)
    return dot_tn(ah, bh) + dot_tn(al, bh) + dot_tn(ah, bl)


def standard(x, epsilon=1e-05):
    centred = x - jnp.mean(x, axis=-1, keepdims=True)
    scale = lax.rsqrt(jnp.mean(centred * centred, axis=-1, keepdims=True) + epsilon)
    return centred * scale, scale


def standard_back(grad, normal, scale):
    return scale * (
        grad
        - jnp.mean(grad, axis=-1, keepdims=True)
        - normal * jnp.mean(grad * normal, axis=-1, keepdims=True)
    )


def first_lanes(rows):
    return lax.broadcasted_iota(jnp.int32, (rows, PAIR), 1) < LANE_FEATURES


def head_ones(scale):
    row = lax.broadcasted_iota(jnp.int32, (2 * PAIR, PAIR), 0) // LANE_FEATURES % 2
    col = lax.broadcasted_iota(jnp.int32, (2 * PAIR, PAIR), 1) // LANE_FEATURES
    return jnp.where(row == col, scale, 0.0).astype(bf16)


def head_sum(x, ones):
    return dot(jnp.concatenate(split(x), axis=1), ones)


def widen(state):
    first = first_lanes(LANE_FEATURES)
    return jnp.concatenate([jnp.where(first, state, 0.0), jnp.where(first, 0.0, state)], axis=0)


def compact(square):
    first = first_lanes(LANE_FEATURES)
    return jnp.where(first, square[:LANE_FEATURES], square[LANE_FEATURES:])


def times_state(x, square):
    xh, xl = split(x)
    sh, sl = split(square)
    return dot(jnp.concatenate([xh, xl], axis=1), jnp.concatenate([sh, sh], axis=0)) + dot(xh, sl)


def times_state_t(x, square):
    xh, xl = split(x)
    sh, sl = split(square)
    return dot_nt(jnp.concatenate([xh, xl], axis=1), jnp.concatenate([sh, sh], axis=1)) + dot_nt(xh, sl)


def cut(x):
    high = x.astype(bf16).astype(f32)
    low = x - high
    return high, low, pltpu.roll(high, LANE_FEATURES, 1), pltpu.roll(low, LANE_FEATURES, 1)


def high_low(pieces, first, head):
    high, low, high_r, low_r = pieces
    return (jnp.where(first, high, low_r) if head == 0 else jnp.where(first, high_r, low)).astype(bf16)


def doubled(pieces, first, head):
    high, low, high_r, low_r = pieces
    if head == 0:
        both = (jnp.where(first, high, high_r), jnp.where(first, low, low_r))
    else:
        both = (jnp.where(first, high_r, high), jnp.where(first, low_r, low))
    return jnp.concatenate([part.astype(bf16) for part in both], axis=1)


def twice(x):
    return jnp.concatenate([x, x], axis=1)


def folded(parts, first):
    sums = [part + pltpu.roll(part, LANE_FEATURES, 1) for part in parts]
    return jnp.where(first, sums[0], sums[1])


def decays(log_decay):
    step = lax.broadcasted_iota(jnp.int32, (BLOCK, PAIR), 0).astype(f32)
    return step, jnp.exp(log_decay * step), jnp.exp(-log_decay * (step + 1.0)), jnp.exp(log_decay * BLOCK)


def shifted(normal, row_before, keep):
    rows = lax.broadcasted_iota(jnp.int32, normal.shape, 0)
    return jnp.where(rows == 0, row_before, pltpu.roll(normal, 1, 0)) * keep


GAIN, BIAS, MIX_R, MIX_K, MIX_V, MIX_G, DECAY, BOOST, GROUP_GAIN, GROUP_SHIFT, GAIN2, BIAS2, MIX_E, MIX_F = range(14)


def vec(ref, which, lanes=slice(None)):
    return ref[which : which + 1, lanes]


def bounds_of(lengths_ref, batch):
    at, bounds = jnp.int32(0), []
    for j in range(lengths_ref.shape[1]):
        bounds.append(at)
        at = at + lengths_ref[batch, j]
    return bounds


def segment_of(bounds, position):
    return sum([(position >= bound).astype(jnp.int32) for bound in bounds])


def tokens_kernel(lengths_ref, *refs):
    *vector_refs, cols_ref, row_ref, packed_ref = refs
    for i, ref in enumerate(vector_refs):
        value = ref[...].reshape(1, ref.shape[0])
        packed_ref[i : i + 1] = -jnp.exp(value) if i == DECAY else value
    packed_ref[len(vector_refs) :] = jnp.zeros((2, packed_ref.shape[1]), f32)
    batches, length, columns = cols_ref.shape
    offset = lax.axis_index("seq") * length
    for batch in range(batches):
        bounds = bounds_of(lengths_ref, batch)
        place = offset + lax.broadcasted_iota(jnp.int32, (length, columns), 0)
        segment = segment_of(bounds, place)
        starts = functools.reduce(jnp.logical_or, [place == bound for bound in bounds])
        column = lax.broadcasted_iota(jnp.int32, (length, columns), 1)
        fresh = segment == segment_of(bounds, offset - 1)
        last = segment == segment_of(bounds, offset + length - 1)
        flag = jnp.where(column == 1, jnp.where(starts, 0, 1), jnp.where(column == 2, jnp.where(fresh, 1, 0), jnp.where(last, 1, 0)))
        cols_ref[batch] = jnp.where(column == 0, segment, flag).astype(f32)
        row_ref[batch] = segment_of(bounds, offset + lax.broadcasted_iota(jnp.int32, (1, length), 1)).astype(f32)


def project_kernel(mixes, states, x_ref, before_ref, cols_ref, vec_ref, *refs):
    count = len(mixes)
    weights, outs = refs[:count], refs[count : 2 * count]
    gain, bias = vec(vec_ref, GAIN), vec(vec_ref, BIAS)
    normal = standard(x_ref[0].astype(f32))[0] * gain + bias
    before = standard(before_ref[0])[0] * gain + bias
    earlier = shifted(normal, before, cols_ref[0, :, 1:2])
    difference = normal - earlier
    for mix, weight, out in zip(mixes, weights, outs):
        out[0] = times_weight(earlier + vec(vec_ref, mix) * difference, weight[...])
    if states:
        length, width = normal.shape
        keys, values, end_ref = outs[0], outs[1], refs[2 * count]
        rows = lax.broadcasted_iota(jnp.int32, (length, PAIR), 0).astype(f32)
        for pair in range(width // PAIR):
            lanes = slice(pair * PAIR, (pair + 1) * PAIR)
            tail = jnp.exp(vec(vec_ref, DECAY, lanes) * (length - 1.0 - rows)) * cols_ref[0, :, 3:4]
            end_ref[0, pair] = compact(outer_sum(keys[0, :, lanes] * tail, values[0, :, lanes]))


def allowed_here(cols_ref, row_ref, at, of, across):
    t_col = cols_ref[0, pl.ds(at * BLOCK, BLOCK), 0:1]
    s_row = row_ref[0, :, pl.ds(of * BLOCK, BLOCK)]
    mask = t_col == s_row
    if at == of:
        shape = (BLOCK, BLOCK)
        low, high = (1, 0) if not across else (0, 1)
        mask = jnp.logical_and(
            mask,
            lax.broadcasted_iota(jnp.int32, shape, low) < lax.broadcasted_iota(jnp.int32, shape, high),
        )
    return mask


def mix_kernel(recept_ref, keys_ref, values_ref, cols_ref, row_ref, vec_ref, out_ref):
    length = recept_ref.shape[1]
    log_decay, boost = vec(vec_ref, DECAY), vec(vec_ref, BOOST)
    first = first_lanes(BLOCK)
    step, fall, rise, whole = decays(log_decay)
    ones = head_ones(1.0)
    queries, near, far, values = [], [], [], []
    for at in range(length // BLOCK):
        here = pl.ds(at * BLOCK, BLOCK)
        queries.append(cut(recept_ref[0, here] * fall))
        raised = keys_ref[0, here] * rise
        near.append(cut(raised))
        far.append(raised * whole)
        values.append(cut(values_ref[0, here]))
    for at in range(length // BLOCK):
        here = pl.ds(at * BLOCK, BLOCK)
        totals = [jnp.zeros((BLOCK, PAIR), f32)] * 2
        for of in range(at + 1):
            mask = allowed_here(cols_ref, row_ref, at, of, False)
            gap = jnp.exp(log_decay * (BLOCK * (at - of - 1))) if at > of + 1 else None
            keys = near[of] if of == at else cut(far[of] if gap is None else far[of] * gap)
            for head in range(2):
                scores = dot_nt(twice(high_low(queries[at], first, head)), doubled(keys, first, head))
                sh, sl = split(jnp.where(mask, scores, 0.0))
                held = high_low(values[of], first, head)
                totals[head] = totals[head] + dot(sh, held) + dot(sl, held)
        present = head_sum(recept_ref[0, here] * boost * keys_ref[0, here], ones)
        out_ref[0, here] = folded(totals, first) + present * values_ref[0, here]


def readout_kernel(
    mixed_ref, recept_ref, state_ref, valve_ref, cols_ref, vec_ref, x_ref, weight_ref,
    wkv_ref, attended_ref, second_ref, last_ref,
):
    length, width = mixed_ref.shape[1:]
    rows = lax.broadcasted_iota(jnp.int32, (length, PAIR), 0).astype(f32)
    ones = head_ones(1.0 / LANE_FEATURES)
    fresh = cols_ref[0, :, 2:3]
    gated = []
    for pair in range(width // PAIR):
        lanes = slice(pair * PAIR, (pair + 1) * PAIR)
        query = recept_ref[0, :, lanes] * jnp.exp(vec(vec_ref, DECAY, lanes) * rows) * fresh
        wkv = mixed_ref[0, :, lanes] + times_state(query, widen(state_ref[0, pair]))
        wkv_ref[0, :, lanes] = wkv
        centred = wkv - head_sum(wkv, ones)
        normal = centred * lax.rsqrt(head_sum(centred * centred, ones) + 0.00064)
        grouped = normal * vec(vec_ref, GROUP_GAIN, lanes) + vec(vec_ref, GROUP_SHIFT, lanes)
        gated.append(grouped * jax.nn.silu(valve_ref[0, :, lanes]))
    attended = x_ref[0].astype(f32) + times_weight(jnp.concatenate(gated, axis=1), weight_ref[...])
    attended_ref[0] = attended
    second = standard(attended)[0] * vec(vec_ref, GAIN2) + vec(vec_ref, BIAS2)
    second_ref[0] = second
    last_ref[0] = second[length - 1 :]


def pieces_of(total):
    cuts, at = [], 0
    while at < total:
        size = min(512, total - at)
        cuts.append((at, size))
        at += size
    return cuts


def channel_kernel(low, size, first, last, *refs, tick=nothing):
    refs = list(refs)
    take = lambda count: [refs.pop(0) for _ in range(count)]
    second_ref, ahead_ref, received_ref, grad_ref, cols_ref, vec_ref, expand_any, shrink_any = take(8)
    filter_ref = take(1)[0] if first or last else None
    gate_ref = None if first else take(1)[0]
    total_in, inner_in = (None, None) if first else take(2)
    attended_ref = take(1)[0] if last else None
    gate_out = take(1)[0] if first else None
    if last:
        block_ref, d_second_ref, d_row_ref, d_filter_ref, d_vec_ref = take(5)
    else:
        total_out, inner_out = take(2)
    d_expand_ref, d_shrink_ref, hidden_ref, expand_ref, shrink_ref, sems, carry_ref = refs
    tiles = pl.num_programs(1)
    batch, turn = pl.program_id(0), pl.program_id(1)
    tile = tiles - 1 - turn
    start = jnp.logical_and(batch == 0, turn == 0)

    @pl.when(start)
    def _():
        loads = [
            pltpu.make_async_copy(expand_any.at[:, pl.ds(low, size)], expand_ref, sems.at[0]),
            pltpu.make_async_copy(shrink_any.at[pl.ds(low, size)], shrink_ref, sems.at[1]),
        ]
        for load in loads:
            load.start()
        for ref in [d_expand_ref, d_shrink_ref] + ([d_filter_ref, d_vec_ref] if last else []):
            ref[...] = jnp.zeros_like(ref)
        for load in loads:
            load.wait()

    keep = cols_ref[0, :, 1:2]
    second = second_ref[0]
    before = jnp.where(tile == 0, received_ref[0], ahead_ref[0, 7:8])
    earlier = shifted(second, before, keep)
    difference = second - earlier
    mix_e, mix_f = vec(vec_ref, MIX_E), vec(vec_ref, MIX_F)
    inner_h, inner_l = split(earlier + mix_e * difference)
    if first or last:
        side_h, side_l = split(earlier + mix_f * difference)
    if first:
        gate = jax.nn.sigmoid(dot(side_h, filter_ref[...]) + dot(side_l, filter_ref[...]))
        gate_out[0] = gate
    else:
        gate = gate_ref[0]
    grad = grad_ref[0].astype(f32)
    dt_h, dt_l = split(grad * gate)
    total = jnp.zeros(second.shape, f32) if first else total_in[0]
    d_inner = jnp.zeros(second.shape, f32) if first else inner_in[0]
    for at, wide in pieces_of(size):
        if at:
            tick()
        lanes = slice(at, at + wide)
        raw = jnp.maximum(dot(inner_h, expand_ref[:, lanes]) + dot(inner_l, expand_ref[:, lanes]), 0.0)
        hid_h, hid_l = split(raw * raw)
        total = total + dot(hid_h, shrink_ref[lanes, :]) + dot(hid_l, shrink_ref[lanes, :])
        d_hidden = dot_nt(dt_h, shrink_ref[lanes, :]) + dot_nt(dt_l, shrink_ref[lanes, :])
        dr_h, dr_l = split(d_hidden * (2.0 * raw))
        d_shrink_ref[lanes, :] += dot_tn(hid_h, dt_h) + dot_tn(hid_l, dt_h) + dot_tn(hid_h, dt_l)
        d_expand_ref[:, lanes] += dot_tn(inner_h, dr_h) + dot_tn(inner_l, dr_h) + dot_tn(inner_h, dr_l)
        d_inner = d_inner + dot_nt(dr_h, expand_ref[:, lanes]) + dot_nt(dr_l, expand_ref[:, lanes])
    if not last:
        total_out[0] = total
        inner_out[0] = d_inner
        return
    block_ref[0] = (attended_ref[0] + gate * total).astype(bf16)
    ds_h, ds_l = split(grad * total * (gate * (1.0 - gate)))
    d_filter_ref[...] += dot_tn(side_h, ds_h) + dot_tn(side_l, ds_h) + dot_tn(side_h, ds_l)
    d_side = dot_nt(ds_h, filter_ref[...]) + dot_nt(ds_l, filter_ref[...])
    d_vec_ref[0:1] += jnp.sum(d_inner * difference, axis=0, keepdims=True)
    d_vec_ref[1:2] += jnp.sum(d_side * difference, axis=0, keepdims=True)
    direct = mix_e * d_inner + mix_f * d_side
    passed = (d_inner + d_side - direct) * keep
    rows = lax.broadcasted_iota(jnp.int32, second.shape, 0)
    above = pltpu.roll(passed, second.shape[0] - 1, 0)
    outside = jnp.where(turn == 0, 0.0, carry_ref[...])
    d_second_ref[0] = direct + jnp.where(rows == second.shape[0] - 1, outside, above)
    carry_ref[...] = passed[0:1]
    d_row_ref[0] = passed[0:1]


def attention_back_kernel(
    d_second_ref, back_ref, attended_ref, grad_ref, wkv_ref, valve_ref, recept_ref, cols_ref, vec_ref, weight_ref,
    x_ref, before_ref, d_attended_ref, d_wkv_ref, d_valve_ref, carry_ref, d_weight_ref, d_gate_ref, d_vec_ref,
    tick=nothing,
):
    length, width = attended_ref.shape[1:]

    @pl.when(pl.program_id(0) == 0)
    def _():
        for ref in (d_weight_ref, d_gate_ref, d_vec_ref):
            ref[...] = jnp.zeros_like(ref)

    rows = lax.broadcasted_iota(jnp.int32, (length, width), 0)
    d_second = d_second_ref[0] + jnp.where(rows == length - 1, back_ref[0], 0.0)
    normal2, scale2 = standard(attended_ref[0])
    d_vec_ref[2:3] += jnp.sum(d_second * normal2, axis=0, keepdims=True)
    d_vec_ref[3:4] += jnp.sum(d_second, axis=0, keepdims=True)
    d_attended = grad_ref[0].astype(f32) + standard_back(d_second * vec(vec_ref, GAIN2), normal2, scale2)
    d_attended_ref[0] = d_attended
    d_gated = times_weight_t(d_attended, weight_ref[...])
    steps = lax.broadcasted_iota(jnp.int32, (length, PAIR), 0).astype(f32)
    ones = head_ones(1.0 / LANE_FEATURES)
    fresh = cols_ref[0, :, 2:3]
    gated = []
    for pair in range(width // PAIR):
        lanes = slice(pair * PAIR, (pair + 1) * PAIR)
        wkv = wkv_ref[0, :, lanes]
        centred = wkv - head_sum(wkv, ones)
        scale = lax.rsqrt(head_sum(centred * centred, ones) + 0.00064)
        normal = centred * scale
        grouped = normal * vec(vec_ref, GROUP_GAIN, lanes) + vec(vec_ref, GROUP_SHIFT, lanes)
        valve = valve_ref[0, :, lanes]
        sigmoid = jax.nn.sigmoid(valve)
        gate = valve * sigmoid
        gated.append(grouped * gate)
        d_here = d_gated[:, lanes]
        d_valve_ref[0, :, lanes] = d_here * grouped * (sigmoid * (1.0 + valve * (1.0 - sigmoid)))
        d_grouped = d_here * gate
        d_vec_ref[0:1, lanes] += jnp.sum(d_grouped * normal, axis=0, keepdims=True)
        d_vec_ref[1:2, lanes] += jnp.sum(d_grouped, axis=0, keepdims=True)
        d_normal = d_grouped * vec(vec_ref, GROUP_GAIN, lanes)
        d_wkv = scale * (d_normal - head_sum(d_normal, ones) - normal * head_sum(d_normal * normal, ones))
        d_wkv_ref[0, :, lanes] = d_wkv
        query = recept_ref[0, :, lanes] * jnp.exp(vec(vec_ref, DECAY, lanes) * steps) * fresh
        carry_ref[0, pair] = compact(outer_sum(query, d_wkv))
        if pair == width // PAIR // 2 - 1:
            tick()
    tick()
    d_weight_ref[...] += outer_sum(jnp.concatenate(gated, axis=1), d_attended)
    tick()
    gain, bias = vec(vec_ref, GAIN), vec(vec_ref, BIAS)
    normal = standard(x_ref[0].astype(f32))[0] * gain + bias
    earlier = shifted(normal, standard(before_ref[0])[0] * gain + bias, cols_ref[0, :, 1:2])
    d_gate_ref[...] += outer_sum(earlier + vec(vec_ref, MIX_G) * (normal - earlier), d_valve_ref[0])


def mix_back_kernel(
    recept_ref, keys_ref, values_ref, grad_ref, state_ref, cols_ref, row_ref, vec_ref,
    d_recept_ref, d_keys_ref, d_values_ref, d_vec_ref,
):
    length = recept_ref.shape[1]
    blocks = length // BLOCK
    first = first_lanes(BLOCK)
    log_decay, boost = vec(vec_ref, DECAY), vec(vec_ref, BOOST)
    step, fall, rise, whole = decays(log_decay)
    ones = head_ones(1.0)
    square = widen(state_ref[0, 0])
    queries, near, far, values, grads = [], [], [], [], []
    for at in range(blocks):
        here = pl.ds(at * BLOCK, BLOCK)
        queries.append(cut(recept_ref[0, here] * fall))
        raised = keys_ref[0, here] * rise
        near.append(cut(raised))
        far.append(raised * whole)
        values.append(cut(values_ref[0, here]))
        grads.append(cut(grad_ref[0, here]))
    zero = jnp.zeros((BLOCK, PAIR), f32)
    d_query = [[zero, zero] for _ in range(blocks)]
    d_value = [[zero, zero] for _ in range(blocks)]
    d_near = [[zero, zero] for _ in range(blocks)]
    d_far = [[zero, zero] for _ in range(blocks)]
    for at in range(blocks):
        for of in range(at + 1):
            mask = allowed_here(cols_ref, row_ref, at, of, False)
            t_row = row_ref[0, :, pl.ds(at * BLOCK, BLOCK)]
            s_col = cols_ref[0, pl.ds(of * BLOCK, BLOCK), 0:1]
            mask_t = s_col == t_row
            if at == of:
                shape = (BLOCK, BLOCK)
                mask_t = jnp.logical_and(
                    mask_t, lax.broadcasted_iota(jnp.int32, shape, 0) < lax.broadcasted_iota(jnp.int32, shape, 1)
                )
            gap = jnp.exp(log_decay * (BLOCK * (at - of - 1))) if at > of + 1 else None
            keys = near[of] if of == at else cut(far[of] if gap is None else far[of] * gap)
            for head in range(2):
                q_hl = high_low(queries[at], first, head)
                g_hl = high_low(grads[at], first, head)
                k_hl = high_low(keys, first, head)
                v_hl = high_low(values[of], first, head)
                scores_t = dot_nt(twice(k_hl), doubled(queries[at], first, head))
                s_h, s_l = split(jnp.where(mask_t, scores_t, 0.0))
                d_value[of][head] = d_value[of][head] + dot(s_h, g_hl) + dot(s_l, g_hl)
                d_scores = dot_nt(twice(g_hl), doubled(values[of], first, head))
                s_h, s_l = split(jnp.where(mask, d_scores, 0.0))
                d_query[at][head] = d_query[at][head] + dot(s_h, k_hl) + dot(s_l, k_hl)
                d_scores_t = dot_nt(twice(v_hl), doubled(grads[at], first, head))
                s_h, s_l = split(jnp.where(mask_t, d_scores_t, 0.0))
                d_key = dot(s_h, q_hl) + dot(s_l, q_hl)
                if of == at:
                    d_near[of][head] = d_key
                else:
                    if gap is not None:
                        d_key = d_key * gap
                    d_far[of][head] = d_far[of][head] + d_key
    d_decay = jnp.zeros((1, PAIR), f32)
    d_boost = jnp.zeros((1, PAIR), f32)
    for at in range(blocks):
        here = pl.ds(at * BLOCK, BLOCK)
        recept, keys, value, grad = recept_ref[0, here], keys_ref[0, here], values_ref[0, here], grad_ref[0, here]
        fresh = cols_ref[0, here, 2:3]
        d_in = folded(d_query[at], first) * fall
        d_state = times_state_t(grad, square) * (fall * jnp.exp(log_decay * (BLOCK * at)) * fresh)
        d_here = folded(d_near[at], first) * rise
        d_later = folded(d_far[at], first) * (rise * whole)
        present = head_sum(recept * boost * keys, ones)
        d_present = head_sum(grad * value, ones)
        d_recept_ref[0, here] = d_in + d_state + boost * keys * d_present
        d_keys_ref[0, here] = d_here + d_later + boost * recept * d_present
        d_values_ref[0, here] = folded(d_value[at], first) + present * grad
        d_boost = d_boost + jnp.sum(recept * keys * d_present, axis=0, keepdims=True)
        d_decay = d_decay + jnp.sum(
            recept * (step * d_in + (step + float(BLOCK * at)) * d_state)
            + keys * ((BLOCK - 1.0 - step) * d_later - (step + 1.0) * d_here),
            axis=0,
            keepdims=True,
        )
    d_vec_ref[0, 0:1] = d_decay
    d_vec_ref[0, 1:2] = d_boost


def project_back_kernel(
    x_ref, before_ref, cols_ref, vec_ref, d_attended_ref,
    d_recept_ref, d_keys_ref, d_values_ref, d_valve_ref, keys_ref, values_ref, state_ref, out_state_ref,
    mix_vec_ref, attention_vec_ref, channel_vec_ref, w_r, w_k, w_v, w_g,
    d_x_ref, d_row_ref, packed_ref, dw_r, dw_k, dw_v,
    earlier_ref, difference_ref, direct_ref, passed_ref,
):
    length, width = x_ref.shape[1:]
    turn = pl.program_id(1)
    gain, bias = vec(vec_ref, GAIN), vec(vec_ref, BIAS)
    steps = lax.broadcasted_iota(jnp.int32, (length, PAIR), 0).astype(f32)
    pairs = [(pair, slice(pair * PAIR, (pair + 1) * PAIR)) for pair in range(width // PAIR)]

    @pl.when(jnp.logical_and(pl.program_id(0) == 0, turn == 0))
    def _():
        for ref in (packed_ref, dw_r, dw_k, dw_v):
            ref[...] = jnp.zeros_like(ref)
        packed_ref[GROUP_GAIN : BIAS2 + 1] = attention_vec_ref[...]
        packed_ref[MIX_E : MIX_F + 1] = channel_vec_ref[...]

    def tail_of(lanes):
        return jnp.exp(vec(vec_ref, DECAY, lanes) * (length - 1.0 - steps)) * cols_ref[0, :, 3:4]

    def through(grad, which, weight, d_weight, first=False):
        mix, difference = vec(vec_ref, which), difference_ref[...]
        gh, gl = split(grad)
        if d_weight is not None:
            mh, ml = split(earlier_ref[...] + mix * difference)
            d_weight[...] += dot_tn(mh, gh) + dot_tn(ml, gh) + dot_tn(mh, gl)
        d_mixed = dot_nt(gh, weight[...]) + dot_nt(gl, weight[...])
        packed_ref[which : which + 1] += jnp.sum(d_mixed * difference, axis=0, keepdims=True)
        direct, passed = mix * d_mixed, d_mixed - mix * d_mixed
        direct_ref[...] = direct if first else direct_ref[...] + direct
        passed_ref[...] = passed if first else passed_ref[...] + passed

    @pl.when(turn == 0)
    def _():
        normal = standard(x_ref[0].astype(f32))[0] * gain + bias
        before = standard(before_ref[0])[0] * gain + bias
        earlier = shifted(normal, before, cols_ref[0, :, 1:2])
        earlier_ref[...] = earlier
        difference_ref[...] = normal - earlier
        through(d_recept_ref[0], MIX_R, w_r, dw_r, True)
        packed_ref[DECAY : BOOST + 1] += mix_vec_ref[0]

    @pl.when(turn == 1)
    def _():
        through(d_valve_ref[0], MIX_G, w_g, None)

    @pl.when(turn == 2)
    def _():
        parts = []
        for pair, lanes in pairs:
            d_keys = times_state_t(values_ref[0, :, lanes], widen(out_state_ref[0, pair])) * tail_of(lanes)
            later = (length - 1.0 - steps) * keys_ref[0, :, lanes] * d_keys
            both = widen(state_ref[0, pair]) * widen(out_state_ref[0, pair])
            ones = jnp.ones((8, PAIR), bf16)
            kept = sum([dot_nt(ones, part)[0:1] for part in split(both)])
            kept = kept * jnp.exp(vec(vec_ref, DECAY, lanes) * length) * (float(length) * cols_ref[0, length - 1 :, 2:3])
            packed_ref[DECAY : DECAY + 1, lanes] += jnp.sum(later, axis=0, keepdims=True) + kept
            parts.append(d_keys_ref[0, :, lanes] + d_keys)
        through(jnp.concatenate(parts, axis=1), MIX_K, w_k, dw_k)

    @pl.when(turn == 3)
    def _():
        parts = []
        for pair, lanes in pairs:
            ended = times_state(keys_ref[0, :, lanes] * tail_of(lanes), widen(out_state_ref[0, pair]))
            parts.append(d_values_ref[0, :, lanes] + ended)
        through(jnp.concatenate(parts, axis=1), MIX_V, w_v, dw_v)
        passed = passed_ref[...] * cols_ref[0, :, 1:2]
        rows = lax.broadcasted_iota(jnp.int32, (length, width), 0)
        d_normal = direct_ref[...] + jnp.where(rows == length - 1, 0.0, pltpu.roll(passed, length - 1, 0))
        hat, scale = standard(x_ref[0].astype(f32))
        hat_before, scale_before = standard(before_ref[0])
        out = passed[0:1]
        packed_ref[GAIN : GAIN + 1] += jnp.sum(d_normal * hat, axis=0, keepdims=True) + out * hat_before
        packed_ref[BIAS : BIAS + 1] += jnp.sum(d_normal, axis=0, keepdims=True) + out
        d_x_ref[0] = d_attended_ref[0] + standard_back(d_normal * gain, hat, scale)
        d_row_ref[0] = standard_back(out * gain, hat_before, scale_before)

        @pl.when(pl.program_id(0) == pl.num_programs(0) - 1)
        def _():
            packed_ref[DECAY : DECAY + 1] = packed_ref[DECAY : DECAY + 1] * vec(vec_ref, DECAY)


def call(kernel, grid, ins, outs, name, scratch=(), flops=0, hosts=(), collective_id=None, ticks=1):
    bytes_accessed = sum(a.size * a.dtype.itemsize for a, _, _ in ins)
    for shape, dtype, _, _ in outs:
        size = jnp.dtype(dtype).itemsize
        for extent in shape:
            size *= extent
        bytes_accessed += size

    def spec(block, index):
        if block == "smem":
            return pl.BlockSpec(memory_space=pltpu.SMEM)
        if block == "any":
            return pl.BlockSpec(memory_space=pl.ANY)
        if index is None:
            return pl.BlockSpec(block, lambda *_: (0,) * len(block), pipeline_mode=pl.Buffered(1))
        return pl.BlockSpec(block, index)

    ins, outs, scratch = list(ins), list(outs), list(scratch)
    own, places, aliases = (len(ins), len(outs), len(scratch)), [], {}
    for exchange, _ in hosts:
        more_in, more_out, alias = exchange.operands()
        aliases.update({len(ins) + i: len(outs) + j for i, j in alias})
        place = [len(ins), len(outs), len(scratch)]
        ins, outs, scratch = ins + more_in, outs + more_out, scratch + exchange.scratch()
        places.append([slice(a, b) for a, b in zip(place, (len(ins), len(outs), len(scratch)))])
    steps = 1
    for extent in grid:
        steps *= extent

    def body(*refs):
        in_refs, out_refs, scratch_refs = refs[: len(ins)], refs[len(ins) : len(ins) + len(outs)], refs[len(ins) + len(outs) :]
        step = pl.program_id(0)
        for axis in range(1, len(grid)):
            step = step * grid[axis] + pl.program_id(axis)
        for (exchange, _), (i, o, t) in zip(hosts, places):
            exchange.bind(in_refs[i], out_refs[o], scratch_refs[t])

        def enter():
            barrier = pltpu.get_barrier_semaphore()
            partners = [partner for exchange, _ in hosts for partner in exchange.partners()]
            for partner in partners:
                pl.semaphore_signal(barrier, inc=1, device_id=(partner,), device_id_type=MESH)
            pl.semaphore_wait(barrier, len(partners))
            for exchange, _ in hosts:
                exchange.start()

        def advance(turn):
            for exchange, ends in hosts:
                due = [slot for slot in range(exchange.slots) if min(ends[slot], steps * ticks) == turn]
                if due:

                    @pl.when(step == min(turn // ticks, steps - 1))
                    def _():
                        for slot in due:
                            exchange.run(slot)

        if hosts:
            pl.when(step == 0)(enter)
        for turn in range(steps):
            advance(turn * ticks)
        passed = []

        def tick():
            passed.append(0)
            if len(passed) < ticks:
                for turn in range(steps):
                    advance(turn * ticks + len(passed))

        more = {"tick": tick} if ticks > 1 else {}
        kernel(*in_refs[: own[0]], *out_refs[: own[1]], *scratch_refs[: own[2]], **more)
        advance(steps * ticks)
        if hosts:

            @pl.when(step == steps - 1)
            def _():
                for exchange, _ in hosts:
                    exchange.close()

    params = {"collective_id": collective_id, "has_side_effects": True} if hosts else {}
    return pl.pallas_call(
        body,
        grid=grid,
        in_specs=[spec(block, index) for _, block, index in ins],
        out_specs=[spec(block, index) for _, _, block, index in outs],
        out_shape=[jax.ShapeDtypeStruct(shape, dtype) for shape, dtype, _, _ in outs],
        input_output_aliases=aliases,
        scratch_shapes=scratch,
        compiler_params=pltpu.CompilerParams(
            dimension_semantics=("arbitrary",) * len(grid), vmem_limit_bytes=VMEM_LIMIT, **params
        ),
        cost_estimate=pl.CostEstimate(flops=flops, bytes_accessed=bytes_accessed, transcendentals=0),
        name=name,
    )(*[a for a, _, _ in ins])


def moved(value, steps):
    count = lax.axis_size("seq")
    low, high = max(0, -steps), min(count, count - steps)
    return lax.ppermute(value, "seq", [(source, source + steps) for source in range(low, high)])


def reach(count):
    window, needed, hops = 2, {32: 16, 128: 32}.get(count, count) // 2, []
    while window < needed:
        hops.append(window)
        window *= 2
    return hops


class Carrier:
    def __init__(self, parts, lengths, vectors, length, sign, begin=0, end=None):
        self.count = lax.axis_size("seq")
        self.parts, self.lengths, self.vectors, self.length, self.sign = parts, lengths, vectors, length, sign
        self.hops = [[1, 2]] + [[hop] for hop in reach(self.count)]
        self.whole = len(self.hops) + 2
        self.begin, self.end = begin, self.whole if end is None else end
        self.slots = self.end - self.begin
        batches, pairs = parts[0].shape[:2]
        self.half = pairs // 2 if begin == 0 else pairs
        self.shape = (batches, self.half) + parts[0].shape[2:]

    def operands(self):
        shape = self.shape
        full = (shape[0], 2 * self.half) + shape[2:]
        outs = [(full, f32, full, None)] if self.end == self.whole else [(shape, f32, shape, None)] * 2
        ins = [(part, part.shape, None) for part in self.parts]
        return ins + [(self.vectors, self.vectors.shape, None), (self.lengths, "smem", None)], outs, []

    def scratch(self):
        return [
            pltpu.VMEM((self.slots, 2) + self.shape, f32),
            pltpu.VMEM((self.slots + 1,) + self.shape, f32),
            pltpu.VMEM((2,) + self.shape, f32),
            pltpu.SemaphoreType.DMA((self.slots, 2)),
            pltpu.SemaphoreType.DMA((self.slots, 2)),
        ]

    def bind(self, ins, outs, scratch):
        *self.part_refs, self.vec_ref, self.lengths_ref = ins
        self.out_refs = outs
        self.landed, self.totals, self.kept, self.send_sems, self.recv_sems = scratch
        self.mine = lax.axis_index("seq")
        self.core, self.chip = self.mine % 2, self.mine // 2
        self.sibling = self.mine + 1 - 2 * self.core

    def chip_at(self, hop):
        chips = self.count // 2
        return (self.chip + hop + chips) % chips * 2 + self.core

    def partners(self):
        out = []
        for slot in range(self.begin, self.end):
            if slot in (0, self.whole - 1):
                out.append(self.sibling)
            else:
                out += [self.chip_at(sign * hop) for hop in self.hops[slot - 1] for sign in (1, -1)]
        return out

    def first_part(self):
        return self.kept.at[0] if self.begin == 0 else self.part_refs[1]

    def total(self, slot):
        return self.part_refs[0] if slot == self.begin and slot > 0 else self.totals.at[slot - self.begin]

    def copies(self, slot):
        at = slot - self.begin
        if slot == 0:
            away = self.part_refs[0].at[:, pl.ds((1 - self.core) * self.half, self.half)]
            moves = [(away, self.landed.at[at, 0], self.sibling)]
        elif slot == self.whole - 1:
            moves = [(self.kept.at[1], self.landed.at[at, 0], self.sibling)]
        else:
            moves = [
                (self.total(slot), self.landed.at[at, i], self.chip_at(self.sign * hop))
                for i, hop in enumerate(self.hops[slot - 1])
            ]
        return [
            pltpu.make_async_remote_copy(
                src_ref=source, dst_ref=target, send_sem=self.send_sems.at[at, i], recv_sem=self.recv_sems.at[at, i],
                device_id=(device,), device_id_type=MESH,
            )
            for i, (source, target, device) in enumerate(moves)
        ]

    def start(self):
        self.open(self.begin)

    def open(self, slot):
        if slot == self.whole - 1:
            self.finish()
        for copy in self.copies(slot):
            copy.start()

    def fade(self, pair, devices):
        lane = lax.broadcasted_iota(jnp.int32, (LANE_FEATURES, PAIR), 1)
        row = lax.broadcasted_iota(jnp.int32, (LANE_FEATURES, PAIR), 0)
        at = pl.multiple_of((self.core * self.half + pair) * PAIR, PAIR)
        decay = self.vec_ref[DECAY : DECAY + 1, pl.ds(at, PAIR)] * float(self.length * devices)
        heads = [
            jnp.sum(jnp.where(lane == row + head * LANE_FEATURES, decay, 0.0), axis=1, keepdims=True) for head in range(2)
        ]
        return jnp.exp(jnp.where(first_lanes(LANE_FEATURES), heads[0], heads[1]))

    def same(self, batch, bound, other):
        bounds = bounds_of(self.lengths_ref, batch)
        ends = [segment_of(bounds, (device + 1) * self.length - 1) for device in (bound, other)]
        return jnp.where(ends[0] == ends[1], 1.0, 0.0).astype(f32)

    def edges(self):
        middle = 2 * self.chip
        return middle - self.sign, middle, middle + self.sign

    def run(self, slot):
        slot = slot + self.begin
        at = slot - self.begin
        for copy in self.copies(slot):
            copy.wait()
        batches = self.shape[0]
        entry, middle, leaving = self.edges()
        if slot == 0:
            flags = [self.same(batch, middle, leaving) for batch in range(batches)]
            is_first = self.core == (0 if self.sign > 0 else 1)
            for pair in range(self.half):
                fade = self.fade(pair, 1)
                for batch in range(batches):
                    own = self.part_refs[0][batch, self.core * self.half + pair]
                    other = self.landed[at, 0, batch, pair]
                    ahead, behind = jnp.where(is_first, own, other), jnp.where(is_first, other, own)
                    self.kept[0, batch, pair] = ahead
                    self.totals[at + 1, batch, pair] = ahead * fade * flags[batch] + behind
        elif slot < self.whole - 1:
            hops = self.hops[slot - 1]
            chips = self.count // 2
            flags = []
            for hop in hops:
                there = self.chip - self.sign * hop
                exists = jnp.where(jnp.logical_and(there >= 0, there < chips), 1.0, 0.0).astype(f32)
                crossed = hop - 1 if slot == 1 else hop
                flags.append([exists * self.same(batch, entry - 2 * self.sign * crossed, entry) for batch in range(batches)])
            for pair in range(self.half):
                fade = self.fade(pair, 2 if slot == 1 else 2 * hops[0])
                for batch in range(batches):
                    if slot == 1:
                        near, far = self.landed[at, 0, batch, pair], self.landed[at, 1, batch, pair]
                        here = near * flags[0][batch] + far * fade * flags[1][batch]
                    else:
                        here = self.total(slot)[batch, pair] + self.landed[at, 0, batch, pair] * fade * flags[0][batch]
                    self.totals[at + 1, batch, pair] = here
        else:
            for pair in range(self.half):
                for batch in range(batches):
                    self.out_refs[0][batch, (1 - self.core) * self.half + pair] = self.landed[at, 0, batch, pair]
        if slot + 1 < self.end:
            self.open(slot + 1)
        elif self.end < self.whole:
            self.out_refs[0][...] = self.totals[at + 1]
            self.out_refs[1][...] = self.first_part()[...]

    def close(self):
        pass

    def finish(self):
        entry, middle, _ = self.edges()
        total, first_part = self.total(self.whole - 1), self.first_part()
        is_first = self.core == (0 if self.sign > 0 else 1)
        flags = [self.same(batch, entry, middle) for batch in range(self.shape[0])]
        for pair in range(self.half):
            fade = self.fade(pair, 1)
            for batch in range(self.shape[0]):
                first = total[batch, pair]
                second = first * fade * flags[batch] + first_part[batch, pair]
                self.out_refs[0][batch, self.core * self.half + pair] = jnp.where(is_first, first, second)
                self.kept[1, batch, pair] = jnp.where(is_first, second, first)


def bit_orders(count):
    bits = count.bit_length() - 1
    if bits == 5:
        return [(0, 1, 2, 3, 4), (0, 2, 3, 1, 4), (0, 3, 1, 2, 4)]
    chip = list(range(1, bits))
    third = max(1, len(chip) // 3)
    return [tuple([0] + chip[k * third :] + chip[: k * third]) for k in range(3)]


class Unit:
    def __init__(self, array, first, rows, width, order, group, begin, end):
        self.array, self.first, self.rows, self.width, self.group = array, first, rows, width, group
        self.steps, size, landing = [], rows, 0
        bits = self.bits = len(order)
        for k, bit in enumerate(order):
            halved = size % 16 == 0
            sent = size // 2 if halved else size
            self.steps.append((bit, halved, sent, landing))
            if begin <= k < end:
                landing += sent
            size = sent
        phases = [p for p in range(2 * bits) if p < bits or self.steps[2 * bits - 1 - p][1]]
        self.phases = [p for p in phases if begin <= p < end]
        self.sums = [p for p in self.phases if p < bits]
        self.landing = landing
        self.held = self.steps[self.sums[0]][2] if self.sums else 0
        self.stages = len(self.phases)


def add_rows(target, at, source, source_at, rows):
    block = next(b for b in (64, 56, 48, 32, 24, 16, 8) if rows % b == 0)

    def step(i, _):
        here = pl.ds(pl.multiple_of(at + i * block, 8), block)
        target[here] = target[here] + source[pl.ds(pl.multiple_of(source_at + i * block, 8), block)]
        return 0

    lax.fori_loop(0, rows // block, step, 0)


def rows8(at, size):
    return pl.ds(pl.multiple_of(at, 8), size)


class Summer:
    def __init__(self, arrays, layout):
        self.count, self.arrays, self.units = lax.axis_size("seq"), arrays, []
        orders = bit_orders(self.count)
        for array, first, rows, parts, group, turn, begin, end in layout:
            size = rows // parts
            for part in range(parts):
                order, width = orders[(turn + part) % 3], arrays[array].shape[1]
                self.units.append(Unit(array, first + part * size, size, width, order, group, begin, end))
        self.groups = sorted({unit.group for unit in self.units})
        self.stages = max(unit.stages for unit in self.units)
        self.slots = self.stages + len(self.groups) - 1

    def operands(self):
        arrays = self.arrays
        return (
            [(a, "any", None) for a in arrays],
            [(a.shape, a.dtype, "any", None) for a in arrays],
            [(i, i) for i in range(len(arrays))],
        )

    def scratch(self):
        return (
            [pltpu.VMEM((max(8, unit.held), unit.width), f32) for unit in self.units]
            + [pltpu.VMEM((max(8, unit.landing), unit.width), f32) for unit in self.units]
            + [
                pltpu.SemaphoreType.DMA((len(self.units), self.stages)),
                pltpu.SemaphoreType.DMA((len(self.units), self.stages)),
                pltpu.SemaphoreType.DMA((len(self.units), 2)),
                pltpu.SemaphoreType.REGULAR((len(self.units),)),
            ]
        )

    def bind(self, ins, outs, scratch):
        size = len(self.units)
        self.refs, self.held, self.landed = outs, scratch[:size], scratch[size : 2 * size]
        self.send_sems, self.recv_sems, self.local_sems, self.free_sems = scratch[2 * size :]
        mine = lax.axis_index("seq")
        bits = self.count.bit_length() - 1
        self.bit = [mine // (1 << k) % 2 for k in range(bits)]
        self.partner = [mine + (1 - 2 * self.bit[k]) * (1 << k) for k in range(bits)]
        self.offsets = []
        for unit in self.units:
            at, seen = 0, [0]
            for which, halved, sent, _ in unit.steps:
                at = at + self.bit[which] * sent if halved else at
                seen.append(at)
            self.offsets.append(seen)

    def partners(self):
        used = sorted({unit.steps[min(p, 2 * unit.bits - 1 - p)][0] for unit in self.units for p in unit.phases})
        return [self.partner[k] for k in used]

    def start(self):
        for group in self.groups:
            for u, unit in enumerate(self.units):
                if unit.group == group:
                    self.begin(u, 0)

    def own(self, u, step):
        unit = self.units[u]
        return self.refs[unit.array].at[rows8(unit.first + self.offsets[u][step + 1], unit.steps[step][2])]

    def copies(self, u, stage):
        unit, seen, here = self.units[u], self.offsets[u], self.refs[self.units[u].array]
        phase, out = unit.phases[stage], []
        if phase < unit.bits:
            which, halved, sent, landing = unit.steps[phase]
            away = seen[phase] + (1 - self.bit[which]) * sent if halved else seen[phase]
            target = self.landed[u].at[pl.ds(landing, sent)]
            if stage == 0:
                source = here.at[rows8(unit.first + away, sent)]
                out.append(pltpu.make_async_copy(self.own(u, phase), self.held[u], self.local_sems.at[u, 0]))
            else:
                source = self.held[u].at[rows8(away - seen[unit.sums[0] + 1], sent)]
        else:
            step = 2 * unit.bits - 1 - phase
            which, _, sent, _ = unit.steps[step]
            source = target = self.own(u, step)
            if unit.sums and stage == len(unit.sums):
                source = self.held[u].at[rows8(seen[step + 1] - seen[unit.sums[0] + 1], sent)]
        return out + [
            pltpu.make_async_remote_copy(
                src_ref=source, dst_ref=target, send_sem=self.send_sems.at[u, stage],
                recv_sem=self.recv_sems.at[u, stage], device_id=(self.partner[which],), device_id_type=MESH,
            )
        ]

    def store(self, u):
        unit, seen = self.units[u], self.offsets[u]
        step = unit.sums[-1]
        source = self.held[u].at[rows8(seen[step + 1] - seen[unit.sums[0] + 1], unit.steps[step][2])]
        return pltpu.make_async_copy(source, self.own(u, step), self.local_sems.at[u, 1])

    def returns(self, u):
        unit = self.units[u]
        back = 2 * unit.bits - 1 - unit.phases[0]
        return unit.phases.index(back) if unit.sums and back in unit.phases else None

    def begin(self, u, stage):
        if stage == self.returns(u):
            pl.semaphore_wait(self.free_sems.at[u], 1)
        for copy in self.copies(u, stage):
            copy.start()

    def end(self, u, stage):
        unit, seen = self.units[u], self.offsets[u]
        for copy in self.copies(u, stage):
            copy.wait()
        phase, sums = unit.phases[stage], len(unit.sums)
        if stage == 0 and self.returns(u) is not None:
            partner = self.partner[unit.steps[phase][0]]
            pl.semaphore_signal(self.free_sems.at[u], inc=1, device_id=(partner,), device_id_type=MESH)
        if phase < unit.bits:
            _, _, sent, landing = unit.steps[phase]
            add_rows(self.held[u], seen[phase + 1] - seen[unit.sums[0] + 1], self.landed[u], landing, sent)
            if stage == sums - 1:
                self.store(u).start()
        elif sums and stage == sums:
            self.store(u).wait()

    def close(self):
        for u, unit in enumerate(self.units):
            if unit.sums and unit.stages == len(unit.sums):
                self.store(u).wait()

    def run(self, slot):
        for place, group in enumerate(self.groups):
            for u, unit in enumerate(self.units):
                stage = slot - place
                if unit.group != group:
                    continue
                if unit.phases[0] >= unit.bits and unit.phases[-1] == 2 * unit.bits - 1 and stage >= unit.stages - 1:
                    stage = unit.stages - 1 if slot == self.slots - 1 else -1
                if 0 <= stage < unit.stages:
                    self.end(u, stage)
                    if stage + 1 < unit.stages:
                        self.begin(u, stage + 1)


def summed_over_devices(arrays, layout, collective_id):
    summer = Summer(arrays, layout)
    return call(nothing, (1,), [], [], "sum_over_devices", hosts=[(summer, [1] * summer.slots)], collective_id=collective_id)


def gather_kernel(moves, *refs):
    count = len(moves)
    ins, row_ref, (*outs, sems) = refs[:count], refs[count], refs[count + 1 :]
    buffers, outs = outs[-count:], outs[:-count]
    loads = [pltpu.make_async_copy(source, buffer, sems.at[0, i]) for i, (source, buffer) in enumerate(zip(ins, buffers))]
    for load in loads:
        load.start()
    stores = []
    for i, (out, row, column) in enumerate(moves):
        rows, columns = buffers[i].shape[-2:]
        loads[i].wait()
        if i == count - 1:
            for batch in range(row_ref.shape[0]):
                buffers[i][batch, rows - 1 :] += row_ref[batch]
            stores.append(pltpu.make_async_copy(buffers[i], outs[out], sems.at[1, i]))
            stores[-1].start()
            break
        stores.append(pltpu.make_async_copy(buffers[i], outs[out].at[pl.ds(row, rows), pl.ds(column, columns)], sems.at[1, i]))
        stores[-1].start()
    for store in stores:
        store.wait()


def gathered(arrays, spans, hidden_width, tokens, last_row):
    width = arrays[0].shape[0]
    moves, shapes = [], [(width, hidden_width), (hidden_width, width)]
    for low, _ in spans:
        moves += [(0, 0, low), (1, low, 0)]
    arrays = arrays + [tokens]
    for array in arrays[len(moves) :]:
        moves.append((len(shapes), 0, 0))
        shapes.append(array.shape)
    return call(
        functools.partial(gather_kernel, moves),
        (1,),
        [(a, "any", None) for a in arrays] + [(last_row, last_row.shape, None)],
        [(shape, f32, "any", None) for shape in shapes],
        "gather",
        scratch=[pltpu.VMEM(a.shape, f32) for a in arrays] + [pltpu.SemaphoreType.DMA((2, len(moves)))],
    )


def local(
    incoming_hidden,
    packed_run_lengths,
    prior_standardize_factor,
    prior_standardize_addend,
    respond_interpolant,
    address_interpolant,
    content_interpolant,
    valve_interpolant,
    respond_transform,
    address_transform,
    content_transform,
    valve_transform,
    damping_rates,
    immediate_boost,
    cluster_normal_factor,
    cluster_normal_shift_term,
    readout_transform,
    posterior_standardize_factor,
    posterior_standardize_addend,
    dense_address_interpolant,
    dense_respond_interpolant,
    dense_address_transform,
    dense_content_transform,
    dense_respond_transform,
    objective_adjoint,
):
    batches, length, width = incoming_hidden.shape
    hidden_width = dense_address_transform.shape[1]
    pairs = width // PAIR
    depth = lax.axis_size("seq").bit_length() - 1
    lengths = packed_run_lengths
    vectors = [
        prior_standardize_factor, prior_standardize_addend, respond_interpolant, address_interpolant,
        content_interpolant, valve_interpolant, damping_rates, immediate_boost, cluster_normal_factor,
        cluster_normal_shift_term, posterior_standardize_factor, posterior_standardize_addend,
        dense_address_interpolant, dense_respond_interpolant,
    ]

    def table(w):
        return (w, w.shape, None)

    def rows_of(a):
        return (a, (1,) + a.shape[1:], lambda b, *_: (b,) + (0,) * (a.ndim - 1))

    def rows_out(shape, dtype=f32):
        return (shape, dtype, (1,) + tuple(shape[1:]), lambda b, *_: (b,) + (0,) * (len(shape) - 1))

    def sum_out(*shape):
        return (shape, f32, shape, None)

    tokens, states, one_row = (batches, length, width), (batches, pairs, LANE_FEATURES, PAIR), (batches, 1, width)
    square_flops = 2 * batches * length * width * width
    before = moved(incoming_hidden[:, -1, :].astype(f32), 1)[:, None, :]
    cols, row, vectors = call(
        tokens_kernel,
        (1,),
        [(lengths, "smem", None)] + [table(v) for v in vectors],
        [sum_out(batches, length, 8), sum_out(batches, 1, length), sum_out(16, width)],
        "tokens",
    )
    common = [rows_of(incoming_hidden), rows_of(before), rows_of(cols), table(vectors)]
    keys, values, end_state = call(
        functools.partial(project_kernel, (MIX_K, MIX_V), True),
        (batches,),
        common + [table(address_transform), table(content_transform)],
        [rows_out(tokens)] * 2 + [rows_out(states)],
        "project_keys",
        flops=4 * square_flops,
    )
    nearest = Carrier([end_state], lengths, vectors, length, 1, 0, 2)
    recept, valve, *near_state = call(
        functools.partial(project_kernel, (MIX_R, MIX_G), False),
        (batches,),
        common + [table(respond_transform), table(valve_transform)],
        [rows_out(tokens)] * 2,
        "project_recept",
        flops=4 * square_flops,
        hosts=[(nearest, [batches // 2, batches])],
        collective_id=1,
    )
    by_pair = lambda a: (a, (1, length, PAIR), lambda b, p: (b, 0, p))
    pair_vectors = (vectors, (vectors.shape[0], PAIR), lambda b, p: (0, p))
    pair_state = lambda s: (s, (1, 1, LANE_FEATURES, PAIR), lambda b, p: (b, p, 0, 0))
    pair_out = (tokens, f32, (1, length, PAIR), lambda b, p: (b, 0, p))
    further = Carrier(near_state, lengths, vectors, length, 1, 2)
    steps = batches * pairs
    mixed, state = call(
        mix_kernel,
        (batches, pairs),
        [by_pair(recept), by_pair(keys), by_pair(values), rows_of(cols), rows_of(row), pair_vectors],
        [pair_out],
        "mix",
        flops=3 * 2 * batches * length * length * width * 2,
        hosts=[(further, [(i + 1) * steps // further.slots for i in range(further.slots)])],
        collective_id=2,
    )
    wkv, attended, second, second_row = call(
        readout_kernel,
        (batches,),
        [
            rows_of(mixed), rows_of(recept), rows_of(state), rows_of(valve), rows_of(cols), table(vectors),
            rows_of(incoming_hidden), table(readout_transform),
        ],
        [rows_out(tokens)] * 3 + [rows_out(one_row)],
        "readout",
        flops=2 * square_flops,
    )
    second_row = moved(second_row[:, 0, :], 1)[:, None, :]
    tiles = length // BLOCK
    tile_rows = lambda a: (a, (1, BLOCK, a.shape[2]), lambda b, i: (b, tiles - 1 - i, 0))
    ahead = (second, (1, 8, width), lambda b, i: (b, jnp.maximum((tiles - 1 - i) * (BLOCK // 8) - 1, 0), 0))
    tile_out = lambda dtype: (tokens, dtype, (1, BLOCK, width), lambda b, i: (b, tiles - 1 - i, 0))
    spans = [(at, min(1024, hidden_width - at)) for at in range(0, hidden_width, 1024)]
    ends = 2 * depth

    even = [(0, 0, 128, 0), (0, 128, 128, 1), (0, 256, 512, 2), (1, 0, 512, 0), (1, 512, 512, 1)]
    rest_units = [(2, 0, 768, 0), (0, 0, 768, 1), (1, 0, 512, 2), (1, 512, 128, 2)]
    two = [(0, 0, 512, 0), (0, 512, 256, 2), (1, 0, 512, 1), (1, 512, 256, 2)]

    def layout_of(units, group, begin, end, base=0):
        return [(base + i, first, rows, 1, group, order, begin, end) for i, first, rows, order in units]

    def hosted(arrays, units, begin, end, when):
        summer = Summer(arrays, layout_of(units, 0, begin, end))
        return summer, [when[min(i, len(when) - 1)] for i in range(summer.slots)]

    def channel(part, kept, hosts, collective_id):
        low, size = spans[part]
        first, last = part == 0, part == len(spans) - 1
        ins = [
            tile_rows(second), ahead, rows_of(second_row), tile_rows(objective_adjoint), tile_rows(cols), table(vectors),
            (dense_address_transform, "any", None), (dense_content_transform, "any", None),
        ]
        ins += [table(dense_respond_transform)] if first or last else []
        ins += [tile_rows(a) for a in kept]
        ins += [tile_rows(attended)] if last else []
        if last:
            outs = [tile_out(bf16), tile_out(f32), rows_out(one_row), sum_out(width, width), sum_out(2, width)]
        else:
            outs = [tile_out(f32)] * (3 if first else 2)
        return call(
            functools.partial(channel_kernel, low, size, first, last),
            (batches, tiles),
            ins,
            outs + [sum_out(width, size), sum_out(size, width)],
            "channel_%d" % part,
            scratch=[
                pltpu.VMEM((BLOCK, 8), f32), pltpu.VMEM((width, size), bf16), pltpu.VMEM((size, width), bf16),
                pltpu.SemaphoreType.DMA((2,)), pltpu.VMEM((1, width), f32),
            ],
            flops=7 * 2 * batches * length * width * (2 * size + (width if last else 0)),
            hosts=hosts,
            collective_id=collective_id,
            ticks=2,
        )

    steps = batches * tiles
    gate, total, d_inner, *part_a = channel(0, [], [], None)
    total, d_inner, *rest = channel(1, [gate, total, d_inner], [hosted(part_a, even, 0, 3, [3, 6, 8])], 6)
    part_b, part_a = rest[:2], rest[2:]
    block, d_second, d_second_row, grad_filter, channel_vectors, *rest = channel(
        2,
        [gate, total, d_inner],
        [hosted(part_a, even, 3, depth + 1, [2, 5, 8]), hosted(part_b, even, 0, 2, [3, 8])],
        7,
    )
    part_c, part_a, part_b = [rest[0], rest[1], grad_filter], rest[2:4], rest[4:6]
    back_second = moved(d_second_row[:, 0, :], -1)[:, None, :]
    d_attended, d_wkv, d_valve, carry, grad_output, grad_gate_w, attention_vectors, *rest = call(
        attention_back_kernel,
        (batches,),
        [
            rows_of(d_second), rows_of(back_second), rows_of(attended), rows_of(objective_adjoint), rows_of(wkv),
            rows_of(valve), rows_of(recept), rows_of(cols), table(vectors), table(readout_transform),
            rows_of(incoming_hidden), rows_of(before),
        ],
        [rows_out(tokens)] * 3 + [rows_out(states), sum_out(width, width), sum_out(width, width), sum_out(4, width)],
        "attention_back",
        flops=5 * square_flops,
        hosts=[
            hosted(part_a, even, depth + 1, ends - 2, [2, 5]),
            hosted(part_b, even, 2, depth, [2, 4, 8]),
            hosted(part_c, rest_units, 0, 1, [7]),
        ],
        collective_id=3,
        ticks=4,
    )
    part_a, part_b, part_c, pair = rest[:2], rest[2:4], rest[4:7], [grad_output, grad_gate_w]
    steps = batches * pairs
    arriving = Carrier([carry], lengths, vectors, length, -1)
    d_recept, d_keys, d_values, mix_vectors, out_state, *rest = call(
        mix_back_kernel,
        (batches, pairs),
        [
            by_pair(recept), by_pair(keys), by_pair(values), by_pair(d_wkv), pair_state(state), rows_of(cols), rows_of(row),
            pair_vectors,
        ],
        [pair_out] * 3 + [((batches, 2, width), f32, (1, 2, PAIR), lambda b, p: (b, 0, p))],
        "mix_back",
        flops=9 * 2 * batches * length * length * width * 2,
        hosts=[
            (arriving, [(i + 1) * steps // arriving.slots for i in range(arriving.slots)]),
            hosted(part_b, even, depth, ends - 2, [3, 4, 6]),
            hosted(part_c, rest_units, 1, depth - 1, [4, 7, 9]),
            hosted(part_a, even, ends - 2, ends - 1, [9]),
            hosted(pair, two, 0, 1, [6]),
        ],
        collective_id=4,
    )
    part_b, part_c, part_a, pair = rest[:2], rest[2:5], rest[5:7], rest[7:9]
    wide = lambda: pltpu.VMEM((length, width), f32)
    d_x, d_first_row, packed, grad_recept, grad_keys, grad_values, *rest = call(
        project_back_kernel,
        (batches, 4),
        common
        + [
            rows_of(d_attended), rows_of(d_recept), rows_of(d_keys), rows_of(d_values), rows_of(d_valve),
            rows_of(keys), rows_of(values), rows_of(state), rows_of(out_state), rows_of(mix_vectors),
            table(attention_vectors), table(channel_vectors),
        ]
        + [table(w) for w in (respond_transform, address_transform, content_transform, valve_transform)],
        [rows_out(tokens), rows_out(one_row), sum_out(*vectors.shape)] + [sum_out(width, width)] * 3,
        "project_back",
        scratch=[wide(), wide(), wide(), wide()],
        flops=5 * 4 * square_flops,
        hosts=[
            hosted(part_c, rest_units, depth - 1, depth + 1, [3, 6]),
            hosted(pair, two, 1, depth - 1, [3, 5, 7]),
            hosted(part_b, even, ends - 2, ends - 1, [5]),
            hosted(part_a, even, ends - 1, ends, [8]),
        ],
        collective_id=5,
    )
    part_c, pair, part_b, part_a = rest[:3], rest[3:5], rest[5:7], rest[7:9]
    own = [grad_recept, grad_keys, grad_values]
    layout = layout_of(even, 0, ends - 1, ends) + layout_of(rest_units, 0, depth + 1, ends, 2)
    layout += layout_of(two, 0, depth - 1, ends, 5)
    for half in range(2):
        layout += layout_of([(i, half * width // 2, width // 2, i) for i in range(3)], 1 + half, 0, ends, 7)
    layout += [(10, 0, packed.shape[0], 1, 1, 0, 0, ends)]
    last_row = moved(d_first_row[:, 0, :], -1)[:, None, :]
    summed = summed_over_devices(part_b + part_c + pair + own + [packed], layout, 0)
    w_expand, w_shrink, w_filter, w_output, w_gate, w_recept, w_keys, w_values, vectors, grad_tokens = gathered(
        part_a + list(summed), spans, hidden_width, d_x, last_row
    )
    return (
        block, grad_tokens, *[vectors[i] for i in range(6)], w_recept, w_keys, w_values, w_gate,
        vectors[6], vectors[7], vectors[8], vectors[9], w_output, vectors[10], vectors[11], vectors[12], vectors[13],
        w_expand, w_shrink, w_filter,
    )


def solution(mesh):
    rows = P(None, "seq", None)
    return jax.shard_map(
        local,
        mesh=mesh,
        in_specs=(rows,) + (P(),) * 23 + (rows,),
        out_specs=(rows, rows) + (P(),) * 22,
        check_vma=False,
    )
```

```python
import functools

import jax
import jax.numpy as jnp
from jax import lax
from jax.experimental import pallas as pl
from jax.experimental.pallas import tpu as pltpu
from jax.sharding import PartitionSpec as P

LANE_FEATURES = 64
PAIR = 2 * LANE_FEATURES
BLOCK = 256
f32 = jnp.float32
bf16 = jnp.bfloat16
VMEM_LIMIT = 60 * 1024 * 1024
MESH = pl.DeviceIdType.MESH


def nothing():
    pass


def split(x):
    high = x.astype(bf16)
    return high, (x - high.astype(f32)).astype(bf16)


def dot(a, b):
    return lax.dot_general(a, b, (((1,), (0,)), ((), ())), preferred_element_type=f32)


def dot_nt(a, b):
    return lax.dot_general(a, b, (((1,), (1,)), ((), ())), preferred_element_type=f32)


def dot_tn(a, b):
    return lax.dot_general(a, b, (((0,), (0,)), ((), ())), preferred_element_type=f32)


def times_weight(x, w):
    high, low = split(x)
    return dot(high, w) + dot(low, w)


def times_weight_t(x, w):
    high, low = split(x)
    return dot_nt(high, w) + dot_nt(low, w)


def outer_sum(a, b):
    return thrice(*split(a), *split(b))


def thrice(ah, al, bh, bl):
    return dot_tn(jnp.concatenate([ah, al, ah], axis=0), jnp.concatenate([bh, bh, bl], axis=0))


def both(high, low, w):
    out = dot(jnp.concatenate([high, low], axis=0), w)
    return out[: high.shape[0]] + out[high.shape[0] :]


def standard(x, epsilon=1e-05):
    centred = x - jnp.mean(x, axis=-1, keepdims=True)
    scale = lax.rsqrt(jnp.mean(centred * centred, axis=-1, keepdims=True) + epsilon)
    return centred * scale, scale


def standard_back(grad, normal, scale):
    return scale * (
        grad
        - jnp.mean(grad, axis=-1, keepdims=True)
        - normal * jnp.mean(grad * normal, axis=-1, keepdims=True)
    )


def first_lanes(rows):
    return lax.broadcasted_iota(jnp.int32, (rows, PAIR), 1) < LANE_FEATURES


def head_ones(scale):
    row = lax.broadcasted_iota(jnp.int32, (2 * PAIR, PAIR), 0) // LANE_FEATURES % 2
    col = lax.broadcasted_iota(jnp.int32, (2 * PAIR, PAIR), 1) // LANE_FEATURES
    return jnp.where(row == col, scale, 0.0).astype(bf16)


def head_sum(x, ones):
    return dot(jnp.concatenate(split(x), axis=1), ones)


def widen(state):
    first = first_lanes(LANE_FEATURES)
    return jnp.concatenate([jnp.where(first, state, 0.0), jnp.where(first, 0.0, state)], axis=0)


def compact(square):
    first = first_lanes(LANE_FEATURES)
    return jnp.where(first, square[:LANE_FEATURES], square[LANE_FEATURES:])


def times_state(x, square):
    xh, xl = split(x)
    sh, sl = split(square)
    return dot(jnp.concatenate([xh, xl], axis=1), jnp.concatenate([sh, sh], axis=0)) + dot(xh, sl)


def times_state_t(x, square):
    xh, xl = split(x)
    sh, sl = split(square)
    return dot_nt(jnp.concatenate([xh, xl], axis=1), jnp.concatenate([sh, sh], axis=1)) + dot_nt(xh, sl)


def cut(x):
    high = x.astype(bf16).astype(f32)
    low = x - high
    return high, low, pltpu.roll(high, LANE_FEATURES, 1), pltpu.roll(low, LANE_FEATURES, 1)


def high_low(pieces, first, head):
    high, low, high_r, low_r = pieces
    return (jnp.where(first, high, low_r) if head == 0 else jnp.where(first, high_r, low)).astype(bf16)


def doubled(pieces, first, head):
    high, low, high_r, low_r = pieces
    if head == 0:
        both = (jnp.where(first, high, high_r), jnp.where(first, low, low_r))
    else:
        both = (jnp.where(first, high_r, high), jnp.where(first, low_r, low))
    return jnp.concatenate([part.astype(bf16) for part in both], axis=1)


def twice(x):
    return jnp.concatenate([x, x], axis=1)


def folded(parts, first):
    sums = [part + pltpu.roll(part, LANE_FEATURES, 1) for part in parts]
    return jnp.where(first, sums[0], sums[1])


def decays(log_decay):
    step = lax.broadcasted_iota(jnp.int32, (BLOCK, PAIR), 0).astype(f32)
    return step, jnp.exp(log_decay * step), jnp.exp(-log_decay * (step + 1.0)), jnp.exp(log_decay * BLOCK)


def shifted(normal, row_before, keep):
    rows = lax.broadcasted_iota(jnp.int32, normal.shape, 0)
    return jnp.where(rows == 0, row_before, pltpu.roll(normal, 1, 0)) * keep


GAIN, BIAS, MIX_R, MIX_K, MIX_V, MIX_G, DECAY, BOOST, GROUP_GAIN, GROUP_SHIFT, GAIN2, BIAS2, MIX_E, MIX_F = range(14)


def vec(ref, which, lanes=slice(None)):
    return ref[which : which + 1, lanes]


def bounds_of(lengths_ref, batch):
    at, bounds = jnp.int32(0), []
    for j in range(lengths_ref.shape[1]):
        bounds.append(at)
        at = at + lengths_ref[batch, j]
    return bounds


def segment_of(bounds, position):
    return sum([(position >= bound).astype(jnp.int32) for bound in bounds])


def tokens_kernel(lengths_ref, *refs):
    *vector_refs, cols_ref, row_ref, packed_ref = refs
    for i, ref in enumerate(vector_refs):
        value = ref[...].reshape(1, ref.shape[0])
        packed_ref[i : i + 1] = -jnp.exp(value) if i == DECAY else value
    packed_ref[len(vector_refs) :] = jnp.zeros((2, packed_ref.shape[1]), f32)
    batches, length, columns = cols_ref.shape
    offset = lax.axis_index("seq") * length
    for batch in range(batches):
        bounds = bounds_of(lengths_ref, batch)
        place = offset + lax.broadcasted_iota(jnp.int32, (length, columns), 0)
        segment = segment_of(bounds, place)
        starts = functools.reduce(jnp.logical_or, [place == bound for bound in bounds])
        column = lax.broadcasted_iota(jnp.int32, (length, columns), 1)
        fresh = segment == segment_of(bounds, offset - 1)
        last = segment == segment_of(bounds, offset + length - 1)
        flag = jnp.where(column == 1, jnp.where(starts, 0, 1), jnp.where(column == 2, jnp.where(fresh, 1, 0), jnp.where(last, 1, 0)))
        cols_ref[batch] = jnp.where(column == 0, segment, flag).astype(f32)
        row_ref[batch] = segment_of(bounds, offset + lax.broadcasted_iota(jnp.int32, (1, length), 1)).astype(f32)


def project_kernel(mixes, states, x_ref, before_ref, cols_ref, vec_ref, *refs):
    count = len(mixes)
    weights, outs = refs[:count], refs[count : 2 * count]
    gain, bias = vec(vec_ref, GAIN), vec(vec_ref, BIAS)
    normal = standard(x_ref[0].astype(f32))[0] * gain + bias
    before = standard(before_ref[0])[0] * gain + bias
    earlier = shifted(normal, before, cols_ref[0, :, 1:2])
    difference = normal - earlier
    for mix, weight, out in zip(mixes, weights, outs):
        out[0] = times_weight(earlier + vec(vec_ref, mix) * difference, weight[...])
    if states:
        length, width = normal.shape
        keys, values, end_ref = outs[0], outs[1], refs[2 * count]
        rows = lax.broadcasted_iota(jnp.int32, (length, PAIR), 0).astype(f32)
        for pair in range(width // PAIR):
            lanes = slice(pair * PAIR, (pair + 1) * PAIR)
            tail = jnp.exp(vec(vec_ref, DECAY, lanes) * (length - 1.0 - rows)) * cols_ref[0, :, 3:4]
            end_ref[0, pair] = compact(outer_sum(keys[0, :, lanes] * tail, values[0, :, lanes]))


def allowed_here(cols_ref, row_ref, at, of, across):
    t_col = cols_ref[0, pl.ds(at * BLOCK, BLOCK), 0:1]
    s_row = row_ref[0, :, pl.ds(of * BLOCK, BLOCK)]
    mask = t_col == s_row
    if at == of:
        shape = (BLOCK, BLOCK)
        low, high = (1, 0) if not across else (0, 1)
        mask = jnp.logical_and(
            mask,
            lax.broadcasted_iota(jnp.int32, shape, low) < lax.broadcasted_iota(jnp.int32, shape, high),
        )
    return mask


def mix_kernel(recept_ref, keys_ref, values_ref, cols_ref, row_ref, vec_ref, out_ref):
    length = recept_ref.shape[1]
    log_decay, boost = vec(vec_ref, DECAY), vec(vec_ref, BOOST)
    first = first_lanes(BLOCK)
    step, fall, rise, whole = decays(log_decay)
    ones = head_ones(1.0)
    queries, near, far, values = [], [], [], []
    for at in range(length // BLOCK):
        here = pl.ds(at * BLOCK, BLOCK)
        queries.append(cut(recept_ref[0, here] * fall))
        raised = keys_ref[0, here] * rise
        near.append(cut(raised))
        far.append(raised * whole)
        values.append(cut(values_ref[0, here]))
    for at in range(length // BLOCK):
        here = pl.ds(at * BLOCK, BLOCK)
        totals = [jnp.zeros((BLOCK, PAIR), f32)] * 2
        for of in range(at + 1):
            mask = allowed_here(cols_ref, row_ref, at, of, False)
            gap = jnp.exp(log_decay * (BLOCK * (at - of - 1))) if at > of + 1 else None
            keys = near[of] if of == at else cut(far[of] if gap is None else far[of] * gap)
            for head in range(2):
                scores = dot_nt(twice(high_low(queries[at], first, head)), doubled(keys, first, head))
                sh, sl = split(jnp.where(mask, scores, 0.0))
                held = high_low(values[of], first, head)
                totals[head] = totals[head] + both(sh, sl, held)
        present = head_sum(recept_ref[0, here] * boost * keys_ref[0, here], ones)
        out_ref[0, here] = folded(totals, first) + present * values_ref[0, here]


def readout_kernel(
    mixed_ref, recept_ref, state_ref, valve_ref, cols_ref, vec_ref, x_ref, weight_ref,
    wkv_ref, attended_ref, second_ref, last_ref,
):
    length, width = mixed_ref.shape[1:]
    rows = (pl.program_id(1) * length + lax.broadcasted_iota(jnp.int32, (length, PAIR), 0)).astype(f32)
    ones = head_ones(1.0 / LANE_FEATURES)
    fresh = cols_ref[0, :, 2:3]
    gated = []
    for pair in range(width // PAIR):
        lanes = slice(pair * PAIR, (pair + 1) * PAIR)
        query = recept_ref[0, :, lanes] * jnp.exp(vec(vec_ref, DECAY, lanes) * rows) * fresh
        wkv = mixed_ref[0, :, lanes] + times_state(query, widen(state_ref[0, pair]))
        wkv_ref[0, :, lanes] = wkv
        centred = wkv - head_sum(wkv, ones)
        normal = centred * lax.rsqrt(head_sum(centred * centred, ones) + 0.00064)
        grouped = normal * vec(vec_ref, GROUP_GAIN, lanes) + vec(vec_ref, GROUP_SHIFT, lanes)
        gated.append(grouped * jax.nn.silu(valve_ref[0, :, lanes]))
    attended = x_ref[0].astype(f32) + times_weight(jnp.concatenate(gated, axis=1), weight_ref[...])
    attended_ref[0] = attended
    second = standard(attended)[0] * vec(vec_ref, GAIN2) + vec(vec_ref, BIAS2)
    second_ref[0] = second
    last_ref[0] = second[length - 1 :]


def pieces_of(total):
    cuts, at = [], 0
    while at < total:
        size = min(512, total - at)
        cuts.append((at, size))
        at += size
    return cuts


def channel_kernel(low, size, first, last, *refs):
    refs = list(refs)
    take = lambda count: [refs.pop(0) for _ in range(count)]
    second_ref, ahead_ref, received_ref, grad_ref, cols_ref, vec_ref, expand_any, shrink_any = take(8)
    filter_ref = take(1)[0] if first or last else None
    gate_ref = None if first else take(1)[0]
    total_in, inner_in = (None, None) if first else take(2)
    attended_ref = take(1)[0] if last else None
    gate_out = take(1)[0] if first else None
    if last:
        block_ref, d_second_ref, d_row_ref, d_filter_ref, d_vec_ref = take(5)
    else:
        total_out, inner_out = take(2)
    d_expand_ref, d_shrink_ref, hidden_ref, expand_ref, shrink_ref, sems, carry_ref = refs
    tiles = pl.num_programs(1)
    batch, turn = pl.program_id(0), pl.program_id(1)
    tile = tiles - 1 - turn
    start = jnp.logical_and(batch == 0, turn == 0)

    @pl.when(start)
    def _():
        loads = [
            pltpu.make_async_copy(expand_any.at[:, pl.ds(low, size)], expand_ref, sems.at[0]),
            pltpu.make_async_copy(shrink_any.at[pl.ds(low, size)], shrink_ref, sems.at[1]),
        ]
        for load in loads:
            load.start()
        for ref in [d_expand_ref, d_shrink_ref] + ([d_filter_ref, d_vec_ref] if last else []):
            ref[...] = jnp.zeros_like(ref)
        for load in loads:
            load.wait()

    keep = cols_ref[0, :, 1:2]
    second = second_ref[0]
    before = jnp.where(tile == 0, received_ref[0], ahead_ref[0, 7:8])
    earlier = shifted(second, before, keep)
    difference = second - earlier
    mix_e, mix_f = vec(vec_ref, MIX_E), vec(vec_ref, MIX_F)
    inner_h, inner_l = split(earlier + mix_e * difference)
    if first or last:
        side_h, side_l = split(earlier + mix_f * difference)
    if first:
        gate = jax.nn.sigmoid(dot(side_h, filter_ref[...]) + dot(side_l, filter_ref[...]))
        gate_out[0] = gate
    else:
        gate = gate_ref[0]
    grad = grad_ref[0].astype(f32)
    dt_h, dt_l = split(grad * gate)
    total = jnp.zeros(second.shape, f32) if first else total_in[0]
    d_inner = jnp.zeros(second.shape, f32) if first else inner_in[0]
    for at, wide in pieces_of(size):
        lanes = slice(at, at + wide)
        raw = jnp.maximum(dot(inner_h, expand_ref[:, lanes]) + dot(inner_l, expand_ref[:, lanes]), 0.0)
        hid_h, hid_l = split(raw * raw)
        total = total + dot(hid_h, shrink_ref[lanes, :]) + dot(hid_l, shrink_ref[lanes, :])
        d_hidden = dot_nt(dt_h, shrink_ref[lanes, :]) + dot_nt(dt_l, shrink_ref[lanes, :])
        dr_h, dr_l = split(d_hidden * (2.0 * raw))
        d_shrink_ref[lanes, :] += thrice(hid_h, hid_l, dt_h, dt_l)
        d_expand_ref[:, lanes] += thrice(inner_h, inner_l, dr_h, dr_l)
        d_inner = d_inner + dot_nt(dr_h, expand_ref[:, lanes]) + dot_nt(dr_l, expand_ref[:, lanes])
    if not last:
        total_out[0] = total
        inner_out[0] = d_inner
        return
    block_ref[0] = (attended_ref[0] + gate * total).astype(bf16)
    ds_h, ds_l = split(grad * total * (gate * (1.0 - gate)))
    d_filter_ref[...] += thrice(side_h, side_l, ds_h, ds_l)
    d_side = dot_nt(ds_h, filter_ref[...]) + dot_nt(ds_l, filter_ref[...])
    d_vec_ref[0:1] += jnp.sum(d_inner * difference, axis=0, keepdims=True)
    d_vec_ref[1:2] += jnp.sum(d_side * difference, axis=0, keepdims=True)
    direct = mix_e * d_inner + mix_f * d_side
    passed = (d_inner + d_side - direct) * keep
    rows = lax.broadcasted_iota(jnp.int32, second.shape, 0)
    above = pltpu.roll(passed, second.shape[0] - 1, 0)
    outside = jnp.where(turn == 0, 0.0, carry_ref[...])
    d_second_ref[0] = direct + jnp.where(rows == second.shape[0] - 1, outside, above)
    carry_ref[...] = passed[0:1]
    d_row_ref[0] = passed[0:1]


def attention_back_kernel(
    d_second_ref, back_ref, attended_ref, grad_ref, wkv_ref, valve_ref, recept_ref, cols_ref, vec_ref, weight_ref,
    d_attended_ref, d_wkv_ref, d_valve_ref, gated_ref, carry_ref, d_vec_ref,
):
    length, width = attended_ref.shape[1:]

    tile, is_last = pl.program_id(1), pl.program_id(1) == pl.num_programs(1) - 1

    @pl.when(jnp.logical_and(pl.program_id(0) == 0, tile == 0))
    def _():
        d_vec_ref[...] = jnp.zeros_like(d_vec_ref)

    rows = lax.broadcasted_iota(jnp.int32, (length, width), 0)
    d_second = d_second_ref[0] + jnp.where(jnp.logical_and(rows == length - 1, is_last), back_ref[0], 0.0)
    normal2, scale2 = standard(attended_ref[0])
    d_vec_ref[2:3] += jnp.sum(d_second * normal2, axis=0, keepdims=True)
    d_vec_ref[3:4] += jnp.sum(d_second, axis=0, keepdims=True)
    d_attended = grad_ref[0].astype(f32) + standard_back(d_second * vec(vec_ref, GAIN2), normal2, scale2)
    d_attended_ref[0] = d_attended
    d_gated = times_weight_t(d_attended, weight_ref[...])
    steps = (tile * length + lax.broadcasted_iota(jnp.int32, (length, PAIR), 0)).astype(f32)
    ones = head_ones(1.0 / LANE_FEATURES)
    fresh = cols_ref[0, :, 2:3]
    for pair in range(width // PAIR):
        lanes = slice(pair * PAIR, (pair + 1) * PAIR)
        wkv = wkv_ref[0, :, lanes]
        centred = wkv - head_sum(wkv, ones)
        scale = lax.rsqrt(head_sum(centred * centred, ones) + 0.00064)
        normal = centred * scale
        grouped = normal * vec(vec_ref, GROUP_GAIN, lanes) + vec(vec_ref, GROUP_SHIFT, lanes)
        valve = valve_ref[0, :, lanes]
        sigmoid = jax.nn.sigmoid(valve)
        gate = valve * sigmoid
        gated_ref[0, :, lanes] = grouped * gate
        d_here = d_gated[:, lanes]
        d_valve_ref[0, :, lanes] = d_here * grouped * (sigmoid * (1.0 + valve * (1.0 - sigmoid)))
        d_grouped = d_here * gate
        d_vec_ref[0:1, lanes] += jnp.sum(d_grouped * normal, axis=0, keepdims=True)
        d_vec_ref[1:2, lanes] += jnp.sum(d_grouped, axis=0, keepdims=True)
        d_normal = d_grouped * vec(vec_ref, GROUP_GAIN, lanes)
        d_wkv = scale * (d_normal - head_sum(d_normal, ones) - normal * head_sum(d_normal * normal, ones))
        d_wkv_ref[0, :, lanes] = d_wkv
        query = recept_ref[0, :, lanes] * jnp.exp(vec(vec_ref, DECAY, lanes) * steps) * fresh
        carried = compact(outer_sum(query, d_wkv))
        carry_ref[0, pair] = jnp.where(tile == 0, carried, carry_ref[0, pair] + carried)


def mix_back_kernel(
    recept_ref, keys_ref, values_ref, grad_ref, state_ref, cols_ref, row_ref, vec_ref,
    gated_ref, d_attended_ref, d_recept_ref, d_keys_ref, d_values_ref, d_vec_ref, d_weight_ref,
):
    length = recept_ref.shape[1]
    blocks = length // BLOCK
    first = first_lanes(BLOCK)
    log_decay, boost = vec(vec_ref, DECAY), vec(vec_ref, BOOST)
    step, fall, rise, whole = decays(log_decay)
    ones = head_ones(1.0)
    square = widen(state_ref[0, 0])
    queries, near, far, values, grads = [], [], [], [], []
    for at in range(blocks):
        here = pl.ds(at * BLOCK, BLOCK)
        queries.append(cut(recept_ref[0, here] * fall))
        raised = keys_ref[0, here] * rise
        near.append(cut(raised))
        far.append(raised * whole)
        values.append(cut(values_ref[0, here]))
        grads.append(cut(grad_ref[0, here]))
    zero = jnp.zeros((BLOCK, PAIR), f32)
    d_query = [[zero, zero] for _ in range(blocks)]
    d_value = [[zero, zero] for _ in range(blocks)]
    d_near = [[zero, zero] for _ in range(blocks)]
    d_far = [[zero, zero] for _ in range(blocks)]
    for at in range(blocks):
        for of in range(at + 1):
            mask = allowed_here(cols_ref, row_ref, at, of, False)
            t_row = row_ref[0, :, pl.ds(at * BLOCK, BLOCK)]
            s_col = cols_ref[0, pl.ds(of * BLOCK, BLOCK), 0:1]
            mask_t = s_col == t_row
            if at == of:
                shape = (BLOCK, BLOCK)
                mask_t = jnp.logical_and(
                    mask_t, lax.broadcasted_iota(jnp.int32, shape, 0) < lax.broadcasted_iota(jnp.int32, shape, 1)
                )
            gap = jnp.exp(log_decay * (BLOCK * (at - of - 1))) if at > of + 1 else None
            keys = near[of] if of == at else cut(far[of] if gap is None else far[of] * gap)
            mask, mask_t = jnp.where(mask, 1.0, 0.0), jnp.where(mask_t, 1.0, 0.0)
            for head in range(2):
                q_hl = high_low(queries[at], first, head)
                g_hl = high_low(grads[at], first, head)
                k_hl = high_low(keys, first, head)
                v_hl = high_low(values[of], first, head)
                scores_t = dot_nt(twice(k_hl), doubled(queries[at], first, head))
                s_h, s_l = split(scores_t * mask_t)
                d_value[of][head] = d_value[of][head] + both(s_h, s_l, g_hl)
                d_scores = dot_nt(twice(g_hl), doubled(values[of], first, head))
                s_h, s_l = split(d_scores * mask)
                d_query[at][head] = d_query[at][head] + both(s_h, s_l, k_hl)
                d_scores_t = dot_nt(twice(v_hl), doubled(grads[at], first, head))
                s_h, s_l = split(d_scores_t * mask_t)
                d_key = both(s_h, s_l, q_hl)
                if of == at:
                    d_near[of][head] = d_key
                else:
                    if gap is not None:
                        d_key = d_key * gap
                    d_far[of][head] = d_far[of][head] + d_key
    d_decay = jnp.zeros((1, PAIR), f32)
    d_boost = jnp.zeros((1, PAIR), f32)
    for at in range(blocks):
        here = pl.ds(at * BLOCK, BLOCK)
        recept, keys, value, grad = recept_ref[0, here], keys_ref[0, here], values_ref[0, here], grad_ref[0, here]
        fresh = cols_ref[0, here, 2:3]
        d_in = folded(d_query[at], first) * fall
        d_state = times_state_t(grad, square) * (fall * jnp.exp(log_decay * (BLOCK * at)) * fresh)
        d_here = folded(d_near[at], first) * rise
        d_later = folded(d_far[at], first) * (rise * whole)
        present = head_sum(recept * boost * keys, ones)
        d_present = head_sum(grad * value, ones)
        d_recept_ref[0, here] = d_in + d_state + boost * keys * d_present
        d_keys_ref[0, here] = d_here + d_later + boost * recept * d_present
        d_values_ref[0, here] = folded(d_value[at], first) + present * grad
        d_boost = d_boost + jnp.sum(recept * keys * d_present, axis=0, keepdims=True)
        d_decay = d_decay + jnp.sum(
            recept * (step * d_in + (step + float(BLOCK * at)) * d_state)
            + keys * ((BLOCK - 1.0 - step) * d_later - (step + 1.0) * d_here),
            axis=0,
            keepdims=True,
        )
    d_vec_ref[0, 0:1] = d_decay
    d_vec_ref[0, 1:2] = d_boost
    here = rows8(pl.program_id(1) * PAIR, PAIR)
    d_weight = outer_sum(gated_ref[0], d_attended_ref[0])
    first_batch = pl.program_id(0) == 0

    @pl.when(first_batch)
    def _():
        d_weight_ref[here] = d_weight

    @pl.when(jnp.logical_not(first_batch))
    def _():
        d_weight_ref[here] += d_weight


def weights_back_kernel(
    x_ref, before_ref, cols_ref, vec_ref,
    d_recept_ref, d_keys_ref, d_values_ref, d_valve_ref, keys_ref, values_ref, state_ref, out_state_ref,
    dw_r, dw_k, dw_v, dw_g, d_keys_out, d_values_out, d_decay_ref, earlier_ref, difference_ref,
):
    length, width = x_ref.shape[1:]
    turn = pl.program_id(1)
    steps = lax.broadcasted_iota(jnp.int32, (length, PAIR), 0).astype(f32)
    pairs = [(pair, slice(pair * PAIR, (pair + 1) * PAIR)) for pair in range(width // PAIR)]

    @pl.when(jnp.logical_and(pl.program_id(0) == 0, turn == 0))
    def _():
        for ref in (dw_r, dw_k, dw_v, dw_g, d_decay_ref):
            ref[...] = jnp.zeros_like(ref)

    def tail_of(lanes):
        return jnp.exp(vec(vec_ref, DECAY, lanes) * (length - 1.0 - steps)) * cols_ref[0, :, 3:4]

    def weigh(which, grad, d_weight):
        d_weight[...] += outer_sum(earlier_ref[...] + vec(vec_ref, which) * difference_ref[...], grad)

    @pl.when(turn == 0)
    def _():
        gain, bias = vec(vec_ref, GAIN), vec(vec_ref, BIAS)
        normal = standard(x_ref[0].astype(f32))[0] * gain + bias
        before = standard(before_ref[0])[0] * gain + bias
        earlier = shifted(normal, before, cols_ref[0, :, 1:2])
        earlier_ref[...] = earlier
        difference_ref[...] = normal - earlier
        weigh(MIX_G, d_valve_ref[0], dw_g)

    @pl.when(turn == 1)
    def _():
        weigh(MIX_R, d_recept_ref[0], dw_r)

    @pl.when(turn == 2)
    def _():
        for pair, lanes in pairs:
            d_keys = times_state_t(values_ref[0, :, lanes], widen(out_state_ref[0, pair])) * tail_of(lanes)
            later = (length - 1.0 - steps) * keys_ref[0, :, lanes] * d_keys
            square = widen(state_ref[0, pair]) * widen(out_state_ref[0, pair])
            ones = jnp.ones((8, PAIR), bf16)
            kept = sum([dot_nt(ones, part)[0:1] for part in split(square)])
            kept = kept * jnp.exp(vec(vec_ref, DECAY, lanes) * length) * (float(length) * cols_ref[0, length - 1 :, 2:3])
            d_decay_ref[:, lanes] += jnp.sum(later, axis=0, keepdims=True) + kept
            d_keys_out[0, :, lanes] = d_keys_ref[0, :, lanes] + d_keys
        weigh(MIX_K, d_keys_out[0], dw_k)

    @pl.when(turn == 3)
    def _():
        for pair, lanes in pairs:
            ended = times_state(keys_ref[0, :, lanes] * tail_of(lanes), widen(out_state_ref[0, pair]))
            d_values_out[0, :, lanes] = d_values_ref[0, :, lanes] + ended
        weigh(MIX_V, d_values_out[0], dw_v)


def inputs_back_kernel(
    x_ref, before_ref, cols_ref, vec_ref, d_attended_ref, d_recept_ref, d_keys_ref, d_values_ref, d_valve_ref,
    mix_vec_ref, attention_vec_ref, channel_vec_ref, d_decay_ref, w_r, w_k, w_v, w_g,
    d_x_ref, d_row_ref, packed_ref, difference_ref, direct_ref, passed_ref,
):
    length, width = x_ref.shape[1:]
    batch, turn = pl.program_id(0), pl.program_id(1)
    gain, bias = vec(vec_ref, GAIN), vec(vec_ref, BIAS)

    @pl.when(jnp.logical_and(batch == 0, turn == 0))
    def _():
        packed_ref[...] = jnp.zeros_like(packed_ref)
        packed_ref[GROUP_GAIN : BIAS2 + 1] = attention_vec_ref[...]
        packed_ref[MIX_E : MIX_F + 1] = channel_vec_ref[...]
        packed_ref[DECAY : DECAY + 1] = d_decay_ref[...]

    def through(grad, which, weight, first=False):
        mix = vec(vec_ref, which)
        d_mixed = times_weight_t(grad, weight[...])
        packed_ref[which : which + 1] += jnp.sum(d_mixed * difference_ref[...], axis=0, keepdims=True)
        direct, passed = mix * d_mixed, d_mixed - mix * d_mixed
        direct_ref[...] = direct if first else direct_ref[...] + direct
        passed_ref[...] = passed if first else passed_ref[...] + passed

    @pl.when(turn == 0)
    def _():
        normal = standard(x_ref[0].astype(f32))[0] * gain + bias
        before = standard(before_ref[0])[0] * gain + bias
        difference_ref[...] = normal - shifted(normal, before, cols_ref[0, :, 1:2])
        packed_ref[DECAY : BOOST + 1] += mix_vec_ref[0]
        through(d_recept_ref[0], MIX_R, w_r, True)

    @pl.when(turn == 1)
    def _():
        through(d_valve_ref[0], MIX_G, w_g)

    @pl.when(turn == 2)
    def _():
        through(d_keys_ref[0], MIX_K, w_k)

    @pl.when(turn == 3)
    def _():
        through(d_values_ref[0], MIX_V, w_v)
        passed = passed_ref[...] * cols_ref[0, :, 1:2]
        rows = lax.broadcasted_iota(jnp.int32, (length, width), 0)
        d_normal = direct_ref[...] + jnp.where(rows == length - 1, 0.0, pltpu.roll(passed, length - 1, 0))
        hat, scale = standard(x_ref[0].astype(f32))
        hat_before, scale_before = standard(before_ref[0])
        out = passed[0:1]
        packed_ref[GAIN : GAIN + 1] += jnp.sum(d_normal * hat, axis=0, keepdims=True) + out * hat_before
        packed_ref[BIAS : BIAS + 1] += jnp.sum(d_normal, axis=0, keepdims=True) + out
        d_x_ref[0] = d_attended_ref[0] + standard_back(d_normal * gain, hat, scale)
        d_row_ref[pl.ds(batch, 1)] = standard_back(out * gain, hat_before, scale_before)[None]

        @pl.when(batch == pl.num_programs(0) - 1)
        def _():
            packed_ref[DECAY : DECAY + 1] = packed_ref[DECAY : DECAY + 1] * vec(vec_ref, DECAY)


def call(kernel, grid, ins, outs, name, scratch=(), flops=0, hosts=(), collective_id=None, ticks=1):
    bytes_accessed = sum(a.size * a.dtype.itemsize for a, _, _ in ins)
    for shape, dtype, _, _ in outs:
        size = jnp.dtype(dtype).itemsize
        for extent in shape:
            size *= extent
        bytes_accessed += size

    def spec(block, index):
        if block == "smem":
            return pl.BlockSpec(memory_space=pltpu.SMEM)
        if block == "any":
            return pl.BlockSpec(memory_space=pl.ANY)
        if index is None:
            return pl.BlockSpec(block, lambda *_: (0,) * len(block), pipeline_mode=pl.Buffered(1))
        return pl.BlockSpec(block, index)

    ins, outs, scratch = list(ins), list(outs), list(scratch)
    own, places, aliases = (len(ins), len(outs), len(scratch)), [], {}
    for exchange, _ in hosts:
        more_in, more_out, alias = exchange.operands()
        aliases.update({len(ins) + i: len(outs) + j for i, j in alias})
        place = [len(ins), len(outs), len(scratch)]
        ins, outs, scratch = ins + more_in, outs + more_out, scratch + exchange.scratch()
        places.append([slice(a, b) for a, b in zip(place, (len(ins), len(outs), len(scratch)))])
    steps = 1
    for extent in grid:
        steps *= extent

    def body(*refs):
        in_refs, out_refs, scratch_refs = refs[: len(ins)], refs[len(ins) : len(ins) + len(outs)], refs[len(ins) + len(outs) :]
        step = pl.program_id(0)
        for axis in range(1, len(grid)):
            step = step * grid[axis] + pl.program_id(axis)
        for (exchange, _), (i, o, t) in zip(hosts, places):
            exchange.kernel_outs = out_refs[: own[1]]
            exchange.bind(in_refs[i], out_refs[o], scratch_refs[t])

        def enter():
            barrier = pltpu.get_barrier_semaphore()
            partners = [partner for exchange, _ in hosts for partner in exchange.partners()]
            for partner in partners:
                pl.semaphore_signal(barrier, inc=1, device_id=(partner,), device_id_type=MESH)
            pl.semaphore_wait(barrier, len(partners))
            for exchange, _ in hosts:
                exchange.start()

        def advance(turn):
            due = []
            for exchange, ends in hosts:
                slots = [slot for slot in range(exchange.slots) if min(ends[slot], steps * ticks) == turn]
                due += [((slot + 1) / exchange.slots, exchange, slot) for slot in slots]
            due.sort(key=lambda entry: entry[0])
            if due:

                @pl.when(step == min(turn // ticks, steps - 1))
                def _():
                    for _, exchange, slot in due:
                        exchange.run(slot)

        if hosts:
            pl.when(step == 0)(enter)
        for turn in range(steps):
            advance(turn * ticks)
        passed = []

        def tick():
            passed.append(0)
            if len(passed) < ticks:
                for turn in range(steps):
                    advance(turn * ticks + len(passed))

        more = {"tick": tick} if ticks > 1 else {}
        kernel(*in_refs[: own[0]], *out_refs[: own[1]], *scratch_refs[: own[2]], **more)
        advance(steps * ticks)
        if hosts:

            @pl.when(step == steps - 1)
            def _():
                for exchange, _ in hosts:
                    exchange.close()

    params = {"collective_id": collective_id, "has_side_effects": True} if hosts else {}
    return pl.pallas_call(
        body,
        grid=grid,
        in_specs=[spec(block, index) for _, block, index in ins],
        out_specs=[spec(block, index) for _, _, block, index in outs],
        out_shape=[jax.ShapeDtypeStruct(shape, dtype) for shape, dtype, _, _ in outs],
        input_output_aliases=aliases,
        scratch_shapes=scratch,
        compiler_params=pltpu.CompilerParams(
            dimension_semantics=("arbitrary",) * len(grid), vmem_limit_bytes=VMEM_LIMIT, **params
        ),
        cost_estimate=pl.CostEstimate(flops=flops, bytes_accessed=bytes_accessed, transcendentals=0),
        name=name,
    )(*[a for a, _, _ in ins])


def moved(value, steps):
    count = lax.axis_size("seq")
    low, high = max(0, -steps), min(count, count - steps)
    return lax.ppermute(value, "seq", [(source, source + steps) for source in range(low, high)])


def reach(count):
    window, needed, hops = 2, {32: 16, 128: 32}.get(count, count) // 2, []
    while window < needed:
        hops.append(window)
        window *= 2
    return hops


class Carrier:
    def __init__(self, parts, lengths, vectors, length, sign, begin=0, end=None):
        self.count = lax.axis_size("seq")
        self.parts, self.lengths, self.vectors, self.length, self.sign = parts, lengths, vectors, length, sign
        self.hops = [[1, 2]] + [[hop] for hop in reach(self.count)]
        self.whole = len(self.hops) + 2
        self.begin, self.end = begin, self.whole if end is None else end
        self.slots = self.end - self.begin
        batches, pairs = parts[0].shape[:2]
        self.half = pairs // 2 if begin == 0 else pairs
        self.shape = (batches, self.half) + parts[0].shape[2:]

    def operands(self):
        shape = self.shape
        full = (shape[0], 2 * self.half) + shape[2:]
        outs = [(full, f32, full, None)] if self.end == self.whole else [(shape, f32, shape, None)] * 2
        ins = [(part, part.shape, None) for part in self.parts]
        return ins + [(self.vectors, self.vectors.shape, None), (self.lengths, "smem", None)], outs, []

    def scratch(self):
        return [
            pltpu.VMEM((self.slots, 2) + self.shape, f32),
            pltpu.VMEM((self.slots + 1,) + self.shape, f32),
            pltpu.VMEM((2,) + self.shape, f32),
            pltpu.SemaphoreType.DMA((self.slots, 2)),
            pltpu.SemaphoreType.DMA((self.slots, 2)),
        ]

    def bind(self, ins, outs, scratch):
        *self.part_refs, self.vec_ref, self.lengths_ref = ins
        self.out_refs = outs
        self.landed, self.totals, self.kept, self.send_sems, self.recv_sems = scratch
        self.mine = lax.axis_index("seq")
        self.core, self.chip = self.mine % 2, self.mine // 2
        self.sibling = self.mine + 1 - 2 * self.core

    def chip_at(self, hop):
        chips = self.count // 2
        return (self.chip + hop + chips) % chips * 2 + self.core

    def partners(self):
        out = []
        for slot in range(self.begin, self.end):
            if slot in (0, self.whole - 1):
                out.append(self.sibling)
            else:
                out += [self.chip_at(sign * hop) for hop in self.hops[slot - 1] for sign in (1, -1)]
        return out

    def first_part(self):
        return self.kept.at[0] if self.begin == 0 else self.part_refs[1]

    def total(self, slot):
        return self.part_refs[0] if slot == self.begin and slot > 0 else self.totals.at[slot - self.begin]

    def copies(self, slot):
        at = slot - self.begin
        if slot == 0:
            away = self.part_refs[0].at[:, pl.ds((1 - self.core) * self.half, self.half)]
            moves = [(away, self.landed.at[at, 0], self.sibling)]
        elif slot == self.whole - 1:
            moves = [(self.kept.at[1], self.landed.at[at, 0], self.sibling)]
        else:
            moves = [
                (self.total(slot), self.landed.at[at, i], self.chip_at(self.sign * hop))
                for i, hop in enumerate(self.hops[slot - 1])
            ]
        return [
            pltpu.make_async_remote_copy(
                src_ref=source, dst_ref=target, send_sem=self.send_sems.at[at, i], recv_sem=self.recv_sems.at[at, i],
                device_id=(device,), device_id_type=MESH,
            )
            for i, (source, target, device) in enumerate(moves)
        ]

    def start(self):
        self.open(self.begin)

    def open(self, slot):
        if slot == self.whole - 1:
            self.finish()
        for copy in self.copies(slot):
            copy.start()

    def fade(self, pair, devices):
        lane = lax.broadcasted_iota(jnp.int32, (LANE_FEATURES, PAIR), 1)
        row = lax.broadcasted_iota(jnp.int32, (LANE_FEATURES, PAIR), 0)
        at = pl.multiple_of((self.core * self.half + pair) * PAIR, PAIR)
        decay = self.vec_ref[DECAY : DECAY + 1, pl.ds(at, PAIR)] * float(self.length * devices)
        heads = [
            jnp.sum(jnp.where(lane == row + head * LANE_FEATURES, decay, 0.0), axis=1, keepdims=True) for head in range(2)
        ]
        return jnp.exp(jnp.where(first_lanes(LANE_FEATURES), heads[0], heads[1]))

    def same(self, batch, bound, other):
        bounds = bounds_of(self.lengths_ref, batch)
        ends = [segment_of(bounds, (device + 1) * self.length - 1) for device in (bound, other)]
        return jnp.where(ends[0] == ends[1], 1.0, 0.0).astype(f32)

    def edges(self):
        middle = 2 * self.chip
        return middle - self.sign, middle, middle + self.sign

    def run(self, slot):
        slot = slot + self.begin
        at = slot - self.begin
        for copy in self.copies(slot):
            copy.wait()
        batches = self.shape[0]
        entry, middle, leaving = self.edges()
        if slot == 0:
            flags = [self.same(batch, middle, leaving) for batch in range(batches)]
            is_first = self.core == (0 if self.sign > 0 else 1)
            for pair in range(self.half):
                fade = self.fade(pair, 1)
                for batch in range(batches):
                    own = self.part_refs[0][batch, self.core * self.half + pair]
                    other = self.landed[at, 0, batch, pair]
                    ahead, behind = jnp.where(is_first, own, other), jnp.where(is_first, other, own)
                    self.kept[0, batch, pair] = ahead
                    self.totals[at + 1, batch, pair] = ahead * fade * flags[batch] + behind
        elif slot < self.whole - 1:
            hops = self.hops[slot - 1]
            chips = self.count // 2
            flags = []
            for hop in hops:
                there = self.chip - self.sign * hop
                exists = jnp.where(jnp.logical_and(there >= 0, there < chips), 1.0, 0.0).astype(f32)
                crossed = hop - 1 if slot == 1 else hop
                flags.append([exists * self.same(batch, entry - 2 * self.sign * crossed, entry) for batch in range(batches)])
            for pair in range(self.half):
                fade = self.fade(pair, 2 if slot == 1 else 2 * hops[0])
                for batch in range(batches):
                    if slot == 1:
                        near, far = self.landed[at, 0, batch, pair], self.landed[at, 1, batch, pair]
                        here = near * flags[0][batch] + far * fade * flags[1][batch]
                    else:
                        here = self.total(slot)[batch, pair] + self.landed[at, 0, batch, pair] * fade * flags[0][batch]
                    self.totals[at + 1, batch, pair] = here
        else:
            for pair in range(self.half):
                for batch in range(batches):
                    self.out_refs[0][batch, (1 - self.core) * self.half + pair] = self.landed[at, 0, batch, pair]
        if slot + 1 < self.end:
            self.open(slot + 1)
        elif self.end < self.whole:
            self.out_refs[0][...] = self.totals[at + 1]
            self.out_refs[1][...] = self.first_part()[...]

    def close(self):
        pass

    def finish(self):
        entry, middle, _ = self.edges()
        total, first_part = self.total(self.whole - 1), self.first_part()
        is_first = self.core == (0 if self.sign > 0 else 1)
        flags = [self.same(batch, entry, middle) for batch in range(self.shape[0])]
        for pair in range(self.half):
            fade = self.fade(pair, 1)
            for batch in range(self.shape[0]):
                first = total[batch, pair]
                second = first * fade * flags[batch] + first_part[batch, pair]
                self.out_refs[0][batch, self.core * self.half + pair] = jnp.where(is_first, first, second)
                self.kept[1, batch, pair] = jnp.where(is_first, second, first)


def bit_orders(count):
    bits = count.bit_length() - 1
    if bits == 5:
        return [(0, 1, 2, 3, 4), (0, 2, 3, 1, 4), (0, 3, 1, 2, 4)]
    chip = list(range(1, bits))
    third = max(1, len(chip) // 3)
    return [tuple([0] + chip[k * third :] + chip[: k * third]) for k in range(3)]


class Unit:
    def __init__(self, array, first, rows, width, order, group, begin, end):
        self.array, self.first, self.rows, self.width, self.group = array, first, rows, width, group
        self.steps, size, landing = [], rows, 0
        bits = self.bits = len(order)
        for k, bit in enumerate(order):
            halved = size % 16 == 0
            sent = size // 2 if halved else size
            self.steps.append((bit, halved, sent, landing))
            if begin <= k < end:
                landing += sent
            size = sent
        phases = [p for p in range(2 * bits) if p < bits or self.steps[2 * bits - 1 - p][1]]
        self.phases = [p for p in phases if begin <= p < end]
        self.sums = [p for p in self.phases if p < bits]
        self.landing = landing
        self.held = self.steps[self.sums[0]][2] if self.sums else 0
        self.stages = len(self.phases)


class VectorSum:
    def __init__(self, which, row, shape, row_shape):
        self.count = lax.axis_size("seq")
        self.which, self.row, self.shape, self.row_shape = which, row, shape, row_shape
        self.bits = self.count.bit_length() - 1
        self.slots = self.bits + 1

    def operands(self):
        return [], [(self.shape, f32, self.shape, None), (self.row_shape, f32, self.row_shape, None)], []

    def scratch(self):
        return [
            pltpu.VMEM((self.bits + 1,) + self.shape, f32), pltpu.VMEM((self.bits,) + self.shape, f32),
            pltpu.VMEM((2,) + self.row_shape, f32),
            pltpu.SemaphoreType.DMA((self.bits + 1,)), pltpu.SemaphoreType.DMA((self.bits + 1,)),
        ]

    def bind(self, ins, outs, scratch):
        self.out_ref, self.row_ref = outs
        self.sums, self.landed, self.rows, self.send_sems, self.recv_sems = scratch
        mine = lax.axis_index("seq")
        self.partner = [mine + (1 - 2 * (mine // (1 << k) % 2)) * (1 << k) for k in range(self.bits)]
        self.ahead, self.behind = (mine + self.count - 1) % self.count, (mine + 1) % self.count

    def partners(self):
        return self.partner + [self.ahead, self.behind]

    def start(self):
        pass

    def close(self):
        pass

    def copy(self, k):
        if k == self.bits:
            source, target, device = self.rows.at[0], self.rows.at[1], self.ahead
        else:
            source, target, device = self.sums.at[k], self.landed.at[k], self.partner[k]
        return pltpu.make_async_remote_copy(
            src_ref=source, dst_ref=target, send_sem=self.send_sems.at[k], recv_sem=self.recv_sems.at[k],
            device_id=(device,), device_id_type=MESH,
        )

    def run(self, slot):
        if slot == 0:
            self.sums[0] = self.kernel_outs[self.which][...]
            self.rows[0] = self.kernel_outs[self.row][...]
            self.copy(self.bits).start()
        else:
            self.copy(slot - 1).wait()
            self.sums[slot] = self.sums[slot - 1] + self.landed[slot - 1]
        if slot < self.bits:
            self.copy(slot).start()
        else:
            self.out_ref[...] = self.sums[slot]
            self.copy(self.bits).wait()
            self.row_ref[...] = self.rows[1]


def add_rows(target, at, source, source_at, rows):
    block = next(b for b in (64, 56, 48, 32, 24, 16, 8) if rows % b == 0)

    def step(i, _):
        here = pl.ds(pl.multiple_of(at + i * block, 8), block)
        target[here] = target[here] + source[pl.ds(pl.multiple_of(source_at + i * block, 8), block)]
        return 0

    lax.fori_loop(0, rows // block, step, 0)


def rows8(at, size):
    return pl.ds(pl.multiple_of(at, 8), size)


class Summer:
    def __init__(self, arrays, layout):
        self.count, self.arrays, self.units = lax.axis_size("seq"), arrays, []
        orders = bit_orders(self.count)
        for array, first, rows, parts, group, turn, begin, end in layout:
            size = rows // parts
            for part in range(parts):
                order, width = orders[(turn + part) % 3], arrays[array].shape[1]
                unit = Unit(array, first + part * size, size, width, order, group, begin, end)
                self.units += [unit] if unit.phases else []
        self.groups = sorted({unit.group for unit in self.units})
        self.stages = max(unit.stages for unit in self.units)
        self.slots = self.stages + len(self.groups) - 1

    def operands(self):
        arrays = self.arrays
        return (
            [(a, "any", None) for a in arrays],
            [(a.shape, a.dtype, "any", None) for a in arrays],
            [(i, i) for i in range(len(arrays))],
        )

    def scratch(self):
        return (
            [pltpu.VMEM((max(8, unit.held), unit.width), f32) for unit in self.units]
            + [pltpu.VMEM((max(8, unit.landing), unit.width), f32) for unit in self.units]
            + [
                pltpu.SemaphoreType.DMA((len(self.units), self.stages)),
                pltpu.SemaphoreType.DMA((len(self.units), self.stages)),
                pltpu.SemaphoreType.DMA((len(self.units), 2)),
                pltpu.SemaphoreType.REGULAR((len(self.units),)),
            ]
        )

    def bind(self, ins, outs, scratch):
        size = len(self.units)
        self.refs, self.held, self.landed = outs, scratch[:size], scratch[size : 2 * size]
        self.send_sems, self.recv_sems, self.local_sems, self.free_sems = scratch[2 * size :]
        mine = lax.axis_index("seq")
        bits = self.count.bit_length() - 1
        self.bit = [mine // (1 << k) % 2 for k in range(bits)]
        self.partner = [mine + (1 - 2 * self.bit[k]) * (1 << k) for k in range(bits)]
        self.offsets = []
        for unit in self.units:
            at, seen = 0, [0]
            for which, halved, sent, _ in unit.steps:
                at = at + self.bit[which] * sent if halved else at
                seen.append(at)
            self.offsets.append(seen)

    def partners(self):
        used = sorted({unit.steps[min(p, 2 * unit.bits - 1 - p)][0] for unit in self.units for p in unit.phases})
        return [self.partner[k] for k in used]

    def start(self):
        for group in self.groups:
            for u, unit in enumerate(self.units):
                if unit.group == group:
                    self.begin(u, 0)

    def own(self, u, step):
        unit = self.units[u]
        return self.refs[unit.array].at[rows8(unit.first + self.offsets[u][step + 1], unit.steps[step][2])]

    def copies(self, u, stage):
        unit, seen, here = self.units[u], self.offsets[u], self.refs[self.units[u].array]
        phase, out = unit.phases[stage], []
        if phase < unit.bits:
            which, halved, sent, landing = unit.steps[phase]
            away = seen[phase] + (1 - self.bit[which]) * sent if halved else seen[phase]
            target = self.landed[u].at[pl.ds(landing, sent)]
            if stage == 0:
                source = here.at[rows8(unit.first + away, sent)]
                out.append(pltpu.make_async_copy(self.own(u, phase), self.held[u], self.local_sems.at[u, 0]))
            else:
                source = self.held[u].at[rows8(away - seen[unit.sums[0] + 1], sent)]
        else:
            step = 2 * unit.bits - 1 - phase
            which, _, sent, _ = unit.steps[step]
            source = target = self.own(u, step)
            if unit.sums and stage == len(unit.sums):
                source = self.held[u].at[rows8(seen[step + 1] - seen[unit.sums[0] + 1], sent)]
        return out + [
            pltpu.make_async_remote_copy(
                src_ref=source, dst_ref=target, send_sem=self.send_sems.at[u, stage],
                recv_sem=self.recv_sems.at[u, stage], device_id=(self.partner[which],), device_id_type=MESH,
            )
        ]

    def store(self, u):
        unit, seen = self.units[u], self.offsets[u]
        step = unit.sums[-1]
        source = self.held[u].at[rows8(seen[step + 1] - seen[unit.sums[0] + 1], unit.steps[step][2])]
        return pltpu.make_async_copy(source, self.own(u, step), self.local_sems.at[u, 1])

    def returns(self, u):
        unit = self.units[u]
        back = 2 * unit.bits - 1 - unit.phases[0]
        return unit.phases.index(back) if unit.sums and back in unit.phases else None

    def begin(self, u, stage):
        if stage == self.returns(u):
            pl.semaphore_wait(self.free_sems.at[u], 1)
        for copy in self.copies(u, stage):
            copy.start()

    def end(self, u, stage):
        unit, seen = self.units[u], self.offsets[u]
        for copy in self.copies(u, stage):
            copy.wait()
        phase, sums = unit.phases[stage], len(unit.sums)
        if stage == 0 and self.returns(u) is not None:
            partner = self.partner[unit.steps[phase][0]]
            pl.semaphore_signal(self.free_sems.at[u], inc=1, device_id=(partner,), device_id_type=MESH)
        if phase < unit.bits:
            _, _, sent, landing = unit.steps[phase]
            add_rows(self.held[u], seen[phase + 1] - seen[unit.sums[0] + 1], self.landed[u], landing, sent)
            if stage == sums - 1:
                self.store(u).start()
        elif sums and stage == sums:
            self.store(u).wait()

    def close(self):
        for u, unit in enumerate(self.units):
            if unit.sums and unit.stages == len(unit.sums):
                self.store(u).wait()

    def run(self, slot):
        for place, group in enumerate(self.groups):
            for u, unit in enumerate(self.units):
                stage = slot - place
                if unit.group != group:
                    continue
                if unit.phases[0] >= unit.bits and unit.phases[-1] == 2 * unit.bits - 1 and stage >= unit.stages - 1:
                    stage = unit.stages - 1 if slot == self.slots - 1 else -1
                if 0 <= stage < unit.stages:
                    self.end(u, stage)
                    if stage + 1 < unit.stages:
                        self.begin(u, stage + 1)


def gather_kernel(moves, *refs):
    count = len(moves)
    ins, row_ref, (*outs, sems) = refs[:count], refs[count], refs[count + 1 :]
    buffers, outs = outs[-count:], outs[:-count]
    loads = [pltpu.make_async_copy(source, buffer, sems.at[0, i]) for i, (source, buffer) in enumerate(zip(ins, buffers))]
    for load in loads:
        load.start()
    stores = []
    for i, (out, row, column) in enumerate(moves):
        rows, columns = buffers[i].shape[-2:]
        loads[i].wait()
        if i == count - 1:
            for batch in range(row_ref.shape[0]):
                buffers[i][batch, rows - 1 :] += row_ref[batch]
            stores.append(pltpu.make_async_copy(buffers[i], outs[out], sems.at[1, i]))
            stores[-1].start()
            break
        stores.append(pltpu.make_async_copy(buffers[i], outs[out].at[pl.ds(row, rows), pl.ds(column, columns)], sems.at[1, i]))
        stores[-1].start()
    for store in stores:
        store.wait()


def gathered(arrays, spans, hidden_width, tokens, last_row):
    width = arrays[0].shape[0]
    moves, shapes = [], [(width, hidden_width), (hidden_width, width)]
    for low, _ in spans:
        moves += [(0, 0, low), (1, low, 0)]
    arrays = arrays + [tokens]
    for array in arrays[len(moves) :]:
        moves.append((len(shapes), 0, 0))
        shapes.append(array.shape)
    return call(
        functools.partial(gather_kernel, moves),
        (1,),
        [(a, "any", None) for a in arrays] + [(last_row, last_row.shape, None)],
        [(shape, f32, "any", None) for shape in shapes],
        "gather",
        scratch=[pltpu.VMEM(a.shape, f32) for a in arrays] + [pltpu.SemaphoreType.DMA((2, len(moves)))],
    )


def local(
    incoming_hidden,
    packed_run_lengths,
    prior_standardize_factor,
    prior_standardize_addend,
    respond_interpolant,
    address_interpolant,
    content_interpolant,
    valve_interpolant,
    respond_transform,
    address_transform,
    content_transform,
    valve_transform,
    damping_rates,
    immediate_boost,
    cluster_normal_factor,
    cluster_normal_shift_term,
    readout_transform,
    posterior_standardize_factor,
    posterior_standardize_addend,
    dense_address_interpolant,
    dense_respond_interpolant,
    dense_address_transform,
    dense_content_transform,
    dense_respond_transform,
    objective_adjoint,
):
    batches, length, width = incoming_hidden.shape
    hidden_width = dense_address_transform.shape[1]
    pairs = width // PAIR
    depth = lax.axis_size("seq").bit_length() - 1
    lengths = packed_run_lengths
    vectors = [
        prior_standardize_factor, prior_standardize_addend, respond_interpolant, address_interpolant,
        content_interpolant, valve_interpolant, damping_rates, immediate_boost, cluster_normal_factor,
        cluster_normal_shift_term, posterior_standardize_factor, posterior_standardize_addend,
        dense_address_interpolant, dense_respond_interpolant,
    ]

    def table(w):
        return (w, w.shape, None)

    def rows_of(a):
        return (a, (1,) + a.shape[1:], lambda b, *_: (b,) + (0,) * (a.ndim - 1))

    def rows_out(shape, dtype=f32):
        return (shape, dtype, (1,) + tuple(shape[1:]), lambda b, *_: (b,) + (0,) * (len(shape) - 1))

    def sum_out(*shape):
        return (shape, f32, shape, None)

    tokens, states, one_row = (batches, length, width), (batches, pairs, LANE_FEATURES, PAIR), (batches, 1, width)
    square_flops = 2 * batches * length * width * width
    before = moved(incoming_hidden[:, -1, :].astype(f32), 1)[:, None, :]
    cols, row, vectors = call(
        tokens_kernel,
        (1,),
        [(lengths, "smem", None)] + [table(v) for v in vectors],
        [sum_out(batches, length, 8), sum_out(batches, 1, length), sum_out(16, width)],
        "tokens",
    )
    common = [rows_of(incoming_hidden), rows_of(before), rows_of(cols), table(vectors)]
    keys, values, end_state = call(
        functools.partial(project_kernel, (MIX_K, MIX_V), True),
        (batches,),
        common + [table(address_transform), table(content_transform)],
        [rows_out(tokens)] * 2 + [rows_out(states)],
        "project_keys",
        flops=4 * square_flops,
    )
    nearest = Carrier([end_state], lengths, vectors, length, 1, 0, 2)
    recept, valve, *near_state = call(
        functools.partial(project_kernel, (MIX_R, MIX_G), False),
        (batches,),
        common + [table(respond_transform), table(valve_transform)],
        [rows_out(tokens)] * 2,
        "project_recept",
        flops=4 * square_flops,
        hosts=[(nearest, [batches // 2, batches])],
        collective_id=1,
    )
    by_pair = lambda a: (a, (1, length, PAIR), lambda b, p: (b, 0, p))
    pair_vectors = (vectors, (vectors.shape[0], PAIR), lambda b, p: (0, p))
    pair_state = lambda s: (s, (1, 1, LANE_FEATURES, PAIR), lambda b, p: (b, p, 0, 0))
    pair_out = (tokens, f32, (1, length, PAIR), lambda b, p: (b, 0, p))
    further = Carrier(near_state, lengths, vectors, length, 1, 2)
    steps = batches * pairs
    mixed, state = call(
        mix_kernel,
        (batches, pairs),
        [by_pair(recept), by_pair(keys), by_pair(values), rows_of(cols), rows_of(row), pair_vectors],
        [pair_out],
        "mix",
        flops=3 * 2 * batches * length * length * width * 2,
        hosts=[(further, [(i + 1) * steps // further.slots for i in range(further.slots)])],
        collective_id=2,
    )
    tiles = length // BLOCK
    tiled = lambda a: (a, (1, BLOCK, a.shape[2]), lambda b, i: (b, i, 0))
    tiled_out = (tokens, f32, (1, BLOCK, width), lambda b, i: (b, i, 0))
    wkv, attended, second, second_row = call(
        readout_kernel,
        (batches, tiles),
        [
            tiled(mixed), tiled(recept), rows_of(state), tiled(valve), tiled(cols), table(vectors),
            tiled(incoming_hidden), table(readout_transform),
        ],
        [tiled_out] * 3 + [rows_out(one_row)],
        "readout",
        flops=2 * square_flops,
    )
    second_row = moved(second_row[:, 0, :], 1)[:, None, :]
    tile_rows = lambda a: (a, (1, BLOCK, a.shape[2]), lambda b, i: (b, tiles - 1 - i, 0))
    ahead = (second, (1, 8, width), lambda b, i: (b, jnp.maximum((tiles - 1 - i) * (BLOCK // 8) - 1, 0), 0))
    tile_out = lambda dtype: (tokens, dtype, (1, BLOCK, width), lambda b, i: (b, tiles - 1 - i, 0))
    spans = [(at, min(1024, hidden_width - at)) for at in range(0, hidden_width, 1024)]
    ends = 2 * depth

    even = [(0, 0, 128, 0), (0, 128, 128, 1), (0, 256, 512, 2), (1, 0, 512, 0), (1, 512, 512, 1)]
    rest_units = [(2, 0, 768, 0), (0, 0, 768, 1), (1, 0, 512, 2), (1, 512, 128, 2)]
    one = [(0, 0, 256, 0), (0, 256, 256, 1), (0, 512, 256, 2)]

    def layout_of(units, group, begin, end, base=0):
        return [(base + i, first, rows, 1, group, order, begin, end) for i, first, rows, order in units]

    def hosted(arrays, units, begin, end, when):
        summer = Summer(arrays, layout_of(units, 0, begin, end))
        return summer, [when[min(i, len(when) - 1)] for i in range(summer.slots)]

    def channel(part, kept, hosts, collective_id):
        low, size = spans[part]
        first, last = part == 0, part == len(spans) - 1
        ins = [
            tile_rows(second), ahead, rows_of(second_row), tile_rows(objective_adjoint), tile_rows(cols), table(vectors),
            (dense_address_transform, "any", None), (dense_content_transform, "any", None),
        ]
        ins += [table(dense_respond_transform)] if first or last else []
        ins += [tile_rows(a) for a in kept]
        ins += [tile_rows(attended)] if last else []
        if last:
            outs = [tile_out(bf16), tile_out(f32), rows_out(one_row), sum_out(width, width), sum_out(2, width)]
        else:
            outs = [tile_out(f32)] * (3 if first else 2)
        return call(
            functools.partial(channel_kernel, low, size, first, last),
            (batches, tiles),
            ins,
            outs + [sum_out(width, size), sum_out(size, width)],
            "channel_%d" % part,
            scratch=[
                pltpu.VMEM((BLOCK, 8), f32), pltpu.VMEM((width, size), bf16), pltpu.VMEM((size, width), bf16),
                pltpu.SemaphoreType.DMA((2,)), pltpu.VMEM((1, width), f32),
            ],
            flops=7 * 2 * batches * length * width * (2 * size + (width if last else 0)),
            hosts=hosts,
            collective_id=collective_id,
        )

    steps = batches * tiles
    gate, total, d_inner, *part_a = channel(0, [], [], None)
    total, d_inner, *rest = channel(1, [gate, total, d_inner], [hosted(part_a, even, 0, 4, [1, 3, 4])], 6)
    part_b, part_a = rest[:2], rest[2:]
    block, d_second, d_second_row, grad_filter, channel_vectors, *rest = channel(
        2,
        [gate, total, d_inner],
        [hosted(part_b, even, 0, 3, [1, 3, 4]), hosted(part_a, even, 4, depth + 2, [2, 3, 4])],
        7,
    )
    part_c, part_b, part_a = [rest[0], rest[1], grad_filter], rest[2:4], rest[4:6]
    back_second = moved(d_second_row[:, 0, :], -1)[:, None, :]
    d_attended, d_wkv, d_valve, gated, carry, attention_vectors, *rest = call(
        attention_back_kernel,
        (batches, tiles),
        [
            tiled(d_second), rows_of(back_second), tiled(attended), tiled(objective_adjoint), tiled(wkv),
            tiled(valve), tiled(recept), tiled(cols), table(vectors), table(readout_transform),
        ],
        [tiled_out] * 4 + [rows_out(states), sum_out(4, width)],
        "attention_back",
        flops=2 * square_flops,
        hosts=[
            hosted(part_c, rest_units, 0, 1, [3]),
            hosted(part_b, even, 3, depth + 1, [1, 4]),
            hosted(part_a, even, depth + 2, ends - 1, [2, 4]),
        ],
        collective_id=3,
    )
    part_c, part_b, part_a = rest[:3], rest[3:5], rest[5:7]
    steps = batches * pairs
    arriving = Carrier([carry], lengths, vectors, length, -1)
    d_recept, d_keys, d_values, mix_vectors, grad_output, out_state, *rest = call(
        mix_back_kernel,
        (batches, pairs),
        [
            by_pair(recept), by_pair(keys), by_pair(values), by_pair(d_wkv), pair_state(state), rows_of(cols), rows_of(row),
            pair_vectors, by_pair(gated), rows_of(d_attended),
        ],
        [pair_out] * 3 + [((batches, 2, width), f32, (1, 2, PAIR), lambda b, p: (b, 0, p)), sum_out(width, width)],
        "mix_back",
        flops=9 * 2 * batches * length * length * width * 2,
        hosts=[
            (arriving, [(i + 1) * steps // arriving.slots for i in range(arriving.slots)]),
            hosted(part_b, even, depth + 1, ends - 1, [2, 5, 9]),
            hosted(part_c, rest_units, 1, depth, [5, 8, 10, 12]),
            hosted(part_a, even, ends - 1, ends, [6]),
        ],
        collective_id=4,
    )
    part_b, part_c, part_a = rest[:2], rest[2:5], rest[5:7]
    steps = 4 * batches
    wide = lambda: pltpu.VMEM((length, width), f32)
    grad_recept, grad_keys, grad_values, grad_gate_w, d_keys, d_values, decay_vector, *rest = call(
        weights_back_kernel,
        (batches, 4),
        common
        + [
            rows_of(d_recept), rows_of(d_keys), rows_of(d_values), rows_of(d_valve), rows_of(keys), rows_of(values),
            rows_of(state), rows_of(out_state),
        ],
        [sum_out(width, width)] * 4 + [rows_out(tokens)] * 2 + [sum_out(1, width)],
        "weights_back",
        scratch=[wide(), wide()],
        flops=3 * 4 * square_flops,
        hosts=[
            hosted(part_c, rest_units, depth, ends - 2, [4, 6, 8]),
            hosted([grad_output], one, 0, depth - 1, [2, 4, 6, 8]),
            hosted(part_b, even, ends - 1, ends, [8]),
        ],
        collective_id=5,
    )
    part_c, grad_output, part_b = rest[:3], rest[3], rest[4:6]
    layout, part = [], width // 6
    for half in range(2):
        low = half * width // 2
        layout += layout_of([(i, low, width // 2, i) for i in range(3)], half, 0, ends, 4)
        layout += layout_of([(3, low + i * part, part, i) for i in range(3)], half, 0, ends, 4)
    layout += layout_of(rest_units, 2, ends - 2, ends) + layout_of(one, 2, depth - 1, ends, 3)
    summer = Summer(part_c + [grad_output, grad_recept, grad_keys, grad_values, grad_gate_w], layout)
    d_x, _, _, *rest = call(
        inputs_back_kernel,
        (batches, 4),
        common
        + [
            rows_of(d_attended), rows_of(d_recept), rows_of(d_keys), rows_of(d_values), rows_of(d_valve),
            rows_of(mix_vectors), table(attention_vectors), table(channel_vectors), table(decay_vector),
        ]
        + [table(w) for w in (respond_transform, address_transform, content_transform, valve_transform)],
        [rows_out(tokens), sum_out(*one_row), sum_out(*vectors.shape)],
        "inputs_back",
        scratch=[wide(), wide(), wide()],
        flops=2 * 4 * square_flops,
        hosts=[
            (summer, [3, 6, 8] + [steps] * (summer.slots - 3)),
            (VectorSum(2, 1, vectors.shape, one_row), [steps] * (depth + 1)),
        ],
        collective_id=0,
    )
    summed, vectors, last_row = rest[:8], rest[8], rest[9]
    w_expand, w_shrink, w_filter, w_output, w_recept, w_keys, w_values, w_gate, grad_tokens = gathered(
        part_a + part_b + list(summed), spans, hidden_width, d_x, last_row
    )
    return (
        block, grad_tokens, *[vectors[i] for i in range(6)], w_recept, w_keys, w_values, w_gate,
        vectors[6], vectors[7], vectors[8], vectors[9], w_output, vectors[10], vectors[11], vectors[12], vectors[13],
        w_expand, w_shrink, w_filter,
    )


def solution(mesh):
    rows = P(None, "seq", None)
    return jax.shard_map(
        local,
        mesh=mesh,
        in_specs=(rows,) + (P(),) * 23 + (rows,),
        out_specs=(rows, rows) + (P(),) * 22,
        check_vma=False,
    )
```

```python
import functools

import jax
import jax.numpy as jnp
from jax import lax
from jax.experimental import pallas as pl
from jax.experimental.pallas import tpu as pltpu
from jax.sharding import PartitionSpec as P

LANE_FEATURES = 64
PAIR = 2 * LANE_FEATURES
BLOCK = 256
f32 = jnp.float32
bf16 = jnp.bfloat16
VMEM_LIMIT = 60 * 1024 * 1024
MESH = pl.DeviceIdType.MESH


def nothing():
    pass


def split(x):
    high = x.astype(bf16)
    return high, (x - high.astype(f32)).astype(bf16)


def dot(a, b):
    return lax.dot_general(a, b, (((1,), (0,)), ((), ())), preferred_element_type=f32)


def dot_nt(a, b):
    return lax.dot_general(a, b, (((1,), (1,)), ((), ())), preferred_element_type=f32)


def dot_tn(a, b):
    return lax.dot_general(a, b, (((0,), (0,)), ((), ())), preferred_element_type=f32)


def times_weight(x, w):
    high, low = split(x)
    return dot(high, w) + dot(low, w)


def times_weight_t(x, w):
    high, low = split(x)
    return dot_nt(high, w) + dot_nt(low, w)


def outer_sum(a, b):
    return thrice(*split(a), *split(b))


def thrice(ah, al, bh, bl):
    return dot_tn(jnp.concatenate([ah, al, ah], axis=0), jnp.concatenate([bh, bh, bl], axis=0))


def both(high, low, w):
    out = dot(jnp.concatenate([high, low], axis=0), w)
    return out[: high.shape[0]] + out[high.shape[0] :]


def standard(x, epsilon=1e-05):
    centred = x - jnp.mean(x, axis=-1, keepdims=True)
    scale = lax.rsqrt(jnp.mean(centred * centred, axis=-1, keepdims=True) + epsilon)
    return centred * scale, scale


def standard_back(grad, normal, scale):
    return scale * (
        grad
        - jnp.mean(grad, axis=-1, keepdims=True)
        - normal * jnp.mean(grad * normal, axis=-1, keepdims=True)
    )


def first_lanes(rows):
    return lax.broadcasted_iota(jnp.int32, (rows, PAIR), 1) < LANE_FEATURES


def head_ones(scale):
    row = lax.broadcasted_iota(jnp.int32, (2 * PAIR, PAIR), 0) // LANE_FEATURES % 2
    col = lax.broadcasted_iota(jnp.int32, (2 * PAIR, PAIR), 1) // LANE_FEATURES
    return jnp.where(row == col, scale, 0.0).astype(bf16)


def head_sum(x, ones):
    return dot(jnp.concatenate(split(x), axis=1), ones)


def widen(state):
    first = first_lanes(LANE_FEATURES)
    return jnp.concatenate([jnp.where(first, state, 0.0), jnp.where(first, 0.0, state)], axis=0)


def compact(square):
    first = first_lanes(LANE_FEATURES)
    return jnp.where(first, square[:LANE_FEATURES], square[LANE_FEATURES:])


def times_state(x, square):
    xh, xl = split(x)
    sh, sl = split(square)
    return dot(jnp.concatenate([xh, xl], axis=1), jnp.concatenate([sh, sh], axis=0)) + dot(xh, sl)


def times_state_t(x, square):
    xh, xl = split(x)
    sh, sl = split(square)
    return dot_nt(jnp.concatenate([xh, xl], axis=1), jnp.concatenate([sh, sh], axis=1)) + dot_nt(xh, sl)


def cut(x):
    high = x.astype(bf16).astype(f32)
    low = x - high
    return high, low, pltpu.roll(high, LANE_FEATURES, 1), pltpu.roll(low, LANE_FEATURES, 1)


def high_low(pieces, first, head):
    high, low, high_r, low_r = pieces
    return (jnp.where(first, high, low_r) if head == 0 else jnp.where(first, high_r, low)).astype(bf16)


def doubled(pieces, first, head):
    high, low, high_r, low_r = pieces
    if head == 0:
        both = (jnp.where(first, high, high_r), jnp.where(first, low, low_r))
    else:
        both = (jnp.where(first, high_r, high), jnp.where(first, low_r, low))
    return jnp.concatenate([part.astype(bf16) for part in both], axis=1)


def twice(x):
    return jnp.concatenate([x, x], axis=1)


def folded(parts, first):
    sums = [part + pltpu.roll(part, LANE_FEATURES, 1) for part in parts]
    return jnp.where(first, sums[0], sums[1])


def decays(log_decay):
    step = lax.broadcasted_iota(jnp.int32, (BLOCK, PAIR), 0).astype(f32)
    return step, jnp.exp(log_decay * step), jnp.exp(-log_decay * (step + 1.0)), jnp.exp(log_decay * BLOCK)


def shifted(normal, row_before, keep):
    rows = lax.broadcasted_iota(jnp.int32, normal.shape, 0)
    return jnp.where(rows == 0, row_before, pltpu.roll(normal, 1, 0)) * keep


GAIN, BIAS, MIX_R, MIX_K, MIX_V, MIX_G, DECAY, BOOST, GROUP_GAIN, GROUP_SHIFT, GAIN2, BIAS2, MIX_E, MIX_F = range(14)


def vec(ref, which, lanes=slice(None)):
    return ref[which : which + 1, lanes]


def bounds_of(lengths_ref, batch):
    at, bounds = jnp.int32(0), []
    for j in range(lengths_ref.shape[1]):
        bounds.append(at)
        at = at + lengths_ref[batch, j]
    return bounds


def segment_of(bounds, position):
    return sum([(position >= bound).astype(jnp.int32) for bound in bounds])


def tokens_kernel(lengths_ref, *refs):
    *vector_refs, cols_ref, row_ref, packed_ref = refs
    for i, ref in enumerate(vector_refs):
        value = ref[...].reshape(1, ref.shape[0])
        packed_ref[i : i + 1] = -jnp.exp(value) if i == DECAY else value
    packed_ref[len(vector_refs) :] = jnp.zeros((2, packed_ref.shape[1]), f32)
    batches, length, columns = cols_ref.shape
    offset = lax.axis_index("seq") * length
    for batch in range(batches):
        bounds = bounds_of(lengths_ref, batch)
        place = offset + lax.broadcasted_iota(jnp.int32, (length, columns), 0)
        segment = segment_of(bounds, place)
        starts = functools.reduce(jnp.logical_or, [place == bound for bound in bounds])
        column = lax.broadcasted_iota(jnp.int32, (length, columns), 1)
        fresh = segment == segment_of(bounds, offset - 1)
        last = segment == segment_of(bounds, offset + length - 1)
        flag = jnp.where(column == 1, jnp.where(starts, 0, 1), jnp.where(column == 2, jnp.where(fresh, 1, 0), jnp.where(last, 1, 0)))
        cols_ref[batch] = jnp.where(column == 0, segment, flag).astype(f32)
        row_ref[batch] = segment_of(bounds, offset + lax.broadcasted_iota(jnp.int32, (1, length), 1)).astype(f32)


def project_kernel(mixes, states, x_ref, before_ref, cols_ref, vec_ref, *refs):
    count = len(mixes)
    weights, outs = refs[:count], refs[count : 2 * count]
    gain, bias = vec(vec_ref, GAIN), vec(vec_ref, BIAS)
    normal = standard(x_ref[0].astype(f32))[0] * gain + bias
    before = standard(before_ref[0])[0] * gain + bias
    earlier = shifted(normal, before, cols_ref[0, :, 1:2])
    difference = normal - earlier
    for mix, weight, out in zip(mixes, weights, outs):
        out[0] = times_weight(earlier + vec(vec_ref, mix) * difference, weight[...])
    if states:
        length, width = normal.shape
        keys, values, end_ref = outs[0], outs[1], refs[2 * count]
        rows = lax.broadcasted_iota(jnp.int32, (length, PAIR), 0).astype(f32)
        for pair in range(width // PAIR):
            lanes = slice(pair * PAIR, (pair + 1) * PAIR)
            tail = jnp.exp(vec(vec_ref, DECAY, lanes) * (length - 1.0 - rows)) * cols_ref[0, :, 3:4]
            end_ref[0, pair] = compact(outer_sum(keys[0, :, lanes] * tail, values[0, :, lanes]))


def allowed_here(cols_ref, row_ref, at, of, across):
    t_col = cols_ref[0, pl.ds(at * BLOCK, BLOCK), 0:1]
    s_row = row_ref[0, :, pl.ds(of * BLOCK, BLOCK)]
    mask = t_col == s_row
    if at == of:
        shape = (BLOCK, BLOCK)
        low, high = (1, 0) if not across else (0, 1)
        mask = jnp.logical_and(
            mask,
            lax.broadcasted_iota(jnp.int32, shape, low) < lax.broadcasted_iota(jnp.int32, shape, high),
        )
    return mask


def mix_kernel(recept_ref, keys_ref, values_ref, cols_ref, row_ref, vec_ref, out_ref):
    length = recept_ref.shape[1]
    log_decay, boost = vec(vec_ref, DECAY), vec(vec_ref, BOOST)
    first = first_lanes(BLOCK)
    step, fall, rise, whole = decays(log_decay)
    ones = head_ones(1.0)
    queries, near, far, values = [], [], [], []
    for at in range(length // BLOCK):
        here = pl.ds(at * BLOCK, BLOCK)
        queries.append(cut(recept_ref[0, here] * fall))
        raised = keys_ref[0, here] * rise
        near.append(cut(raised))
        far.append(raised * whole)
        values.append(cut(values_ref[0, here]))
    for at in range(length // BLOCK):
        here = pl.ds(at * BLOCK, BLOCK)
        totals = [jnp.zeros((BLOCK, PAIR), f32)] * 2
        for of in range(at + 1):
            mask = allowed_here(cols_ref, row_ref, at, of, False)
            gap = jnp.exp(log_decay * (BLOCK * (at - of - 1))) if at > of + 1 else None
            keys = near[of] if of == at else cut(far[of] if gap is None else far[of] * gap)
            for head in range(2):
                scores = dot_nt(twice(high_low(queries[at], first, head)), doubled(keys, first, head))
                sh, sl = split(jnp.where(mask, scores, 0.0))
                held = high_low(values[of], first, head)
                totals[head] = totals[head] + both(sh, sl, held)
        present = head_sum(recept_ref[0, here] * boost * keys_ref[0, here], ones)
        out_ref[0, here] = folded(totals, first) + present * values_ref[0, here]


def readout_kernel(
    mixed_ref, recept_ref, state_ref, valve_ref, cols_ref, vec_ref, x_ref, weight_ref,
    wkv_ref, attended_ref, second_ref, last_ref,
):
    length, width = mixed_ref.shape[1:]
    rows = (pl.program_id(1) * length + lax.broadcasted_iota(jnp.int32, (length, PAIR), 0)).astype(f32)
    ones = head_ones(1.0 / LANE_FEATURES)
    fresh = cols_ref[0, :, 2:3]
    gated = []
    for pair in range(width // PAIR):
        lanes = slice(pair * PAIR, (pair + 1) * PAIR)
        query = recept_ref[0, :, lanes] * jnp.exp(vec(vec_ref, DECAY, lanes) * rows) * fresh
        wkv = mixed_ref[0, :, lanes] + times_state(query, widen(state_ref[0, pair]))
        wkv_ref[0, :, lanes] = wkv
        centred = wkv - head_sum(wkv, ones)
        normal = centred * lax.rsqrt(head_sum(centred * centred, ones) + 0.00064)
        grouped = normal * vec(vec_ref, GROUP_GAIN, lanes) + vec(vec_ref, GROUP_SHIFT, lanes)
        gated.append(grouped * jax.nn.silu(valve_ref[0, :, lanes]))
    attended = x_ref[0].astype(f32) + times_weight(jnp.concatenate(gated, axis=1), weight_ref[...])
    attended_ref[0] = attended
    second = standard(attended)[0] * vec(vec_ref, GAIN2) + vec(vec_ref, BIAS2)
    second_ref[0] = second
    last_ref[0] = second[length - 1 :]


def pieces_of(total):
    cuts, at = [], 0
    while at < total:
        size = min(1024, total - at)
        cuts.append((at, size))
        at += size
    return cuts


def channel_kernel(low, size, first, last, shift, *refs):
    refs = list(refs)
    take = lambda count: [refs.pop(0) for _ in range(count)]
    second_ref, ahead_ref, received_ref, grad_ref, cols_ref, vec_ref, expand_any, shrink_any = take(8)
    filter_ref = take(1)[0] if first or last else None
    gate_ref = None if first else take(1)[0]
    total_in, inner_in = (None, None) if first else take(2)
    attended_ref = take(1)[0] if last else None
    gate_out = take(1)[0] if first else None
    if last:
        block_ref, d_second_ref, d_row_ref, d_filter_ref, d_vec_ref = take(5)
    else:
        total_out, inner_out = take(2)
    d_expand_ref, d_shrink_ref, hidden_ref, expand_ref, shrink_ref, sems, carry_ref = refs
    tiles = pl.num_programs(1)
    batch, turn = pl.program_id(0), pl.program_id(1)
    tile = tiles - 1 - turn
    start = jnp.logical_and(batch == 0, turn == 0)

    @pl.when(start)
    def _():
        loads = [
            pltpu.make_async_copy(expand_any.at[:, pl.ds(low, size)], expand_ref, sems.at[0]),
            pltpu.make_async_copy(shrink_any.at[pl.ds(low, size)], shrink_ref, sems.at[1]),
        ]
        for load in loads:
            load.start()
        for ref in [d_expand_ref, d_shrink_ref] + ([d_filter_ref, d_vec_ref] if last else []):
            ref[...] = jnp.zeros_like(ref)
        for load in loads:
            load.wait()

    keep = cols_ref[0, :, 1:2]
    second = second_ref[0]
    received = received_ref[0] if shift is None else shift.out_ref[pl.ds(batch, 1)][0]
    before = jnp.where(tile == 0, received, ahead_ref[0, 7:8])
    earlier = shifted(second, before, keep)
    difference = second - earlier
    mix_e, mix_f = vec(vec_ref, MIX_E), vec(vec_ref, MIX_F)
    inner_h, inner_l = split(earlier + mix_e * difference)
    if first or last:
        side_h, side_l = split(earlier + mix_f * difference)
    if first:
        gate = jax.nn.sigmoid(dot(side_h, filter_ref[...]) + dot(side_l, filter_ref[...]))
        gate_out[0] = gate
    else:
        gate = gate_ref[0]
    grad = grad_ref[0].astype(f32)
    dt_h, dt_l = split(grad * gate)
    total = jnp.zeros(second.shape, f32) if first else total_in[0]
    d_inner = jnp.zeros(second.shape, f32) if first else inner_in[0]
    for at, wide in pieces_of(size):
        lanes = slice(at, at + wide)
        raw = jnp.maximum(dot(inner_h, expand_ref[:, lanes]) + dot(inner_l, expand_ref[:, lanes]), 0.0)
        hid_h, hid_l = split(raw * raw)
        total = total + dot(hid_h, shrink_ref[lanes, :]) + dot(hid_l, shrink_ref[lanes, :])
        d_hidden = dot_nt(dt_h, shrink_ref[lanes, :]) + dot_nt(dt_l, shrink_ref[lanes, :])
        dr_h, dr_l = split(d_hidden * (2.0 * raw))
        d_shrink_ref[lanes, :] += thrice(hid_h, hid_l, dt_h, dt_l)
        d_expand_ref[:, lanes] += thrice(inner_h, inner_l, dr_h, dr_l)
        d_inner = d_inner + dot_nt(dr_h, expand_ref[:, lanes]) + dot_nt(dr_l, expand_ref[:, lanes])
    if not last:
        total_out[0] = total
        inner_out[0] = d_inner
        return
    block_ref[0] = (attended_ref[0] + gate * total).astype(bf16)
    ds_h, ds_l = split(grad * total * (gate * (1.0 - gate)))
    d_filter_ref[...] += thrice(side_h, side_l, ds_h, ds_l)
    d_side = dot_nt(ds_h, filter_ref[...]) + dot_nt(ds_l, filter_ref[...])
    d_vec_ref[0:1] += jnp.sum(d_inner * difference, axis=0, keepdims=True)
    d_vec_ref[1:2] += jnp.sum(d_side * difference, axis=0, keepdims=True)
    direct = mix_e * d_inner + mix_f * d_side
    passed = (d_inner + d_side - direct) * keep
    rows = lax.broadcasted_iota(jnp.int32, second.shape, 0)
    above = pltpu.roll(passed, second.shape[0] - 1, 0)
    outside = jnp.where(turn == 0, 0.0, carry_ref[...])
    d_second_ref[0] = direct + jnp.where(rows == second.shape[0] - 1, outside, above)
    carry_ref[...] = passed[0:1]
    d_row_ref[pl.ds(batch, 1)] = passed[0:1][None]


def attention_back_kernel(
    d_second_ref, back_ref, attended_ref, grad_ref, wkv_ref, valve_ref, recept_ref, cols_ref, vec_ref, weight_ref,
    d_attended_ref, d_wkv_ref, d_valve_ref, gated_ref, carry_ref, d_vec_ref,
):
    length, width = attended_ref.shape[1:]

    tile, is_last = pl.program_id(1), pl.program_id(1) == pl.num_programs(1) - 1

    @pl.when(jnp.logical_and(pl.program_id(0) == 0, tile == 0))
    def _():
        d_vec_ref[...] = jnp.zeros_like(d_vec_ref)

    rows = lax.broadcasted_iota(jnp.int32, (length, width), 0)
    d_second = d_second_ref[0] + jnp.where(jnp.logical_and(rows == length - 1, is_last), back_ref[0], 0.0)
    normal2, scale2 = standard(attended_ref[0])
    d_vec_ref[2:3] += jnp.sum(d_second * normal2, axis=0, keepdims=True)
    d_vec_ref[3:4] += jnp.sum(d_second, axis=0, keepdims=True)
    d_attended = grad_ref[0].astype(f32) + standard_back(d_second * vec(vec_ref, GAIN2), normal2, scale2)
    d_attended_ref[0] = d_attended
    d_gated = times_weight_t(d_attended, weight_ref[...])
    steps = (tile * length + lax.broadcasted_iota(jnp.int32, (length, PAIR), 0)).astype(f32)
    ones = head_ones(1.0 / LANE_FEATURES)
    fresh = cols_ref[0, :, 2:3]
    for pair in range(width // PAIR):
        lanes = slice(pair * PAIR, (pair + 1) * PAIR)
        wkv = wkv_ref[0, :, lanes]
        centred = wkv - head_sum(wkv, ones)
        scale = lax.rsqrt(head_sum(centred * centred, ones) + 0.00064)
        normal = centred * scale
        grouped = normal * vec(vec_ref, GROUP_GAIN, lanes) + vec(vec_ref, GROUP_SHIFT, lanes)
        valve = valve_ref[0, :, lanes]
        sigmoid = jax.nn.sigmoid(valve)
        gate = valve * sigmoid
        gated_ref[0, :, lanes] = grouped * gate
        d_here = d_gated[:, lanes]
        d_valve_ref[0, :, lanes] = d_here * grouped * (sigmoid * (1.0 + valve * (1.0 - sigmoid)))
        d_grouped = d_here * gate
        d_vec_ref[0:1, lanes] += jnp.sum(d_grouped * normal, axis=0, keepdims=True)
        d_vec_ref[1:2, lanes] += jnp.sum(d_grouped, axis=0, keepdims=True)
        d_normal = d_grouped * vec(vec_ref, GROUP_GAIN, lanes)
        d_wkv = scale * (d_normal - head_sum(d_normal, ones) - normal * head_sum(d_normal * normal, ones))
        d_wkv_ref[0, :, lanes] = d_wkv
        query = recept_ref[0, :, lanes] * jnp.exp(vec(vec_ref, DECAY, lanes) * steps) * fresh
        carried = compact(outer_sum(query, d_wkv))
        carry_ref[0, pair] = jnp.where(tile == 0, carried, carry_ref[0, pair] + carried)


def mix_back_kernel(
    recept_ref, keys_ref, values_ref, grad_ref, state_ref, cols_ref, row_ref, vec_ref,
    gated_ref, d_attended_ref, d_recept_ref, d_keys_ref, d_values_ref, d_vec_ref, d_weight_ref,
):
    length = recept_ref.shape[1]
    blocks = length // BLOCK
    first = first_lanes(BLOCK)
    log_decay, boost = vec(vec_ref, DECAY), vec(vec_ref, BOOST)
    step, fall, rise, whole = decays(log_decay)
    ones = head_ones(1.0)
    square = widen(state_ref[0, 0])
    queries, near, far, values, grads = [], [], [], [], []
    for at in range(blocks):
        here = pl.ds(at * BLOCK, BLOCK)
        queries.append(cut(recept_ref[0, here] * fall))
        raised = keys_ref[0, here] * rise
        near.append(cut(raised))
        far.append(raised * whole)
        values.append(cut(values_ref[0, here]))
        grads.append(cut(grad_ref[0, here]))
    zero = jnp.zeros((BLOCK, PAIR), f32)
    d_query = [[zero, zero] for _ in range(blocks)]
    d_value = [[zero, zero] for _ in range(blocks)]
    d_near = [[zero, zero] for _ in range(blocks)]
    d_far = [[zero, zero] for _ in range(blocks)]
    for at in range(blocks):
        for of in range(at + 1):
            mask = allowed_here(cols_ref, row_ref, at, of, False)
            t_row = row_ref[0, :, pl.ds(at * BLOCK, BLOCK)]
            s_col = cols_ref[0, pl.ds(of * BLOCK, BLOCK), 0:1]
            mask_t = s_col == t_row
            if at == of:
                shape = (BLOCK, BLOCK)
                mask_t = jnp.logical_and(
                    mask_t, lax.broadcasted_iota(jnp.int32, shape, 0) < lax.broadcasted_iota(jnp.int32, shape, 1)
                )
            gap = jnp.exp(log_decay * (BLOCK * (at - of - 1))) if at > of + 1 else None
            keys = near[of] if of == at else cut(far[of] if gap is None else far[of] * gap)
            mask, mask_t = jnp.where(mask, 1.0, 0.0), jnp.where(mask_t, 1.0, 0.0)
            for head in range(2):
                q_hl = high_low(queries[at], first, head)
                g_hl = high_low(grads[at], first, head)
                k_hl = high_low(keys, first, head)
                v_hl = high_low(values[of], first, head)
                scores_t = dot_nt(twice(k_hl), doubled(queries[at], first, head))
                s_h, s_l = split(scores_t * mask_t)
                d_value[of][head] = d_value[of][head] + both(s_h, s_l, g_hl)
                d_scores = dot_nt(twice(g_hl), doubled(values[of], first, head))
                s_h, s_l = split(d_scores * mask)
                d_query[at][head] = d_query[at][head] + both(s_h, s_l, k_hl)
                d_scores_t = dot_nt(twice(v_hl), doubled(grads[at], first, head))
                s_h, s_l = split(d_scores_t * mask_t)
                d_key = both(s_h, s_l, q_hl)
                if of == at:
                    d_near[of][head] = d_key
                else:
                    if gap is not None:
                        d_key = d_key * gap
                    d_far[of][head] = d_far[of][head] + d_key
    d_decay = jnp.zeros((1, PAIR), f32)
    d_boost = jnp.zeros((1, PAIR), f32)
    for at in range(blocks):
        here = pl.ds(at * BLOCK, BLOCK)
        recept, keys, value, grad = recept_ref[0, here], keys_ref[0, here], values_ref[0, here], grad_ref[0, here]
        fresh = cols_ref[0, here, 2:3]
        d_in = folded(d_query[at], first) * fall
        d_state = times_state_t(grad, square) * (fall * jnp.exp(log_decay * (BLOCK * at)) * fresh)
        d_here = folded(d_near[at], first) * rise
        d_later = folded(d_far[at], first) * (rise * whole)
        present = head_sum(recept * boost * keys, ones)
        d_present = head_sum(grad * value, ones)
        d_recept_ref[0, here] = d_in + d_state + boost * keys * d_present
        d_keys_ref[0, here] = d_here + d_later + boost * recept * d_present
        d_values_ref[0, here] = folded(d_value[at], first) + present * grad
        d_boost = d_boost + jnp.sum(recept * keys * d_present, axis=0, keepdims=True)
        d_decay = d_decay + jnp.sum(
            recept * (step * d_in + (step + float(BLOCK * at)) * d_state)
            + keys * ((BLOCK - 1.0 - step) * d_later - (step + 1.0) * d_here),
            axis=0,
            keepdims=True,
        )
    d_vec_ref[0, 0:1] = d_decay
    d_vec_ref[0, 1:2] = d_boost
    here = rows8(pl.program_id(1) * PAIR, PAIR)
    d_weight = outer_sum(gated_ref[0], d_attended_ref[0])
    first_batch = pl.program_id(0) == 0

    @pl.when(first_batch)
    def _():
        d_weight_ref[here] = d_weight

    @pl.when(jnp.logical_not(first_batch))
    def _():
        d_weight_ref[here] += d_weight


def weights_back_kernel(
    x_ref, before_ref, cols_ref, vec_ref,
    d_recept_ref, d_keys_ref, d_values_ref, d_valve_ref, keys_ref, values_ref, state_ref, out_state_ref,
    dw_r, dw_k, dw_v, dw_g, d_keys_out, d_values_out, d_decay_ref, earlier_ref, difference_ref,
):
    length, width = x_ref.shape[1:]
    turn = pl.program_id(1)
    steps = lax.broadcasted_iota(jnp.int32, (length, PAIR), 0).astype(f32)
    pairs = [(pair, slice(pair * PAIR, (pair + 1) * PAIR)) for pair in range(width // PAIR)]

    @pl.when(jnp.logical_and(pl.program_id(0) == 0, turn == 0))
    def _():
        for ref in (dw_r, dw_k, dw_v, dw_g, d_decay_ref):
            ref[...] = jnp.zeros_like(ref)

    def tail_of(lanes):
        return jnp.exp(vec(vec_ref, DECAY, lanes) * (length - 1.0 - steps)) * cols_ref[0, :, 3:4]

    def weigh(which, grad, d_weight):
        d_weight[...] += outer_sum(earlier_ref[...] + vec(vec_ref, which) * difference_ref[...], grad)

    @pl.when(turn == 0)
    def _():
        gain, bias = vec(vec_ref, GAIN), vec(vec_ref, BIAS)
        normal = standard(x_ref[0].astype(f32))[0] * gain + bias
        before = standard(before_ref[0])[0] * gain + bias
        earlier = shifted(normal, before, cols_ref[0, :, 1:2])
        earlier_ref[...] = earlier
        difference_ref[...] = normal - earlier
        weigh(MIX_G, d_valve_ref[0], dw_g)

    @pl.when(turn == 1)
    def _():
        weigh(MIX_R, d_recept_ref[0], dw_r)

    @pl.when(turn == 2)
    def _():
        for pair, lanes in pairs:
            d_keys = times_state_t(values_ref[0, :, lanes], widen(out_state_ref[0, pair])) * tail_of(lanes)
            later = (length - 1.0 - steps) * keys_ref[0, :, lanes] * d_keys
            square = widen(state_ref[0, pair]) * widen(out_state_ref[0, pair])
            ones = jnp.ones((8, PAIR), bf16)
            kept = sum([dot_nt(ones, part)[0:1] for part in split(square)])
            kept = kept * jnp.exp(vec(vec_ref, DECAY, lanes) * length) * (float(length) * cols_ref[0, length - 1 :, 2:3])
            d_decay_ref[:, lanes] += jnp.sum(later, axis=0, keepdims=True) + kept
            d_keys_out[0, :, lanes] = d_keys_ref[0, :, lanes] + d_keys
        weigh(MIX_K, d_keys_out[0], dw_k)

    @pl.when(turn == 3)
    def _():
        for pair, lanes in pairs:
            ended = times_state(keys_ref[0, :, lanes] * tail_of(lanes), widen(out_state_ref[0, pair]))
            d_values_out[0, :, lanes] = d_values_ref[0, :, lanes] + ended
        weigh(MIX_V, d_values_out[0], dw_v)


def inputs_back_kernel(
    x_ref, before_ref, cols_ref, vec_ref, d_attended_ref, d_recept_ref, d_keys_ref, d_values_ref, d_valve_ref,
    mix_vec_ref, attention_vec_ref, channel_vec_ref, d_decay_ref, w_r, w_k, w_v, w_g,
    d_x_ref, d_row_ref, packed_ref, difference_ref, direct_ref, passed_ref,
):
    length, width = x_ref.shape[1:]
    batch, turn = pl.program_id(0), pl.program_id(1)
    gain, bias = vec(vec_ref, GAIN), vec(vec_ref, BIAS)

    @pl.when(jnp.logical_and(batch == 0, turn == 0))
    def _():
        packed_ref[...] = jnp.zeros_like(packed_ref)
        packed_ref[GROUP_GAIN : BIAS2 + 1] = attention_vec_ref[...]
        packed_ref[MIX_E : MIX_F + 1] = channel_vec_ref[...]
        packed_ref[DECAY : DECAY + 1] = d_decay_ref[...]

    def through(grad, which, weight, first=False):
        mix = vec(vec_ref, which)
        d_mixed = times_weight_t(grad, weight[...])
        packed_ref[which : which + 1] += jnp.sum(d_mixed * difference_ref[...], axis=0, keepdims=True)
        direct, passed = mix * d_mixed, d_mixed - mix * d_mixed
        direct_ref[...] = direct if first else direct_ref[...] + direct
        passed_ref[...] = passed if first else passed_ref[...] + passed

    @pl.when(turn == 0)
    def _():
        normal = standard(x_ref[0].astype(f32))[0] * gain + bias
        before = standard(before_ref[0])[0] * gain + bias
        difference_ref[...] = normal - shifted(normal, before, cols_ref[0, :, 1:2])
        packed_ref[DECAY : BOOST + 1] += mix_vec_ref[0]
        through(d_recept_ref[0], MIX_R, w_r, True)

    @pl.when(turn == 1)
    def _():
        through(d_valve_ref[0], MIX_G, w_g)

    @pl.when(turn == 2)
    def _():
        through(d_keys_ref[0], MIX_K, w_k)

    @pl.when(turn == 3)
    def _():
        through(d_values_ref[0], MIX_V, w_v)
        passed = passed_ref[...] * cols_ref[0, :, 1:2]
        rows = lax.broadcasted_iota(jnp.int32, (length, width), 0)
        d_normal = direct_ref[...] + jnp.where(rows == length - 1, 0.0, pltpu.roll(passed, length - 1, 0))
        hat, scale = standard(x_ref[0].astype(f32))
        hat_before, scale_before = standard(before_ref[0])
        out = passed[0:1]
        packed_ref[GAIN : GAIN + 1] += jnp.sum(d_normal * hat, axis=0, keepdims=True) + out * hat_before
        packed_ref[BIAS : BIAS + 1] += jnp.sum(d_normal, axis=0, keepdims=True) + out
        d_x_ref[0] = d_attended_ref[0] + standard_back(d_normal * gain, hat, scale)
        d_row_ref[pl.ds(batch, 1)] = standard_back(out * gain, hat_before, scale_before)[None]

        @pl.when(batch == pl.num_programs(0) - 1)
        def _():
            packed_ref[DECAY : DECAY + 1] = packed_ref[DECAY : DECAY + 1] * vec(vec_ref, DECAY)


def call(kernel, grid, ins, outs, name, scratch=(), flops=0, hosts=(), collective_id=None, ticks=1):
    bytes_accessed = sum(a.size * a.dtype.itemsize for a, _, _ in ins)
    for shape, dtype, _, _ in outs:
        size = jnp.dtype(dtype).itemsize
        for extent in shape:
            size *= extent
        bytes_accessed += size

    def spec(block, index):
        if block == "smem":
            return pl.BlockSpec(memory_space=pltpu.SMEM)
        if block == "any":
            return pl.BlockSpec(memory_space=pl.ANY)
        if index is None:
            return pl.BlockSpec(block, lambda *_: (0,) * len(block), pipeline_mode=pl.Buffered(1))
        return pl.BlockSpec(block, index)

    ins, outs, scratch = list(ins), list(outs), list(scratch)
    own, places, aliases = (len(ins), len(outs), len(scratch)), [], {}
    for exchange, _ in hosts:
        more_in, more_out, alias = exchange.operands()
        aliases.update({len(ins) + i: len(outs) + j for i, j in alias})
        place = [len(ins), len(outs), len(scratch)]
        ins, outs, scratch = ins + more_in, outs + more_out, scratch + exchange.scratch()
        places.append([slice(a, b) for a, b in zip(place, (len(ins), len(outs), len(scratch)))])
    steps = 1
    for extent in grid:
        steps *= extent

    def body(*refs):
        in_refs, out_refs, scratch_refs = refs[: len(ins)], refs[len(ins) : len(ins) + len(outs)], refs[len(ins) + len(outs) :]
        step = pl.program_id(0)
        for axis in range(1, len(grid)):
            step = step * grid[axis] + pl.program_id(axis)
        for (exchange, _), (i, o, t) in zip(hosts, places):
            exchange.kernel_outs = out_refs[: own[1]]
            exchange.bind(in_refs[i], out_refs[o], scratch_refs[t])

        def enter():
            barrier = pltpu.get_barrier_semaphore()
            partners = [partner for exchange, _ in hosts for partner in exchange.partners()]
            for partner in partners:
                pl.semaphore_signal(barrier, inc=1, device_id=(partner,), device_id_type=MESH)
            pl.semaphore_wait(barrier, len(partners))
            for exchange, _ in hosts:
                exchange.start()

        def advance(turn):
            due = []
            for exchange, ends in hosts:
                slots = [slot for slot in range(exchange.slots) if min(ends[slot], steps * ticks) == turn]
                due += [((slot + 1) / exchange.slots, exchange, slot) for slot in slots]
            due.sort(key=lambda entry: entry[0])
            if due:

                @pl.when(step == min(turn // ticks, steps - 1))
                def _():
                    for _, exchange, slot in due:
                        exchange.run(slot)

        if hosts:
            pl.when(step == 0)(enter)
        for turn in range(steps):
            advance(turn * ticks)
        passed = []

        def tick():
            passed.append(0)
            if len(passed) < ticks:
                for turn in range(steps):
                    advance(turn * ticks + len(passed))

        more = {"tick": tick} if ticks > 1 else {}
        kernel(*in_refs[: own[0]], *out_refs[: own[1]], *scratch_refs[: own[2]], **more)
        advance(steps * ticks)
        if hosts:

            @pl.when(step == steps - 1)
            def _():
                for exchange, _ in hosts:
                    exchange.close()

    params = {"collective_id": collective_id, "has_side_effects": True} if hosts else {}
    return pl.pallas_call(
        body,
        grid=grid,
        in_specs=[spec(block, index) for _, block, index in ins],
        out_specs=[spec(block, index) for _, _, block, index in outs],
        out_shape=[jax.ShapeDtypeStruct(shape, dtype) for shape, dtype, _, _ in outs],
        input_output_aliases=aliases,
        scratch_shapes=scratch,
        compiler_params=pltpu.CompilerParams(
            dimension_semantics=("arbitrary",) * len(grid), vmem_limit_bytes=VMEM_LIMIT, **params
        ),
        cost_estimate=pl.CostEstimate(flops=flops, bytes_accessed=bytes_accessed, transcendentals=0),
        name=name,
    )(*[a for a, _, _ in ins])


def moved(value, steps):
    count = lax.axis_size("seq")
    low, high = max(0, -steps), min(count, count - steps)
    return lax.ppermute(value, "seq", [(source, source + steps) for source in range(low, high)])


def reach(count):
    window, needed, hops = 2, {32: 16, 128: 32}.get(count, count) // 2, []
    while window < needed:
        hops.append(window)
        window *= 2
    return hops


class Carrier:
    def __init__(self, parts, lengths, vectors, length, sign, begin=0, end=None):
        self.count = lax.axis_size("seq")
        self.parts, self.lengths, self.vectors, self.length, self.sign = parts, lengths, vectors, length, sign
        self.hops = [[1, 2]] + [[hop] for hop in reach(self.count)]
        self.whole = len(self.hops) + 2
        self.begin, self.end = begin, self.whole if end is None else end
        self.slots = self.end - self.begin
        batches, pairs = parts[0].shape[:2]
        self.half = pairs // 2 if begin == 0 else pairs
        self.shape = (batches, self.half) + parts[0].shape[2:]

    def operands(self):
        shape = self.shape
        full = (shape[0], 2 * self.half) + shape[2:]
        outs = [(full, f32, full, None)] if self.end == self.whole else [(shape, f32, shape, None)] * 2
        ins = [(part, part.shape, None) for part in self.parts]
        return ins + [(self.vectors, self.vectors.shape, None), (self.lengths, "smem", None)], outs, []

    def scratch(self):
        return [
            pltpu.VMEM((self.slots, 2) + self.shape, f32),
            pltpu.VMEM((self.slots + 1,) + self.shape, f32),
            pltpu.VMEM((2,) + self.shape, f32),
            pltpu.SemaphoreType.DMA((self.slots, 2)),
            pltpu.SemaphoreType.DMA((self.slots, 2)),
        ]

    def bind(self, ins, outs, scratch):
        *self.part_refs, self.vec_ref, self.lengths_ref = ins
        self.out_refs = outs
        self.landed, self.totals, self.kept, self.send_sems, self.recv_sems = scratch
        self.mine = lax.axis_index("seq")
        self.core, self.chip = self.mine % 2, self.mine // 2
        self.sibling = self.mine + 1 - 2 * self.core

    def chip_at(self, hop):
        chips = self.count // 2
        return (self.chip + hop + chips) % chips * 2 + self.core

    def partners(self):
        out = []
        for slot in range(self.begin, self.end):
            if slot in (0, self.whole - 1):
                out.append(self.sibling)
            else:
                out += [self.chip_at(sign * hop) for hop in self.hops[slot - 1] for sign in (1, -1)]
        return out

    def first_part(self):
        return self.kept.at[0] if self.begin == 0 else self.part_refs[1]

    def total(self, slot):
        return self.part_refs[0] if slot == self.begin and slot > 0 else self.totals.at[slot - self.begin]

    def copies(self, slot):
        at = slot - self.begin
        if slot == 0:
            away = self.part_refs[0].at[:, pl.ds((1 - self.core) * self.half, self.half)]
            moves = [(away, self.landed.at[at, 0], self.sibling)]
        elif slot == self.whole - 1:
            moves = [(self.kept.at[1], self.landed.at[at, 0], self.sibling)]
        else:
            moves = [
                (self.total(slot), self.landed.at[at, i], self.chip_at(self.sign * hop))
                for i, hop in enumerate(self.hops[slot - 1])
            ]
        return [
            pltpu.make_async_remote_copy(
                src_ref=source, dst_ref=target, send_sem=self.send_sems.at[at, i], recv_sem=self.recv_sems.at[at, i],
                device_id=(device,), device_id_type=MESH,
            )
            for i, (source, target, device) in enumerate(moves)
        ]

    def start(self):
        self.open(self.begin)

    def open(self, slot):
        if slot == self.whole - 1:
            self.finish()
        for copy in self.copies(slot):
            copy.start()

    def fade(self, pair, devices):
        lane = lax.broadcasted_iota(jnp.int32, (LANE_FEATURES, PAIR), 1)
        row = lax.broadcasted_iota(jnp.int32, (LANE_FEATURES, PAIR), 0)
        at = pl.multiple_of((self.core * self.half + pair) * PAIR, PAIR)
        decay = self.vec_ref[DECAY : DECAY + 1, pl.ds(at, PAIR)] * float(self.length * devices)
        heads = [
            jnp.sum(jnp.where(lane == row + head * LANE_FEATURES, decay, 0.0), axis=1, keepdims=True) for head in range(2)
        ]
        return jnp.exp(jnp.where(first_lanes(LANE_FEATURES), heads[0], heads[1]))

    def same(self, batch, bound, other):
        bounds = bounds_of(self.lengths_ref, batch)
        ends = [segment_of(bounds, (device + 1) * self.length - 1) for device in (bound, other)]
        return jnp.where(ends[0] == ends[1], 1.0, 0.0).astype(f32)

    def edges(self):
        middle = 2 * self.chip
        return middle - self.sign, middle, middle + self.sign

    def run(self, slot):
        slot = slot + self.begin
        at = slot - self.begin
        for copy in self.copies(slot):
            copy.wait()
        batches = self.shape[0]
        entry, middle, leaving = self.edges()
        if slot == 0:
            flags = [self.same(batch, middle, leaving) for batch in range(batches)]
            is_first = self.core == (0 if self.sign > 0 else 1)
            for pair in range(self.half):
                fade = self.fade(pair, 1)
                for batch in range(batches):
                    own = self.part_refs[0][batch, self.core * self.half + pair]
                    other = self.landed[at, 0, batch, pair]
                    ahead, behind = jnp.where(is_first, own, other), jnp.where(is_first, other, own)
                    self.kept[0, batch, pair] = ahead
                    self.totals[at + 1, batch, pair] = ahead * fade * flags[batch] + behind
        elif slot < self.whole - 1:
            hops = self.hops[slot - 1]
            chips = self.count // 2
            flags = []
            for hop in hops:
                there = self.chip - self.sign * hop
                exists = jnp.where(jnp.logical_and(there >= 0, there < chips), 1.0, 0.0).astype(f32)
                crossed = hop - 1 if slot == 1 else hop
                flags.append([exists * self.same(batch, entry - 2 * self.sign * crossed, entry) for batch in range(batches)])
            for pair in range(self.half):
                fade = self.fade(pair, 2 if slot == 1 else 2 * hops[0])
                for batch in range(batches):
                    if slot == 1:
                        near, far = self.landed[at, 0, batch, pair], self.landed[at, 1, batch, pair]
                        here = near * flags[0][batch] + far * fade * flags[1][batch]
                    else:
                        here = self.total(slot)[batch, pair] + self.landed[at, 0, batch, pair] * fade * flags[0][batch]
                    self.totals[at + 1, batch, pair] = here
        else:
            for pair in range(self.half):
                for batch in range(batches):
                    self.out_refs[0][batch, (1 - self.core) * self.half + pair] = self.landed[at, 0, batch, pair]
        if slot + 1 < self.end:
            self.open(slot + 1)
        elif self.end < self.whole:
            self.out_refs[0][...] = self.totals[at + 1]
            self.out_refs[1][...] = self.first_part()[...]

    def close(self):
        pass

    def finish(self):
        entry, middle, _ = self.edges()
        total, first_part = self.total(self.whole - 1), self.first_part()
        is_first = self.core == (0 if self.sign > 0 else 1)
        flags = [self.same(batch, entry, middle) for batch in range(self.shape[0])]
        for pair in range(self.half):
            fade = self.fade(pair, 1)
            for batch in range(self.shape[0]):
                first = total[batch, pair]
                second = first * fade * flags[batch] + first_part[batch, pair]
                self.out_refs[0][batch, self.core * self.half + pair] = jnp.where(is_first, first, second)
                self.kept[1, batch, pair] = jnp.where(is_first, second, first)


def bit_orders(count):
    bits = count.bit_length() - 1
    if bits == 5:
        return [(0, 1, 2, 3, 4), (0, 2, 3, 1, 4), (0, 3, 1, 2, 4)]
    chip = list(range(1, bits))
    third = max(1, len(chip) // 3)
    return [tuple([0] + chip[k * third :] + chip[: k * third]) for k in range(3)]


class Unit:
    def __init__(self, array, first, rows, width, order, group, begin, end):
        self.array, self.first, self.rows, self.width, self.group = array, first, rows, width, group
        self.steps, size, landing = [], rows, 0
        bits = self.bits = len(order)
        for k, bit in enumerate(order):
            halved = size % 16 == 0
            sent = size // 2 if halved else size
            self.steps.append((bit, halved, sent, landing))
            if begin <= k < end:
                landing += sent
            size = sent
        phases = [p for p in range(2 * bits) if p < bits or self.steps[2 * bits - 1 - p][1]]
        self.phases = [p for p in phases if begin <= p < end]
        self.sums = [p for p in self.phases if p < bits]
        self.landing = landing
        self.held = self.steps[self.sums[0]][2] if self.sums else 0
        self.stages = len(self.phases)


class RowShift:
    def __init__(self, shape, hops, row=None, which=None):
        self.count, self.shape, self.hops, self.row, self.which = lax.axis_size("seq"), shape, hops, row, which
        self.slots = 1 if which is None else 2

    def operands(self):
        ins = [(self.row, self.shape, None)] if self.which is None else []
        return ins, [(self.shape, f32, self.shape, None)], []

    def scratch(self):
        return [pltpu.VMEM((2,) + self.shape, f32), pltpu.SemaphoreType.DMA, pltpu.SemaphoreType.DMA]

    def bind(self, ins, outs, scratch):
        self.in_refs, (self.out_ref,) = ins, outs
        self.rows, self.send_sem, self.recv_sem = scratch
        mine = lax.axis_index("seq")
        self.sent_to, self.got_from = (mine + self.hops + self.count) % self.count, mine - self.hops

    def partners(self):
        return [self.sent_to, (self.got_from + self.count) % self.count]

    def copy(self):
        return pltpu.make_async_remote_copy(
            src_ref=self.rows.at[0], dst_ref=self.rows.at[1], send_sem=self.send_sem, recv_sem=self.recv_sem,
            device_id=(self.sent_to,), device_id_type=MESH,
        )

    def send(self, source):
        self.rows[0] = source[...]
        self.copy().start()

    def start(self):
        if self.which is None:
            self.send(self.in_refs[0])

    def run(self, slot):
        if slot < self.slots - 1:
            self.send(self.kernel_outs[self.which])
        else:
            self.copy().wait()
            inside = jnp.logical_and(self.got_from >= 0, self.got_from < self.count)
            self.out_ref[...] = jnp.where(inside, self.rows[1], 0.0)

    def close(self):
        pass


class VectorSum:
    def __init__(self, which, row, shape, row_shape):
        self.count = lax.axis_size("seq")
        self.which, self.row, self.shape, self.row_shape = which, row, shape, row_shape
        self.bits = self.count.bit_length() - 1
        self.slots = self.bits + 1

    def operands(self):
        return [], [(self.shape, f32, self.shape, None), (self.row_shape, f32, self.row_shape, None)], []

    def scratch(self):
        return [
            pltpu.VMEM((self.bits + 1,) + self.shape, f32), pltpu.VMEM((self.bits,) + self.shape, f32),
            pltpu.VMEM((2,) + self.row_shape, f32),
            pltpu.SemaphoreType.DMA((self.bits + 1,)), pltpu.SemaphoreType.DMA((self.bits + 1,)),
        ]

    def bind(self, ins, outs, scratch):
        self.out_ref, self.row_ref = outs
        self.sums, self.landed, self.rows, self.send_sems, self.recv_sems = scratch
        mine = lax.axis_index("seq")
        self.partner = [mine + (1 - 2 * (mine // (1 << k) % 2)) * (1 << k) for k in range(self.bits)]
        self.ahead, self.behind = (mine + self.count - 1) % self.count, (mine + 1) % self.count

    def partners(self):
        return self.partner + [self.ahead, self.behind]

    def start(self):
        pass

    def close(self):
        pass

    def copy(self, k):
        if k == self.bits:
            source, target, device = self.rows.at[0], self.rows.at[1], self.ahead
        else:
            source, target, device = self.sums.at[k], self.landed.at[k], self.partner[k]
        return pltpu.make_async_remote_copy(
            src_ref=source, dst_ref=target, send_sem=self.send_sems.at[k], recv_sem=self.recv_sems.at[k],
            device_id=(device,), device_id_type=MESH,
        )

    def run(self, slot):
        if slot == 0:
            self.sums[0] = self.kernel_outs[self.which][...]
            self.rows[0] = self.kernel_outs[self.row][...]
            self.copy(self.bits).start()
        else:
            self.copy(slot - 1).wait()
            self.sums[slot] = self.sums[slot - 1] + self.landed[slot - 1]
        if slot < self.bits:
            self.copy(slot).start()
        else:
            self.out_ref[...] = self.sums[slot]
            self.copy(self.bits).wait()
            self.row_ref[...] = self.rows[1]


def add_rows(target, at, source, source_at, rows):
    block = next(b for b in (64, 56, 48, 32, 24, 16, 8) if rows % b == 0)

    def step(i, _):
        here = pl.ds(pl.multiple_of(at + i * block, 8), block)
        target[here] = target[here] + source[pl.ds(pl.multiple_of(source_at + i * block, 8), block)]
        return 0

    lax.fori_loop(0, rows // block, step, 0)


def rows8(at, size):
    return pl.ds(pl.multiple_of(at, 8), size)


class Summer:
    def __init__(self, arrays, layout):
        self.count, self.arrays, self.units = lax.axis_size("seq"), arrays, []
        orders = bit_orders(self.count)
        for array, first, rows, parts, group, turn, begin, end in layout:
            size = rows // parts
            for part in range(parts):
                order, width = orders[(turn + part) % 3], arrays[array].shape[1]
                unit = Unit(array, first + part * size, size, width, order, group, begin, end)
                self.units += [unit] if unit.phases else []
        self.groups = sorted({unit.group for unit in self.units})
        self.stages = max(unit.stages for unit in self.units)
        self.slots = self.stages + len(self.groups) - 1

    def operands(self):
        arrays = self.arrays
        return (
            [(a, "any", None) for a in arrays],
            [(a.shape, a.dtype, "any", None) for a in arrays],
            [(i, i) for i in range(len(arrays))],
        )

    def scratch(self):
        return (
            [pltpu.VMEM((max(8, unit.held), unit.width), f32) for unit in self.units]
            + [pltpu.VMEM((max(8, unit.landing), unit.width), f32) for unit in self.units]
            + [
                pltpu.SemaphoreType.DMA((len(self.units), self.stages)),
                pltpu.SemaphoreType.DMA((len(self.units), self.stages)),
                pltpu.SemaphoreType.DMA((len(self.units), 2)),
                pltpu.SemaphoreType.REGULAR((len(self.units),)),
            ]
        )

    def bind(self, ins, outs, scratch):
        size = len(self.units)
        self.refs, self.held, self.landed = outs, scratch[:size], scratch[size : 2 * size]
        self.send_sems, self.recv_sems, self.local_sems, self.free_sems = scratch[2 * size :]
        mine = lax.axis_index("seq")
        bits = self.count.bit_length() - 1
        self.bit = [mine // (1 << k) % 2 for k in range(bits)]
        self.partner = [mine + (1 - 2 * self.bit[k]) * (1 << k) for k in range(bits)]
        self.offsets = []
        for unit in self.units:
            at, seen = 0, [0]
            for which, halved, sent, _ in unit.steps:
                at = at + self.bit[which] * sent if halved else at
                seen.append(at)
            self.offsets.append(seen)

    def partners(self):
        used = sorted({unit.steps[min(p, 2 * unit.bits - 1 - p)][0] for unit in self.units for p in unit.phases})
        return [self.partner[k] for k in used]

    def start(self):
        for group in self.groups:
            for u, unit in enumerate(self.units):
                if unit.group == group:
                    self.begin(u, 0)

    def own(self, u, step):
        unit = self.units[u]
        return self.refs[unit.array].at[rows8(unit.first + self.offsets[u][step + 1], unit.steps[step][2])]

    def copies(self, u, stage):
        unit, seen, here = self.units[u], self.offsets[u], self.refs[self.units[u].array]
        phase, out = unit.phases[stage], []
        if phase < unit.bits:
            which, halved, sent, landing = unit.steps[phase]
            away = seen[phase] + (1 - self.bit[which]) * sent if halved else seen[phase]
            target = self.landed[u].at[pl.ds(landing, sent)]
            if stage == 0:
                source = here.at[rows8(unit.first + away, sent)]
                out.append(pltpu.make_async_copy(self.own(u, phase), self.held[u], self.local_sems.at[u, 0]))
            else:
                source = self.held[u].at[rows8(away - seen[unit.sums[0] + 1], sent)]
        else:
            step = 2 * unit.bits - 1 - phase
            which, _, sent, _ = unit.steps[step]
            source = target = self.own(u, step)
            if unit.sums and stage == len(unit.sums):
                source = self.held[u].at[rows8(seen[step + 1] - seen[unit.sums[0] + 1], sent)]
        return out + [
            pltpu.make_async_remote_copy(
                src_ref=source, dst_ref=target, send_sem=self.send_sems.at[u, stage],
                recv_sem=self.recv_sems.at[u, stage], device_id=(self.partner[which],), device_id_type=MESH,
            )
        ]

    def store(self, u):
        unit, seen = self.units[u], self.offsets[u]
        step = unit.sums[-1]
        source = self.held[u].at[rows8(seen[step + 1] - seen[unit.sums[0] + 1], unit.steps[step][2])]
        return pltpu.make_async_copy(source, self.own(u, step), self.local_sems.at[u, 1])

    def returns(self, u):
        unit = self.units[u]
        back = 2 * unit.bits - 1 - unit.phases[0]
        return unit.phases.index(back) if unit.sums and back in unit.phases else None

    def begin(self, u, stage):
        if stage == self.returns(u):
            pl.semaphore_wait(self.free_sems.at[u], 1)
        for copy in self.copies(u, stage):
            copy.start()

    def end(self, u, stage):
        unit, seen = self.units[u], self.offsets[u]
        for copy in self.copies(u, stage):
            copy.wait()
        phase, sums = unit.phases[stage], len(unit.sums)
        if stage == 0 and self.returns(u) is not None:
            partner = self.partner[unit.steps[phase][0]]
            pl.semaphore_signal(self.free_sems.at[u], inc=1, device_id=(partner,), device_id_type=MESH)
        if phase < unit.bits:
            _, _, sent, landing = unit.steps[phase]
            add_rows(self.held[u], seen[phase + 1] - seen[unit.sums[0] + 1], self.landed[u], landing, sent)
            if stage == sums - 1:
                self.store(u).start()
        elif sums and stage == sums:
            self.store(u).wait()

    def close(self):
        for u, unit in enumerate(self.units):
            if unit.sums and unit.stages == len(unit.sums):
                self.store(u).wait()

    def run(self, slot):
        for place, group in enumerate(self.groups):
            for u, unit in enumerate(self.units):
                stage = slot - place
                if unit.group != group:
                    continue
                if unit.phases[0] >= unit.bits and unit.phases[-1] == 2 * unit.bits - 1 and stage >= unit.stages - 1:
                    stage = unit.stages - 1 if slot == self.slots - 1 else -1
                if 0 <= stage < unit.stages:
                    self.end(u, stage)
                    if stage + 1 < unit.stages:
                        self.begin(u, stage + 1)


def gather_kernel(moves, *refs):
    count = len(moves)
    ins, row_ref, vectors_ref, (*outs, sems) = refs[:count], refs[count], refs[count + 1], refs[count + 2 :]
    buffers, outs = outs[-count:], outs[:-count]
    loads = [pltpu.make_async_copy(source, buffer, sems.at[0, i]) for i, (source, buffer) in enumerate(zip(ins, buffers))]
    for load in loads:
        load.start()
    for i, ref in enumerate(outs[moves[-1][0] + 1 :]):
        ref[...] = vectors_ref[i : i + 1].reshape(ref.shape)
    stores = []
    for i, (out, row, column) in enumerate(moves):
        rows, columns = buffers[i].shape[-2:]
        loads[i].wait()
        if i == count - 1:
            for batch in range(row_ref.shape[0]):
                buffers[i][batch, rows - 1 :] += row_ref[batch]
            stores.append(pltpu.make_async_copy(buffers[i], outs[out], sems.at[1, i]))
            stores[-1].start()
            break
        stores.append(pltpu.make_async_copy(buffers[i], outs[out].at[pl.ds(row, rows), pl.ds(column, columns)], sems.at[1, i]))
        stores[-1].start()
    for store in stores:
        store.wait()


def gathered(arrays, spans, hidden_width, tokens, last_row, vectors, count):
    width = arrays[0].shape[0]
    moves, shapes = [], [(width, hidden_width), (hidden_width, width)]
    for low, _ in spans:
        moves += [(0, 0, low), (1, low, 0)]
    arrays = arrays + [tokens]
    for array in arrays[len(moves) :]:
        moves.append((len(shapes), 0, 0))
        shapes.append(array.shape)
    return call(
        functools.partial(gather_kernel, moves),
        (1,),
        [(a, "any", None) for a in arrays] + [(last_row, last_row.shape, None), (vectors, vectors.shape, None)],
        [(shape, f32, "any", None) for shape in shapes] + [((width,), f32, (width,), None)] * count,
        "gather",
        scratch=[pltpu.VMEM(a.shape, f32) for a in arrays] + [pltpu.SemaphoreType.DMA((2, len(moves)))],
    )


def local(
    incoming_hidden,
    packed_run_lengths,
    prior_standardize_factor,
    prior_standardize_addend,
    respond_interpolant,
    address_interpolant,
    content_interpolant,
    valve_interpolant,
    respond_transform,
    address_transform,
    content_transform,
    valve_transform,
    damping_rates,
    immediate_boost,
    cluster_normal_factor,
    cluster_normal_shift_term,
    readout_transform,
    posterior_standardize_factor,
    posterior_standardize_addend,
    dense_address_interpolant,
    dense_respond_interpolant,
    dense_address_transform,
    dense_content_transform,
    dense_respond_transform,
    objective_adjoint,
):
    batches, length, width = incoming_hidden.shape
    hidden_width = dense_address_transform.shape[1]
    pairs = width // PAIR
    depth = lax.axis_size("seq").bit_length() - 1
    lengths = packed_run_lengths
    vectors = [
        prior_standardize_factor, prior_standardize_addend, respond_interpolant, address_interpolant,
        content_interpolant, valve_interpolant, damping_rates, immediate_boost, cluster_normal_factor,
        cluster_normal_shift_term, posterior_standardize_factor, posterior_standardize_addend,
        dense_address_interpolant, dense_respond_interpolant,
    ]

    def table(w):
        return (w, w.shape, None)

    def rows_of(a):
        return (a, (1,) + a.shape[1:], lambda b, *_: (b,) + (0,) * (a.ndim - 1))

    def rows_out(shape, dtype=f32):
        return (shape, dtype, (1,) + tuple(shape[1:]), lambda b, *_: (b,) + (0,) * (len(shape) - 1))

    def sum_out(*shape):
        return (shape, f32, shape, None)

    tokens, states, one_row = (batches, length, width), (batches, pairs, LANE_FEATURES, PAIR), (batches, 1, width)
    square_flops = 2 * batches * length * width * width
    before = moved(incoming_hidden[:, -1, :].astype(f32), 1)[:, None, :]
    cols, row, vectors = call(
        tokens_kernel,
        (1,),
        [(lengths, "smem", None)] + [table(v) for v in vectors],
        [sum_out(batches, length, 8), sum_out(batches, 1, length), sum_out(16, width)],
        "tokens",
    )
    common = [rows_of(incoming_hidden), rows_of(before), rows_of(cols), table(vectors)]
    keys, values, end_state = call(
        functools.partial(project_kernel, (MIX_K, MIX_V), True),
        (batches,),
        common + [table(address_transform), table(content_transform)],
        [rows_out(tokens)] * 2 + [rows_out(states)],
        "project_keys",
        flops=4 * square_flops,
    )
    nearest = Carrier([end_state], lengths, vectors, length, 1, 0, 2)
    recept, valve, *near_state = call(
        functools.partial(project_kernel, (MIX_R, MIX_G), False),
        (batches,),
        common + [table(respond_transform), table(valve_transform)],
        [rows_out(tokens)] * 2,
        "project_recept",
        flops=4 * square_flops,
        hosts=[(nearest, [batches // 2, batches])],
        collective_id=1,
    )
    by_pair = lambda a: (a, (1, length, PAIR), lambda b, p: (b, 0, p))
    pair_vectors = (vectors, (vectors.shape[0], PAIR), lambda b, p: (0, p))
    pair_state = lambda s: (s, (1, 1, LANE_FEATURES, PAIR), lambda b, p: (b, p, 0, 0))
    pair_out = (tokens, f32, (1, length, PAIR), lambda b, p: (b, 0, p))
    further = Carrier(near_state, lengths, vectors, length, 1, 2)
    steps = batches * pairs
    mixed, state = call(
        mix_kernel,
        (batches, pairs),
        [by_pair(recept), by_pair(keys), by_pair(values), rows_of(cols), rows_of(row), pair_vectors],
        [pair_out],
        "mix",
        flops=3 * 2 * batches * length * length * width * 2,
        hosts=[(further, [(i + 1) * steps // further.slots for i in range(further.slots)])],
        collective_id=2,
    )
    tiles = length // BLOCK
    tiled = lambda a: (a, (1, BLOCK, a.shape[2]), lambda b, i: (b, i, 0))
    tiled_out = (tokens, f32, (1, BLOCK, width), lambda b, i: (b, i, 0))
    wkv, attended, second, second_row = call(
        readout_kernel,
        (batches, tiles),
        [
            tiled(mixed), tiled(recept), rows_of(state), tiled(valve), tiled(cols), table(vectors),
            tiled(incoming_hidden), table(readout_transform),
        ],
        [tiled_out] * 3 + [rows_out(one_row)],
        "readout",
        flops=2 * square_flops,
    )
    tile_rows = lambda a: (a, (1, BLOCK, a.shape[2]), lambda b, i: (b, tiles - 1 - i, 0))
    ahead = (second, (1, 8, width), lambda b, i: (b, jnp.maximum((tiles - 1 - i) * (BLOCK // 8) - 1, 0), 0))
    tile_out = lambda dtype: (tokens, dtype, (1, BLOCK, width), lambda b, i: (b, tiles - 1 - i, 0))
    spans = [(at, min(1024, hidden_width - at)) for at in range(0, hidden_width, 1024)]
    ends = 2 * depth

    even = [(0, 0, 128, 0), (0, 128, 128, 1), (0, 256, 512, 2), (1, 0, 512, 0), (1, 512, 512, 1)]
    rest_units = [(2, 0, 768, 0), (0, 0, 768, 1), (1, 0, 512, 2), (1, 512, 128, 2)]
    one = [(0, 0, 256, 0), (0, 256, 256, 1), (0, 512, 256, 2)]

    def layout_of(units, group, begin, end, base=0):
        return [(base + i, first, rows, 1, group, order, begin, end) for i, first, rows, order in units]

    def hosted(arrays, units, begin, end, when):
        summer = Summer(arrays, layout_of(units, 0, begin, end))
        return summer, [when[min(i, len(when) - 1)] for i in range(summer.slots)]

    def channel(part, kept, hosts, collective_id, shift=None):
        low, size = spans[part]
        first, last = part == 0, part == len(spans) - 1
        ins = [
            tile_rows(second), ahead, rows_of(second_row), tile_rows(objective_adjoint), tile_rows(cols), table(vectors),
            (dense_address_transform, "any", None), (dense_content_transform, "any", None),
        ]
        ins += [table(dense_respond_transform)] if first or last else []
        ins += [tile_rows(a) for a in kept]
        ins += [tile_rows(attended)] if last else []
        if last:
            outs = [tile_out(bf16), tile_out(f32), sum_out(*one_row), sum_out(width, width), sum_out(2, width)]
        else:
            outs = [tile_out(f32)] * (3 if first else 2)
        return call(
            functools.partial(channel_kernel, low, size, first, last, shift),
            (batches, tiles),
            ins,
            outs + [sum_out(width, size), sum_out(size, width)],
            "channel_%d" % part,
            scratch=[
                pltpu.VMEM((BLOCK, 8), f32), pltpu.VMEM((width, size), bf16), pltpu.VMEM((size, width), bf16),
                pltpu.SemaphoreType.DMA((2,)), pltpu.VMEM((1, width), f32),
            ],
            flops=7 * 2 * batches * length * width * (2 * size + (width if last else 0)),
            hosts=hosts,
            collective_id=collective_id,
        )

    steps = batches * tiles
    shift = RowShift(one_row, 1, second_row)
    gate, total, d_inner, *part_a, second_row = channel(0, [], [(shift, [1])], 8, shift)
    total, d_inner, *rest = channel(1, [gate, total, d_inner], [hosted(part_a, even, 0, 4, [1, 3, 4])], 6)
    part_b, part_a = rest[:2], rest[2:]
    block, d_second, _, grad_filter, channel_vectors, *rest = channel(
        2,
        [gate, total, d_inner],
        [hosted(part_b, even, 0, 3, [1, 3, 4]), hosted(part_a, even, 4, depth + 2, [2, 3, 4]), (RowShift(one_row, -1, which=2), [steps] * 2)],
        7,
    )
    part_c, part_b, part_a, back_second = [rest[0], rest[1], grad_filter], rest[2:4], rest[4:6], rest[6]
    d_attended, d_wkv, d_valve, gated, carry, attention_vectors, *rest = call(
        attention_back_kernel,
        (batches, tiles),
        [
            tiled(d_second), rows_of(back_second), tiled(attended), tiled(objective_adjoint), tiled(wkv),
            tiled(valve), tiled(recept), tiled(cols), table(vectors), table(readout_transform),
        ],
        [tiled_out] * 4 + [rows_out(states), sum_out(4, width)],
        "attention_back",
        flops=2 * square_flops,
        hosts=[
            hosted(part_c, rest_units, 0, 1, [3]),
            hosted(part_b, even, 3, depth + 1, [1, 4]),
            hosted(part_a, even, depth + 2, ends - 1, [2, 4]),
        ],
        collective_id=3,
    )
    part_c, part_b, part_a = rest[:3], rest[3:5], rest[5:7]
    steps = batches * pairs
    arriving = Carrier([carry], lengths, vectors, length, -1)
    d_recept, d_keys, d_values, mix_vectors, grad_output, out_state, *rest = call(
        mix_back_kernel,
        (batches, pairs),
        [
            by_pair(recept), by_pair(keys), by_pair(values), by_pair(d_wkv), pair_state(state), rows_of(cols), rows_of(row),
            pair_vectors, by_pair(gated), rows_of(d_attended),
        ],
        [pair_out] * 3 + [((batches, 2, width), f32, (1, 2, PAIR), lambda b, p: (b, 0, p)), sum_out(width, width)],
        "mix_back",
        flops=9 * 2 * batches * length * length * width * 2,
        hosts=[
            (arriving, [(i + 1) * steps // arriving.slots for i in range(arriving.slots)]),
            hosted(part_b, even, depth + 1, ends - 1, [2, 5, 9]),
            hosted(part_c, rest_units, 1, depth, [5, 8, 10, 12]),
            hosted(part_a, even, ends - 1, ends, [6]),
        ],
        collective_id=4,
    )
    part_b, part_c, part_a = rest[:2], rest[2:5], rest[5:7]
    steps = 4 * batches
    wide = lambda: pltpu.VMEM((length, width), f32)
    grad_recept, grad_keys, grad_values, grad_gate_w, d_keys, d_values, decay_vector, *rest = call(
        weights_back_kernel,
        (batches, 4),
        common
        + [
            rows_of(d_recept), rows_of(d_keys), rows_of(d_values), rows_of(d_valve), rows_of(keys), rows_of(values),
            rows_of(state), rows_of(out_state),
        ],
        [sum_out(width, width)] * 4 + [rows_out(tokens)] * 2 + [sum_out(1, width)],
        "weights_back",
        scratch=[wide(), wide()],
        flops=3 * 4 * square_flops,
        hosts=[
            hosted([grad_output], one, 0, depth, [1, 3, 4, 6, 8]),
            hosted(part_c, rest_units, depth, ends - 1, [3, 4, 6, 8]),
            hosted(part_b, even, ends - 1, ends, [8]),
        ],
        collective_id=5,
    )
    grad_output, part_c, part_b = rest[0], rest[1:4], rest[4:6]
    layout, part = [], width // 6
    for half in range(2):
        low = half * width // 2
        layout += layout_of([(i, low, width // 2, (i + half) % 3) for i in range(3)], half, 0, ends, 4)
        layout += layout_of([(3, low + i * part, part, i) for i in range(3)], half, 0, ends, 4)
    layout += layout_of(rest_units, 2, ends - 1, ends) + layout_of(one, 2, depth, ends, 3)
    summer = Summer(part_c + [grad_output, grad_recept, grad_keys, grad_values, grad_gate_w], layout)
    d_x, _, _, *rest = call(
        inputs_back_kernel,
        (batches, 4),
        common
        + [
            rows_of(d_attended), rows_of(d_recept), rows_of(d_keys), rows_of(d_values), rows_of(d_valve),
            rows_of(mix_vectors), table(attention_vectors), table(channel_vectors), table(decay_vector),
        ]
        + [table(w) for w in (respond_transform, address_transform, content_transform, valve_transform)],
        [rows_out(tokens), sum_out(*one_row), sum_out(*vectors.shape)],
        "inputs_back",
        scratch=[wide(), wide(), wide()],
        flops=2 * 4 * square_flops,
        hosts=[
            (summer, [3, 6, 8] + [steps] * (summer.slots - 3)),
            (VectorSum(2, 1, vectors.shape, one_row), [steps] * (depth + 1)),
        ],
        collective_id=0,
    )
    summed, vectors, last_row = rest[:8], rest[8], rest[9]
    w_expand, w_shrink, w_filter, w_output, w_recept, w_keys, w_values, w_gate, grad_tokens, *vectors = gathered(
        part_a + part_b + list(summed), spans, hidden_width, d_x, last_row, vectors, MIX_F + 1
    )
    return (
        block, grad_tokens, *[vectors[i] for i in range(6)], w_recept, w_keys, w_values, w_gate,
        vectors[6], vectors[7], vectors[8], vectors[9], w_output, vectors[10], vectors[11], vectors[12], vectors[13],
        w_expand, w_shrink, w_filter,
    )


def solution(mesh):
    rows = P(None, "seq", None)
    return jax.shard_map(
        local,
        mesh=mesh,
        in_specs=(rows,) + (P(),) * 23 + (rows,),
        out_specs=(rows, rows) + (P(),) * 22,
        check_vma=False,
    )
```

```python
import functools

import jax
import jax.numpy as jnp
from jax import lax
from jax.experimental import pallas as pl
from jax.experimental.pallas import tpu as pltpu
from jax.sharding import PartitionSpec as P

LANE_FEATURES = 64
PAIR = 2 * LANE_FEATURES
BLOCK = 256
f32 = jnp.float32
bf16 = jnp.bfloat16
VMEM_LIMIT = 60 * 1024 * 1024
MESH = pl.DeviceIdType.MESH


def nothing():
    pass


def split(x):
    high = x.astype(bf16)
    return high, (x - high.astype(f32)).astype(bf16)


def dot(a, b):
    return lax.dot_general(a, b, (((1,), (0,)), ((), ())), preferred_element_type=f32)


def dot_nt(a, b):
    return lax.dot_general(a, b, (((1,), (1,)), ((), ())), preferred_element_type=f32)


def dot_tn(a, b):
    return lax.dot_general(a, b, (((0,), (0,)), ((), ())), preferred_element_type=f32)


def times_weight(x, w):
    high, low = split(x)
    return dot(high, w) + dot(low, w)


def times_weight_t(x, w):
    high, low = split(x)
    return dot_nt(high, w) + dot_nt(low, w)


def outer_sum(a, b):
    return thrice(*split(a), *split(b))


def thrice(ah, al, bh, bl):
    return dot_tn(jnp.concatenate([ah, al, ah], axis=0), jnp.concatenate([bh, bh, bl], axis=0))


def both(high, low, w):
    out = dot(jnp.concatenate([high, low], axis=0), w)
    return out[: high.shape[0]] + out[high.shape[0] :]


def standard(x, epsilon=1e-05):
    centred = x - jnp.mean(x, axis=-1, keepdims=True)
    scale = lax.rsqrt(jnp.mean(centred * centred, axis=-1, keepdims=True) + epsilon)
    return centred * scale, scale


def standard_back(grad, normal, scale):
    return scale * (
        grad
        - jnp.mean(grad, axis=-1, keepdims=True)
        - normal * jnp.mean(grad * normal, axis=-1, keepdims=True)
    )


def first_lanes(rows):
    return lax.broadcasted_iota(jnp.int32, (rows, PAIR), 1) < LANE_FEATURES


def head_ones(scale):
    row = lax.broadcasted_iota(jnp.int32, (2 * PAIR, PAIR), 0) // LANE_FEATURES % 2
    col = lax.broadcasted_iota(jnp.int32, (2 * PAIR, PAIR), 1) // LANE_FEATURES
    return jnp.where(row == col, scale, 0.0).astype(bf16)


def head_sum(x, ones):
    return dot(jnp.concatenate(split(x), axis=1), ones)


def widen(state):
    first = first_lanes(LANE_FEATURES)
    return jnp.concatenate([jnp.where(first, state, 0.0), jnp.where(first, 0.0, state)], axis=0)


def compact(square):
    first = first_lanes(LANE_FEATURES)
    return jnp.where(first, square[:LANE_FEATURES], square[LANE_FEATURES:])


def times_state(x, square):
    xh, xl = split(x)
    sh, sl = split(square)
    return dot(jnp.concatenate([xh, xl], axis=1), jnp.concatenate([sh, sh], axis=0)) + dot(xh, sl)


def times_state_t(x, square):
    xh, xl = split(x)
    sh, sl = split(square)
    return dot_nt(jnp.concatenate([xh, xl], axis=1), jnp.concatenate([sh, sh], axis=1)) + dot_nt(xh, sl)


def cut(x):
    high = x.astype(bf16).astype(f32)
    low = x - high
    return high, low, pltpu.roll(high, LANE_FEATURES, 1), pltpu.roll(low, LANE_FEATURES, 1)


def high_low(pieces, first, head):
    high, low, high_r, low_r = pieces
    return (jnp.where(first, high, low_r) if head == 0 else jnp.where(first, high_r, low)).astype(bf16)


def doubled(pieces, first, head):
    high, low, high_r, low_r = pieces
    if head == 0:
        both = (jnp.where(first, high, high_r), jnp.where(first, low, low_r))
    else:
        both = (jnp.where(first, high_r, high), jnp.where(first, low_r, low))
    return jnp.concatenate([part.astype(bf16) for part in both], axis=1)


def twice(x):
    return jnp.concatenate([x, x], axis=1)


def folded(parts, first):
    sums = [part + pltpu.roll(part, LANE_FEATURES, 1) for part in parts]
    return jnp.where(first, sums[0], sums[1])


def decays(log_decay):
    step = lax.broadcasted_iota(jnp.int32, (BLOCK, PAIR), 0).astype(f32)
    return step, jnp.exp(log_decay * step), jnp.exp(-log_decay * (step + 1.0)), jnp.exp(log_decay * BLOCK)


def shifted(normal, row_before, keep):
    rows = lax.broadcasted_iota(jnp.int32, normal.shape, 0)
    return jnp.where(rows == 0, row_before, pltpu.roll(normal, 1, 0)) * keep


GAIN, BIAS, MIX_R, MIX_K, MIX_V, MIX_G, DECAY, BOOST, GROUP_GAIN, GROUP_SHIFT, GAIN2, BIAS2, MIX_E, MIX_F = range(14)


def vec(ref, which, lanes=slice(None)):
    return ref[which : which + 1, lanes]


def bounds_of(lengths_ref, batch):
    at, bounds = jnp.int32(0), []
    for j in range(lengths_ref.shape[1]):
        bounds.append(at)
        at = at + lengths_ref[batch, j]
    return bounds


def segment_of(bounds, position):
    return sum([(position >= bound).astype(jnp.int32) for bound in bounds])


def tokens_kernel(lengths_ref, *refs):
    *vector_refs, cols_ref, row_ref, packed_ref = refs
    for i, ref in enumerate(vector_refs):
        value = ref[...].reshape(1, ref.shape[0])
        packed_ref[i : i + 1] = -jnp.exp(value) if i == DECAY else value
    packed_ref[len(vector_refs) :] = jnp.zeros((2, packed_ref.shape[1]), f32)
    batches, length, columns = cols_ref.shape
    offset = lax.axis_index("seq") * length
    for batch in range(batches):
        bounds = bounds_of(lengths_ref, batch)
        place = offset + lax.broadcasted_iota(jnp.int32, (length, columns), 0)
        segment = segment_of(bounds, place)
        starts = functools.reduce(jnp.logical_or, [place == bound for bound in bounds])
        column = lax.broadcasted_iota(jnp.int32, (length, columns), 1)
        fresh = segment == segment_of(bounds, offset - 1)
        last = segment == segment_of(bounds, offset + length - 1)
        flag = jnp.where(column == 1, jnp.where(starts, 0, 1), jnp.where(column == 2, jnp.where(fresh, 1, 0), jnp.where(last, 1, 0)))
        cols_ref[batch] = jnp.where(column == 0, segment, flag).astype(f32)
        row_ref[batch] = segment_of(bounds, offset + lax.broadcasted_iota(jnp.int32, (1, length), 1)).astype(f32)


def project_kernel(mixes, states, x_ref, before_ref, cols_ref, vec_ref, *refs):
    count = len(mixes)
    weights, outs = refs[:count], refs[count : 2 * count]
    gain, bias = vec(vec_ref, GAIN), vec(vec_ref, BIAS)
    normal = standard(x_ref[0].astype(f32))[0] * gain + bias
    before = standard(before_ref[0])[0] * gain + bias
    earlier = shifted(normal, before, cols_ref[0, :, 1:2])
    difference = normal - earlier
    for mix, weight, out in zip(mixes, weights, outs):
        out[0] = times_weight(earlier + vec(vec_ref, mix) * difference, weight[...])
    if states:
        length, width = normal.shape
        keys, values, end_ref = outs[0], outs[1], refs[2 * count]
        rows = lax.broadcasted_iota(jnp.int32, (length, PAIR), 0).astype(f32)
        for pair in range(width // PAIR):
            lanes = slice(pair * PAIR, (pair + 1) * PAIR)
            tail = jnp.exp(vec(vec_ref, DECAY, lanes) * (length - 1.0 - rows)) * cols_ref[0, :, 3:4]
            end_ref[0, pair] = compact(outer_sum(keys[0, :, lanes] * tail, values[0, :, lanes]))


def allowed_here(cols_ref, row_ref, at, of, across):
    t_col = cols_ref[0, pl.ds(at * BLOCK, BLOCK), 0:1]
    s_row = row_ref[0, :, pl.ds(of * BLOCK, BLOCK)]
    mask = t_col == s_row
    if at == of:
        shape = (BLOCK, BLOCK)
        low, high = (1, 0) if not across else (0, 1)
        mask = jnp.logical_and(
            mask,
            lax.broadcasted_iota(jnp.int32, shape, low) < lax.broadcasted_iota(jnp.int32, shape, high),
        )
    return mask


def mix_kernel(recept_ref, keys_ref, values_ref, cols_ref, row_ref, vec_ref, out_ref):
    length = recept_ref.shape[1]
    log_decay, boost = vec(vec_ref, DECAY), vec(vec_ref, BOOST)
    first = first_lanes(BLOCK)
    step, fall, rise, whole = decays(log_decay)
    ones = head_ones(1.0)
    queries, near, far, values = [], [], [], []
    for at in range(length // BLOCK):
        here = pl.ds(at * BLOCK, BLOCK)
        queries.append(cut(recept_ref[0, here] * fall))
        raised = keys_ref[0, here] * rise
        near.append(cut(raised))
        far.append(raised * whole)
        values.append(cut(values_ref[0, here]))
    for at in range(length // BLOCK):
        here = pl.ds(at * BLOCK, BLOCK)
        totals = [jnp.zeros((BLOCK, PAIR), f32)] * 2
        for of in range(at + 1):
            mask = allowed_here(cols_ref, row_ref, at, of, False)
            gap = jnp.exp(log_decay * (BLOCK * (at - of - 1))) if at > of + 1 else None
            keys = near[of] if of == at else cut(far[of] if gap is None else far[of] * gap)
            for head in range(2):
                scores = dot_nt(twice(high_low(queries[at], first, head)), doubled(keys, first, head))
                sh, sl = split(jnp.where(mask, scores, 0.0))
                held = high_low(values[of], first, head)
                totals[head] = totals[head] + both(sh, sl, held)
        present = head_sum(recept_ref[0, here] * boost * keys_ref[0, here], ones)
        out_ref[0, here] = folded(totals, first) + present * values_ref[0, here]


def readout_kernel(
    mixed_ref, recept_ref, state_ref, valve_ref, cols_ref, vec_ref, x_ref, weight_ref,
    wkv_ref, attended_ref, second_ref, last_ref,
):
    length, width = mixed_ref.shape[1:]
    rows = (pl.program_id(1) * length + lax.broadcasted_iota(jnp.int32, (length, PAIR), 0)).astype(f32)
    ones = head_ones(1.0 / LANE_FEATURES)
    fresh = cols_ref[0, :, 2:3]
    gated = []
    for pair in range(width // PAIR):
        lanes = slice(pair * PAIR, (pair + 1) * PAIR)
        query = recept_ref[0, :, lanes] * jnp.exp(vec(vec_ref, DECAY, lanes) * rows) * fresh
        wkv = mixed_ref[0, :, lanes] + times_state(query, widen(state_ref[0, pair]))
        wkv_ref[0, :, lanes] = wkv
        centred = wkv - head_sum(wkv, ones)
        normal = centred * lax.rsqrt(head_sum(centred * centred, ones) + 0.00064)
        grouped = normal * vec(vec_ref, GROUP_GAIN, lanes) + vec(vec_ref, GROUP_SHIFT, lanes)
        gated.append(grouped * jax.nn.silu(valve_ref[0, :, lanes]))
    attended = x_ref[0].astype(f32) + times_weight(jnp.concatenate(gated, axis=1), weight_ref[...])
    attended_ref[0] = attended
    second = standard(attended)[0] * vec(vec_ref, GAIN2) + vec(vec_ref, BIAS2)
    second_ref[0] = second
    last_ref[0] = second[length - 1 :]


def pieces_of(total):
    cuts, at = [], 0
    while at < total:
        size = min(1024, total - at)
        cuts.append((at, size))
        at += size
    return cuts


def channel_kernel(low, size, first, last, shift, *refs):
    refs = list(refs)
    take = lambda count: [refs.pop(0) for _ in range(count)]
    second_ref, ahead_ref, received_ref, grad_ref, cols_ref, vec_ref, expand_any, shrink_any = take(8)
    filter_ref = take(1)[0] if first or last else None
    gate_ref = None if first else take(1)[0]
    total_in, inner_in = (None, None) if first else take(2)
    attended_ref = take(1)[0] if last else None
    gate_out = take(1)[0] if first else None
    if last:
        block_ref, d_second_ref, d_row_ref, d_filter_ref, d_vec_ref = take(5)
    else:
        total_out, inner_out = take(2)
    d_expand_ref, d_shrink_ref, hidden_ref, expand_ref, shrink_ref, sems, carry_ref = refs
    tiles = pl.num_programs(1)
    batch, turn = pl.program_id(0), pl.program_id(1)
    tile = tiles - 1 - turn
    start = jnp.logical_and(batch == 0, turn == 0)

    @pl.when(start)
    def _():
        loads = [
            pltpu.make_async_copy(expand_any.at[:, pl.ds(low, size)], expand_ref, sems.at[0]),
            pltpu.make_async_copy(shrink_any.at[pl.ds(low, size)], shrink_ref, sems.at[1]),
        ]
        for load in loads:
            load.start()
        for ref in [d_expand_ref, d_shrink_ref] + ([d_filter_ref, d_vec_ref] if last else []):
            ref[...] = jnp.zeros_like(ref)
        for load in loads:
            load.wait()

    keep = cols_ref[0, :, 1:2]
    second = second_ref[0]
    received = received_ref[0] if shift is None else shift.out_ref[pl.ds(batch, 1)][0]
    before = jnp.where(tile == 0, received, ahead_ref[0, 7:8])
    earlier = shifted(second, before, keep)
    difference = second - earlier
    mix_e, mix_f = vec(vec_ref, MIX_E), vec(vec_ref, MIX_F)
    inner_h, inner_l = split(earlier + mix_e * difference)
    if first or last:
        side_h, side_l = split(earlier + mix_f * difference)
    if first:
        gate = jax.nn.sigmoid(dot(side_h, filter_ref[...]) + dot(side_l, filter_ref[...]))
        gate_out[0] = gate
    else:
        gate = gate_ref[0]
    grad = grad_ref[0].astype(f32)
    dt_h, dt_l = split(grad * gate)
    total = jnp.zeros(second.shape, f32) if first else total_in[0]
    d_inner = jnp.zeros(second.shape, f32) if first else inner_in[0]
    for at, wide in pieces_of(size):
        lanes = slice(at, at + wide)
        raw = jnp.maximum(dot(inner_h, expand_ref[:, lanes]) + dot(inner_l, expand_ref[:, lanes]), 0.0)
        hid_h, hid_l = split(raw * raw)
        total = total + dot(hid_h, shrink_ref[lanes, :]) + dot(hid_l, shrink_ref[lanes, :])
        d_hidden = dot_nt(dt_h, shrink_ref[lanes, :]) + dot_nt(dt_l, shrink_ref[lanes, :])
        dr_h, dr_l = split(d_hidden * (2.0 * raw))
        d_shrink_ref[lanes, :] += thrice(hid_h, hid_l, dt_h, dt_l)
        d_expand_ref[:, lanes] += thrice(inner_h, inner_l, dr_h, dr_l)
        d_inner = d_inner + dot_nt(dr_h, expand_ref[:, lanes]) + dot_nt(dr_l, expand_ref[:, lanes])
    if not last:
        total_out[0] = total
        inner_out[0] = d_inner
        return
    block_ref[0] = (attended_ref[0] + gate * total).astype(bf16)
    ds_h, ds_l = split(grad * total * (gate * (1.0 - gate)))
    d_filter_ref[...] += thrice(side_h, side_l, ds_h, ds_l)
    d_side = dot_nt(ds_h, filter_ref[...]) + dot_nt(ds_l, filter_ref[...])
    d_vec_ref[0:1] += jnp.sum(d_inner * difference, axis=0, keepdims=True)
    d_vec_ref[1:2] += jnp.sum(d_side * difference, axis=0, keepdims=True)
    direct = mix_e * d_inner + mix_f * d_side
    passed = (d_inner + d_side - direct) * keep
    rows = lax.broadcasted_iota(jnp.int32, second.shape, 0)
    above = pltpu.roll(passed, second.shape[0] - 1, 0)
    outside = jnp.where(turn == 0, 0.0, carry_ref[...])
    d_second_ref[0] = direct + jnp.where(rows == second.shape[0] - 1, outside, above)
    carry_ref[...] = passed[0:1]
    d_row_ref[pl.ds(batch, 1)] = passed[0:1][None]


def attention_back_kernel(
    d_second_ref, back_ref, attended_ref, grad_ref, wkv_ref, valve_ref, recept_ref, cols_ref, vec_ref, weight_ref,
    d_attended_ref, d_wkv_ref, d_valve_ref, carry_ref, d_weight_ref, d_vec_ref,
):
    length, width = attended_ref.shape[1:]

    tile, is_last = pl.program_id(1), pl.program_id(1) == pl.num_programs(1) - 1

    @pl.when(jnp.logical_and(pl.program_id(0) == 0, tile == 0))
    def _():
        d_vec_ref[...] = jnp.zeros_like(d_vec_ref)
        d_weight_ref[...] = jnp.zeros_like(d_weight_ref)

    rows = lax.broadcasted_iota(jnp.int32, (length, width), 0)
    d_second = d_second_ref[0] + jnp.where(jnp.logical_and(rows == length - 1, is_last), back_ref[0], 0.0)
    normal2, scale2 = standard(attended_ref[0])
    d_vec_ref[2:3] += jnp.sum(d_second * normal2, axis=0, keepdims=True)
    d_vec_ref[3:4] += jnp.sum(d_second, axis=0, keepdims=True)
    d_attended = grad_ref[0].astype(f32) + standard_back(d_second * vec(vec_ref, GAIN2), normal2, scale2)
    d_attended_ref[0] = d_attended
    d_gated = times_weight_t(d_attended, weight_ref[...])
    steps = (tile * length + lax.broadcasted_iota(jnp.int32, (length, PAIR), 0)).astype(f32)
    ones = head_ones(1.0 / LANE_FEATURES)
    fresh = cols_ref[0, :, 2:3]
    gated = []
    for pair in range(width // PAIR):
        lanes = slice(pair * PAIR, (pair + 1) * PAIR)
        wkv = wkv_ref[0, :, lanes]
        centred = wkv - head_sum(wkv, ones)
        scale = lax.rsqrt(head_sum(centred * centred, ones) + 0.00064)
        normal = centred * scale
        grouped = normal * vec(vec_ref, GROUP_GAIN, lanes) + vec(vec_ref, GROUP_SHIFT, lanes)
        valve = valve_ref[0, :, lanes]
        sigmoid = jax.nn.sigmoid(valve)
        gate = valve * sigmoid
        gated.append(grouped * gate)
        d_here = d_gated[:, lanes]
        d_valve_ref[0, :, lanes] = d_here * grouped * (sigmoid * (1.0 + valve * (1.0 - sigmoid)))
        d_grouped = d_here * gate
        d_vec_ref[0:1, lanes] += jnp.sum(d_grouped * normal, axis=0, keepdims=True)
        d_vec_ref[1:2, lanes] += jnp.sum(d_grouped, axis=0, keepdims=True)
        d_normal = d_grouped * vec(vec_ref, GROUP_GAIN, lanes)
        d_wkv = scale * (d_normal - head_sum(d_normal, ones) - normal * head_sum(d_normal * normal, ones))
        d_wkv_ref[0, :, lanes] = d_wkv
        query = recept_ref[0, :, lanes] * jnp.exp(vec(vec_ref, DECAY, lanes) * steps) * fresh
        carried = compact(outer_sum(query, d_wkv))
        carry_ref[0, pair] = jnp.where(tile == 0, carried, carry_ref[0, pair] + carried)
    d_weight_ref[...] += outer_sum(jnp.concatenate(gated, axis=1), d_attended)


def mix_back_kernel(
    recept_ref, keys_ref, values_ref, grad_ref, state_ref, cols_ref, row_ref, vec_ref,
    d_recept_ref, d_keys_ref, d_values_ref, d_vec_ref,
):
    length = recept_ref.shape[1]
    blocks = length // BLOCK
    first = first_lanes(BLOCK)
    log_decay, boost = vec(vec_ref, DECAY), vec(vec_ref, BOOST)
    step, fall, rise, whole = decays(log_decay)
    ones = head_ones(1.0)
    square = widen(state_ref[0, 0])
    queries, near, far, values, grads = [], [], [], [], []
    for at in range(blocks):
        here = pl.ds(at * BLOCK, BLOCK)
        queries.append(cut(recept_ref[0, here] * fall))
        raised = keys_ref[0, here] * rise
        near.append(cut(raised))
        far.append(raised * whole)
        values.append(cut(values_ref[0, here]))
        grads.append(cut(grad_ref[0, here]))
    zero = jnp.zeros((BLOCK, PAIR), f32)
    d_query = [[zero, zero] for _ in range(blocks)]
    d_value = [[zero, zero] for _ in range(blocks)]
    d_near = [[zero, zero] for _ in range(blocks)]
    d_far = [[zero, zero] for _ in range(blocks)]
    for at in range(blocks):
        for of in range(at + 1):
            mask = allowed_here(cols_ref, row_ref, at, of, False)
            t_row = row_ref[0, :, pl.ds(at * BLOCK, BLOCK)]
            s_col = cols_ref[0, pl.ds(of * BLOCK, BLOCK), 0:1]
            mask_t = s_col == t_row
            if at == of:
                shape = (BLOCK, BLOCK)
                mask_t = jnp.logical_and(
                    mask_t, lax.broadcasted_iota(jnp.int32, shape, 0) < lax.broadcasted_iota(jnp.int32, shape, 1)
                )
            gap = jnp.exp(log_decay * (BLOCK * (at - of - 1))) if at > of + 1 else None
            keys = near[of] if of == at else cut(far[of] if gap is None else far[of] * gap)
            mask, mask_t = jnp.where(mask, 1.0, 0.0), jnp.where(mask_t, 1.0, 0.0)
            for head in range(2):
                q_hl = high_low(queries[at], first, head)
                g_hl = high_low(grads[at], first, head)
                k_hl = high_low(keys, first, head)
                v_hl = high_low(values[of], first, head)
                scores_t = dot_nt(twice(k_hl), doubled(queries[at], first, head))
                s_h, s_l = split(scores_t * mask_t)
                d_value[of][head] = d_value[of][head] + both(s_h, s_l, g_hl)
                d_scores = dot_nt(twice(g_hl), doubled(values[of], first, head))
                s_h, s_l = split(d_scores * mask)
                d_query[at][head] = d_query[at][head] + both(s_h, s_l, k_hl)
                d_scores_t = dot_nt(twice(v_hl), doubled(grads[at], first, head))
                s_h, s_l = split(d_scores_t * mask_t)
                d_key = both(s_h, s_l, q_hl)
                if of == at:
                    d_near[of][head] = d_key
                else:
                    if gap is not None:
                        d_key = d_key * gap
                    d_far[of][head] = d_far[of][head] + d_key
    d_decay = jnp.zeros((1, PAIR), f32)
    d_boost = jnp.zeros((1, PAIR), f32)
    for at in range(blocks):
        here = pl.ds(at * BLOCK, BLOCK)
        recept, keys, value, grad = recept_ref[0, here], keys_ref[0, here], values_ref[0, here], grad_ref[0, here]
        fresh = cols_ref[0, here, 2:3]
        d_in = folded(d_query[at], first) * fall
        d_state = times_state_t(grad, square) * (fall * jnp.exp(log_decay * (BLOCK * at)) * fresh)
        d_here = folded(d_near[at], first) * rise
        d_later = folded(d_far[at], first) * (rise * whole)
        present = head_sum(recept * boost * keys, ones)
        d_present = head_sum(grad * value, ones)
        d_recept_ref[0, here] = d_in + d_state + boost * keys * d_present
        d_keys_ref[0, here] = d_here + d_later + boost * recept * d_present
        d_values_ref[0, here] = folded(d_value[at], first) + present * grad
        d_boost = d_boost + jnp.sum(recept * keys * d_present, axis=0, keepdims=True)
        d_decay = d_decay + jnp.sum(
            recept * (step * d_in + (step + float(BLOCK * at)) * d_state)
            + keys * ((BLOCK - 1.0 - step) * d_later - (step + 1.0) * d_here),
            axis=0,
            keepdims=True,
        )
    d_vec_ref[0, 0:1] = d_decay
    d_vec_ref[0, 1:2] = d_boost


def weights_back_kernel(
    x_ref, before_ref, cols_ref, vec_ref,
    d_recept_ref, d_keys_ref, d_values_ref, d_valve_ref, keys_ref, values_ref, state_ref, out_state_ref,
    dw_r, dw_k, dw_v, dw_g, d_keys_out, d_values_out, d_decay_ref, earlier_ref, difference_ref,
):
    length, width = x_ref.shape[1:]
    turn = pl.program_id(1)
    steps = lax.broadcasted_iota(jnp.int32, (length, PAIR), 0).astype(f32)
    pairs = [(pair, slice(pair * PAIR, (pair + 1) * PAIR)) for pair in range(width // PAIR)]

    @pl.when(jnp.logical_and(pl.program_id(0) == 0, turn == 0))
    def _():
        for ref in (dw_r, dw_k, dw_v, dw_g, d_decay_ref):
            ref[...] = jnp.zeros_like(ref)

    def tail_of(lanes):
        return jnp.exp(vec(vec_ref, DECAY, lanes) * (length - 1.0 - steps)) * cols_ref[0, :, 3:4]

    def weigh(which, grad, d_weight):
        d_weight[...] += outer_sum(earlier_ref[...] + vec(vec_ref, which) * difference_ref[...], grad)

    @pl.when(turn == 0)
    def _():
        gain, bias = vec(vec_ref, GAIN), vec(vec_ref, BIAS)
        normal = standard(x_ref[0].astype(f32))[0] * gain + bias
        before = standard(before_ref[0])[0] * gain + bias
        earlier = shifted(normal, before, cols_ref[0, :, 1:2])
        earlier_ref[...] = earlier
        difference_ref[...] = normal - earlier
        weigh(MIX_G, d_valve_ref[0], dw_g)

    @pl.when(turn == 1)
    def _():
        weigh(MIX_R, d_recept_ref[0], dw_r)

    @pl.when(turn == 2)
    def _():
        for pair, lanes in pairs:
            d_keys = times_state_t(values_ref[0, :, lanes], widen(out_state_ref[0, pair])) * tail_of(lanes)
            later = (length - 1.0 - steps) * keys_ref[0, :, lanes] * d_keys
            square = widen(state_ref[0, pair]) * widen(out_state_ref[0, pair])
            ones = jnp.ones((8, PAIR), bf16)
            kept = sum([dot_nt(ones, part)[0:1] for part in split(square)])
            kept = kept * jnp.exp(vec(vec_ref, DECAY, lanes) * length) * (float(length) * cols_ref[0, length - 1 :, 2:3])
            d_decay_ref[:, lanes] += jnp.sum(later, axis=0, keepdims=True) + kept
            d_keys_out[0, :, lanes] = d_keys_ref[0, :, lanes] + d_keys
        weigh(MIX_K, d_keys_out[0], dw_k)

    @pl.when(turn == 3)
    def _():
        for pair, lanes in pairs:
            ended = times_state(keys_ref[0, :, lanes] * tail_of(lanes), widen(out_state_ref[0, pair]))
            d_values_out[0, :, lanes] = d_values_ref[0, :, lanes] + ended
        weigh(MIX_V, d_values_out[0], dw_v)


def inputs_back_kernel(
    x_ref, before_ref, cols_ref, vec_ref, d_attended_ref, d_recept_ref, d_keys_ref, d_values_ref, d_valve_ref,
    mix_vec_ref, attention_vec_ref, channel_vec_ref, d_decay_ref, w_r, w_k, w_v, w_g,
    d_x_ref, d_row_ref, packed_ref, difference_ref, direct_ref, passed_ref,
):
    length, width = x_ref.shape[1:]
    batch, turn = pl.program_id(0), pl.program_id(1)
    gain, bias = vec(vec_ref, GAIN), vec(vec_ref, BIAS)

    @pl.when(jnp.logical_and(batch == 0, turn == 0))
    def _():
        packed_ref[...] = jnp.zeros_like(packed_ref)
        packed_ref[GROUP_GAIN : BIAS2 + 1] = attention_vec_ref[...]
        packed_ref[MIX_E : MIX_F + 1] = channel_vec_ref[...]
        packed_ref[DECAY : DECAY + 1] = d_decay_ref[...]

    def through(grad, which, weight, first=False):
        mix = vec(vec_ref, which)
        d_mixed = times_weight_t(grad, weight[...])
        packed_ref[which : which + 1] += jnp.sum(d_mixed * difference_ref[...], axis=0, keepdims=True)
        direct, passed = mix * d_mixed, d_mixed - mix * d_mixed
        direct_ref[...] = direct if first else direct_ref[...] + direct
        passed_ref[...] = passed if first else passed_ref[...] + passed

    @pl.when(turn == 0)
    def _():
        normal = standard(x_ref[0].astype(f32))[0] * gain + bias
        before = standard(before_ref[0])[0] * gain + bias
        difference_ref[...] = normal - shifted(normal, before, cols_ref[0, :, 1:2])
        packed_ref[DECAY : BOOST + 1] += mix_vec_ref[0]
        through(d_recept_ref[0], MIX_R, w_r, True)

    @pl.when(turn == 1)
    def _():
        through(d_valve_ref[0], MIX_G, w_g)

    @pl.when(turn == 2)
    def _():
        through(d_keys_ref[0], MIX_K, w_k)

    @pl.when(turn == 3)
    def _():
        through(d_values_ref[0], MIX_V, w_v)
        passed = passed_ref[...] * cols_ref[0, :, 1:2]
        rows = lax.broadcasted_iota(jnp.int32, (length, width), 0)
        d_normal = direct_ref[...] + jnp.where(rows == length - 1, 0.0, pltpu.roll(passed, length - 1, 0))
        hat, scale = standard(x_ref[0].astype(f32))
        hat_before, scale_before = standard(before_ref[0])
        out = passed[0:1]
        packed_ref[GAIN : GAIN + 1] += jnp.sum(d_normal * hat, axis=0, keepdims=True) + out * hat_before
        packed_ref[BIAS : BIAS + 1] += jnp.sum(d_normal, axis=0, keepdims=True) + out
        d_x_ref[0] = d_attended_ref[0] + standard_back(d_normal * gain, hat, scale)
        d_row_ref[pl.ds(batch, 1)] = standard_back(out * gain, hat_before, scale_before)[None]

        @pl.when(batch == pl.num_programs(0) - 1)
        def _():
            packed_ref[DECAY : DECAY + 1] = packed_ref[DECAY : DECAY + 1] * vec(vec_ref, DECAY)


def call(kernel, grid, ins, outs, name, scratch=(), flops=0, hosts=(), collective_id=None, ticks=1):
    bytes_accessed = sum(a.size * a.dtype.itemsize for a, _, _ in ins)
    for shape, dtype, _, _ in outs:
        size = jnp.dtype(dtype).itemsize
        for extent in shape:
            size *= extent
        bytes_accessed += size

    def spec(block, index):
        if block == "smem":
            return pl.BlockSpec(memory_space=pltpu.SMEM)
        if block == "any":
            return pl.BlockSpec(memory_space=pl.ANY)
        if index is None:
            return pl.BlockSpec(block, lambda *_: (0,) * len(block), pipeline_mode=pl.Buffered(1))
        return pl.BlockSpec(block, index)

    ins, outs, scratch = list(ins), list(outs), list(scratch)
    own, places, aliases = (len(ins), len(outs), len(scratch)), [], {}
    for exchange, _ in hosts:
        more_in, more_out, alias = exchange.operands()
        aliases.update({len(ins) + i: len(outs) + j for i, j in alias})
        place = [len(ins), len(outs), len(scratch)]
        ins, outs, scratch = ins + more_in, outs + more_out, scratch + exchange.scratch()
        places.append([slice(a, b) for a, b in zip(place, (len(ins), len(outs), len(scratch)))])
    steps = 1
    for extent in grid:
        steps *= extent

    def body(*refs):
        in_refs, out_refs, scratch_refs = refs[: len(ins)], refs[len(ins) : len(ins) + len(outs)], refs[len(ins) + len(outs) :]
        step = pl.program_id(0)
        for axis in range(1, len(grid)):
            step = step * grid[axis] + pl.program_id(axis)
        for (exchange, _), (i, o, t) in zip(hosts, places):
            exchange.kernel_outs = out_refs[: own[1]]
            exchange.bind(in_refs[i], out_refs[o], scratch_refs[t])

        def enter():
            barrier = pltpu.get_barrier_semaphore()
            partners = [partner for exchange, _ in hosts for partner in exchange.partners()]
            for partner in partners:
                pl.semaphore_signal(barrier, inc=1, device_id=(partner,), device_id_type=MESH)
            pl.semaphore_wait(barrier, len(partners))
            for exchange, _ in hosts:
                exchange.start()

        def advance(turn):
            due = []
            for exchange, ends in hosts:
                slots = [slot for slot in range(exchange.slots) if min(ends[slot], steps * ticks) == turn]
                due += [((slot + 1) / exchange.slots, exchange, slot) for slot in slots]
            due.sort(key=lambda entry: entry[0])
            if due:

                @pl.when(step == min(turn // ticks, steps - 1))
                def _():
                    for _, exchange, slot in due:
                        exchange.run(slot)

        if hosts:
            pl.when(step == 0)(enter)
        for turn in range(steps):
            advance(turn * ticks)
        passed = []

        def tick():
            passed.append(0)
            if len(passed) < ticks:
                for turn in range(steps):
                    advance(turn * ticks + len(passed))

        more = {"tick": tick} if ticks > 1 else {}
        kernel(*in_refs[: own[0]], *out_refs[: own[1]], *scratch_refs[: own[2]], **more)
        advance(steps * ticks)
        if hosts:

            @pl.when(step == steps - 1)
            def _():
                for exchange, _ in hosts:
                    exchange.close()

    params = {"collective_id": collective_id, "has_side_effects": True} if hosts else {}
    return pl.pallas_call(
        body,
        grid=grid,
        in_specs=[spec(block, index) for _, block, index in ins],
        out_specs=[spec(block, index) for _, _, block, index in outs],
        out_shape=[jax.ShapeDtypeStruct(shape, dtype) for shape, dtype, _, _ in outs],
        input_output_aliases=aliases,
        scratch_shapes=scratch,
        compiler_params=pltpu.CompilerParams(
            dimension_semantics=("arbitrary",) * len(grid), vmem_limit_bytes=VMEM_LIMIT, **params
        ),
        cost_estimate=pl.CostEstimate(flops=flops, bytes_accessed=bytes_accessed, transcendentals=0),
        name=name,
    )(*[a for a, _, _ in ins])


def moved(value, steps):
    count = lax.axis_size("seq")
    low, high = max(0, -steps), min(count, count - steps)
    return lax.ppermute(value, "seq", [(source, source + steps) for source in range(low, high)])


def reach(count):
    window, needed, hops = 2, {32: 16, 128: 32}.get(count, count) // 2, []
    while window < needed:
        hops.append(window)
        window *= 2
    return hops


class Carrier:
    def __init__(self, parts, lengths, vectors, length, sign, begin=0, end=None):
        self.count = lax.axis_size("seq")
        self.parts, self.lengths, self.vectors, self.length, self.sign = parts, lengths, vectors, length, sign
        self.hops = [[1, 2]] + [[hop] for hop in reach(self.count)]
        self.whole = len(self.hops) + 2
        self.begin, self.end = begin, self.whole if end is None else end
        self.slots = self.end - self.begin
        batches, pairs = parts[0].shape[:2]
        self.half = pairs // 2 if begin == 0 else pairs
        self.shape = (batches, self.half) + parts[0].shape[2:]

    def operands(self):
        shape = self.shape
        full = (shape[0], 2 * self.half) + shape[2:]
        outs = [(full, f32, full, None)] if self.end == self.whole else [(shape, f32, shape, None)] * 2
        ins = [(part, part.shape, None) for part in self.parts]
        return ins + [(self.vectors, self.vectors.shape, None), (self.lengths, "smem", None)], outs, []

    def scratch(self):
        return [
            pltpu.VMEM((self.slots, 2) + self.shape, f32),
            pltpu.VMEM((self.slots + 1,) + self.shape, f32),
            pltpu.VMEM((2,) + self.shape, f32),
            pltpu.SemaphoreType.DMA((self.slots, 2)),
            pltpu.SemaphoreType.DMA((self.slots, 2)),
        ]

    def bind(self, ins, outs, scratch):
        *self.part_refs, self.vec_ref, self.lengths_ref = ins
        self.out_refs = outs
        self.landed, self.totals, self.kept, self.send_sems, self.recv_sems = scratch
        self.mine = lax.axis_index("seq")
        self.core, self.chip = self.mine % 2, self.mine // 2
        self.sibling = self.mine + 1 - 2 * self.core

    def chip_at(self, hop):
        chips = self.count // 2
        return (self.chip + hop + chips) % chips * 2 + self.core

    def partners(self):
        out = []
        for slot in range(self.begin, self.end):
            if slot in (0, self.whole - 1):
                out.append(self.sibling)
            else:
                out += [self.chip_at(sign * hop) for hop in self.hops[slot - 1] for sign in (1, -1)]
        return out

    def first_part(self):
        return self.kept.at[0] if self.begin == 0 else self.part_refs[1]

    def total(self, slot):
        return self.part_refs[0] if slot == self.begin and slot > 0 else self.totals.at[slot - self.begin]

    def copies(self, slot):
        at = slot - self.begin
        if slot == 0:
            away = self.part_refs[0].at[:, pl.ds((1 - self.core) * self.half, self.half)]
            moves = [(away, self.landed.at[at, 0], self.sibling)]
        elif slot == self.whole - 1:
            moves = [(self.kept.at[1], self.landed.at[at, 0], self.sibling)]
        else:
            moves = [
                (self.total(slot), self.landed.at[at, i], self.chip_at(self.sign * hop))
                for i, hop in enumerate(self.hops[slot - 1])
            ]
        return [
            pltpu.make_async_remote_copy(
                src_ref=source, dst_ref=target, send_sem=self.send_sems.at[at, i], recv_sem=self.recv_sems.at[at, i],
                device_id=(device,), device_id_type=MESH,
            )
            for i, (source, target, device) in enumerate(moves)
        ]

    def start(self):
        self.open(self.begin)

    def open(self, slot):
        if slot == self.whole - 1:
            self.finish()
        for copy in self.copies(slot):
            copy.start()

    def fade(self, pair, devices):
        lane = lax.broadcasted_iota(jnp.int32, (LANE_FEATURES, PAIR), 1)
        row = lax.broadcasted_iota(jnp.int32, (LANE_FEATURES, PAIR), 0)
        at = pl.multiple_of((self.core * self.half + pair) * PAIR, PAIR)
        decay = self.vec_ref[DECAY : DECAY + 1, pl.ds(at, PAIR)] * float(self.length * devices)
        heads = [
            jnp.sum(jnp.where(lane == row + head * LANE_FEATURES, decay, 0.0), axis=1, keepdims=True) for head in range(2)
        ]
        return jnp.exp(jnp.where(first_lanes(LANE_FEATURES), heads[0], heads[1]))

    def same(self, batch, bound, other):
        bounds = bounds_of(self.lengths_ref, batch)
        ends = [segment_of(bounds, (device + 1) * self.length - 1) for device in (bound, other)]
        return jnp.where(ends[0] == ends[1], 1.0, 0.0).astype(f32)

    def edges(self):
        middle = 2 * self.chip
        return middle - self.sign, middle, middle + self.sign

    def run(self, slot):
        slot = slot + self.begin
        at = slot - self.begin
        for copy in self.copies(slot):
            copy.wait()
        batches = self.shape[0]
        entry, middle, leaving = self.edges()
        if slot == 0:
            flags = [self.same(batch, middle, leaving) for batch in range(batches)]
            is_first = self.core == (0 if self.sign > 0 else 1)
            for pair in range(self.half):
                fade = self.fade(pair, 1)
                for batch in range(batches):
                    own = self.part_refs[0][batch, self.core * self.half + pair]
                    other = self.landed[at, 0, batch, pair]
                    ahead, behind = jnp.where(is_first, own, other), jnp.where(is_first, other, own)
                    self.kept[0, batch, pair] = ahead
                    self.totals[at + 1, batch, pair] = ahead * fade * flags[batch] + behind
        elif slot < self.whole - 1:
            hops = self.hops[slot - 1]
            chips = self.count // 2
            flags = []
            for hop in hops:
                there = self.chip - self.sign * hop
                exists = jnp.where(jnp.logical_and(there >= 0, there < chips), 1.0, 0.0).astype(f32)
                crossed = hop - 1 if slot == 1 else hop
                flags.append([exists * self.same(batch, entry - 2 * self.sign * crossed, entry) for batch in range(batches)])
            for pair in range(self.half):
                fade = self.fade(pair, 2 if slot == 1 else 2 * hops[0])
                for batch in range(batches):
                    if slot == 1:
                        near, far = self.landed[at, 0, batch, pair], self.landed[at, 1, batch, pair]
                        here = near * flags[0][batch] + far * fade * flags[1][batch]
                    else:
                        here = self.total(slot)[batch, pair] + self.landed[at, 0, batch, pair] * fade * flags[0][batch]
                    self.totals[at + 1, batch, pair] = here
        else:
            for pair in range(self.half):
                for batch in range(batches):
                    self.out_refs[0][batch, (1 - self.core) * self.half + pair] = self.landed[at, 0, batch, pair]
        if slot + 1 < self.end:
            self.open(slot + 1)
        elif self.end < self.whole:
            self.out_refs[0][...] = self.totals[at + 1]
            self.out_refs[1][...] = self.first_part()[...]

    def close(self):
        pass

    def finish(self):
        entry, middle, _ = self.edges()
        total, first_part = self.total(self.whole - 1), self.first_part()
        is_first = self.core == (0 if self.sign > 0 else 1)
        flags = [self.same(batch, entry, middle) for batch in range(self.shape[0])]
        for pair in range(self.half):
            fade = self.fade(pair, 1)
            for batch in range(self.shape[0]):
                first = total[batch, pair]
                second = first * fade * flags[batch] + first_part[batch, pair]
                self.out_refs[0][batch, self.core * self.half + pair] = jnp.where(is_first, first, second)
                self.kept[1, batch, pair] = jnp.where(is_first, second, first)


def bit_orders(count):
    bits = count.bit_length() - 1
    if bits == 5:
        return [(0, 1, 2, 3, 4), (0, 2, 3, 1, 4), (0, 3, 1, 2, 4)]
    chip = list(range(1, bits))
    third = max(1, len(chip) // 3)
    return [tuple([0] + chip[k * third :] + chip[: k * third]) for k in range(3)]


class Unit:
    def __init__(self, array, first, rows, width, order, group, begin, end):
        self.array, self.first, self.rows, self.width, self.group = array, first, rows, width, group
        self.steps, size, landing = [], rows, 0
        bits = self.bits = len(order)
        for k, bit in enumerate(order):
            halved = size % 16 == 0
            sent = size // 2 if halved else size
            self.steps.append((bit, halved, sent, landing))
            if begin <= k < end:
                landing += sent
            size = sent
        phases = [p for p in range(2 * bits) if p < bits or self.steps[2 * bits - 1 - p][1]]
        self.phases = [p for p in phases if begin <= p < end]
        self.sums = [p for p in self.phases if p < bits]
        self.landing = landing
        self.held = self.steps[self.sums[0]][2] if self.sums else 0
        self.stages = len(self.phases)


class RowShift:
    def __init__(self, shape, hops, row=None, which=None):
        self.count, self.shape, self.hops, self.row, self.which = lax.axis_size("seq"), shape, hops, row, which
        self.slots = 1 if which is None else 2

    def operands(self):
        ins = [(self.row, self.shape, None)] if self.which is None else []
        return ins, [(self.shape, f32, self.shape, None)], []

    def scratch(self):
        return [pltpu.VMEM((2,) + self.shape, f32), pltpu.SemaphoreType.DMA, pltpu.SemaphoreType.DMA]

    def bind(self, ins, outs, scratch):
        self.in_refs, (self.out_ref,) = ins, outs
        self.rows, self.send_sem, self.recv_sem = scratch
        mine = lax.axis_index("seq")
        self.sent_to, self.got_from = (mine + self.hops + self.count) % self.count, mine - self.hops

    def partners(self):
        return [self.sent_to, (self.got_from + self.count) % self.count]

    def copy(self):
        return pltpu.make_async_remote_copy(
            src_ref=self.rows.at[0], dst_ref=self.rows.at[1], send_sem=self.send_sem, recv_sem=self.recv_sem,
            device_id=(self.sent_to,), device_id_type=MESH,
        )

    def send(self, source):
        self.rows[0] = source[...]
        self.copy().start()

    def start(self):
        if self.which is None:
            self.send(self.in_refs[0])

    def run(self, slot):
        if slot < self.slots - 1:
            self.send(self.kernel_outs[self.which])
        else:
            self.copy().wait()
            inside = jnp.logical_and(self.got_from >= 0, self.got_from < self.count)
            self.out_ref[...] = jnp.where(inside, self.rows[1], 0.0)

    def close(self):
        pass


class VectorSum:
    def __init__(self, which, row, shape, row_shape):
        self.count = lax.axis_size("seq")
        self.which, self.row, self.shape, self.row_shape = which, row, shape, row_shape
        self.bits = self.count.bit_length() - 1
        self.slots = self.bits + 1

    def operands(self):
        return [], [(self.shape, f32, self.shape, None), (self.row_shape, f32, self.row_shape, None)], []

    def scratch(self):
        return [
            pltpu.VMEM((self.bits + 1,) + self.shape, f32), pltpu.VMEM((self.bits,) + self.shape, f32),
            pltpu.VMEM((2,) + self.row_shape, f32),
            pltpu.SemaphoreType.DMA((self.bits + 1,)), pltpu.SemaphoreType.DMA((self.bits + 1,)),
        ]

    def bind(self, ins, outs, scratch):
        self.out_ref, self.row_ref = outs
        self.sums, self.landed, self.rows, self.send_sems, self.recv_sems = scratch
        mine = lax.axis_index("seq")
        self.partner = [mine + (1 - 2 * (mine // (1 << k) % 2)) * (1 << k) for k in range(self.bits)]
        self.ahead, self.behind = (mine + self.count - 1) % self.count, (mine + 1) % self.count

    def partners(self):
        return self.partner + [self.ahead, self.behind]

    def start(self):
        pass

    def close(self):
        pass

    def copy(self, k):
        if k == self.bits:
            source, target, device = self.rows.at[0], self.rows.at[1], self.ahead
        else:
            source, target, device = self.sums.at[k], self.landed.at[k], self.partner[k]
        return pltpu.make_async_remote_copy(
            src_ref=source, dst_ref=target, send_sem=self.send_sems.at[k], recv_sem=self.recv_sems.at[k],
            device_id=(device,), device_id_type=MESH,
        )

    def run(self, slot):
        if slot == 0:
            self.sums[0] = self.kernel_outs[self.which][...]
            self.rows[0] = self.kernel_outs[self.row][...]
            self.copy(self.bits).start()
        else:
            self.copy(slot - 1).wait()
            self.sums[slot] = self.sums[slot - 1] + self.landed[slot - 1]
        if slot < self.bits:
            self.copy(slot).start()
        else:
            self.out_ref[...] = self.sums[slot]
            self.copy(self.bits).wait()
            self.row_ref[...] = self.rows[1]


def add_rows(target, at, source, source_at, rows):
    block = next(b for b in (64, 56, 48, 32, 24, 16, 8) if rows % b == 0)

    def step(i, _):
        here = pl.ds(pl.multiple_of(at + i * block, 8), block)
        target[here] = target[here] + source[pl.ds(pl.multiple_of(source_at + i * block, 8), block)]
        return 0

    lax.fori_loop(0, rows // block, step, 0)


def rows8(at, size):
    return pl.ds(pl.multiple_of(at, 8), size)


class Summer:
    def __init__(self, arrays, layout):
        self.count, self.arrays, self.units = lax.axis_size("seq"), arrays, []
        orders = bit_orders(self.count)
        for array, first, rows, parts, group, turn, begin, end in layout:
            size = rows // parts
            for part in range(parts):
                order, width = orders[(turn + part) % 3], arrays[array].shape[1]
                unit = Unit(array, first + part * size, size, width, order, group, begin, end)
                self.units += [unit] if unit.phases else []
        self.groups = sorted({unit.group for unit in self.units})
        self.stages = max(unit.stages for unit in self.units)
        self.slots = self.stages + len(self.groups) - 1

    def operands(self):
        arrays = self.arrays
        return (
            [(a, "any", None) for a in arrays],
            [(a.shape, a.dtype, "any", None) for a in arrays],
            [(i, i) for i in range(len(arrays))],
        )

    def scratch(self):
        return (
            [pltpu.VMEM((max(8, unit.held), unit.width), f32) for unit in self.units]
            + [pltpu.VMEM((max(8, unit.landing), unit.width), f32) for unit in self.units]
            + [
                pltpu.SemaphoreType.DMA((len(self.units), self.stages)),
                pltpu.SemaphoreType.DMA((len(self.units), self.stages)),
                pltpu.SemaphoreType.DMA((len(self.units), 2)),
                pltpu.SemaphoreType.REGULAR((len(self.units),)),
            ]
        )

    def bind(self, ins, outs, scratch):
        size = len(self.units)
        self.refs, self.held, self.landed = outs, scratch[:size], scratch[size : 2 * size]
        self.send_sems, self.recv_sems, self.local_sems, self.free_sems = scratch[2 * size :]
        mine = lax.axis_index("seq")
        bits = self.count.bit_length() - 1
        self.bit = [mine // (1 << k) % 2 for k in range(bits)]
        self.partner = [mine + (1 - 2 * self.bit[k]) * (1 << k) for k in range(bits)]
        self.offsets = []
        for unit in self.units:
            at, seen = 0, [0]
            for which, halved, sent, _ in unit.steps:
                at = at + self.bit[which] * sent if halved else at
                seen.append(at)
            self.offsets.append(seen)

    def partners(self):
        used = sorted({unit.steps[min(p, 2 * unit.bits - 1 - p)][0] for unit in self.units for p in unit.phases})
        return [self.partner[k] for k in used]

    def start(self):
        for group in self.groups:
            for u, unit in enumerate(self.units):
                if unit.group == group:
                    self.begin(u, 0)

    def own(self, u, step):
        unit = self.units[u]
        return self.refs[unit.array].at[rows8(unit.first + self.offsets[u][step + 1], unit.steps[step][2])]

    def copies(self, u, stage):
        unit, seen, here = self.units[u], self.offsets[u], self.refs[self.units[u].array]
        phase, out = unit.phases[stage], []
        if phase < unit.bits:
            which, halved, sent, landing = unit.steps[phase]
            away = seen[phase] + (1 - self.bit[which]) * sent if halved else seen[phase]
            target = self.landed[u].at[pl.ds(landing, sent)]
            if stage == 0:
                source = here.at[rows8(unit.first + away, sent)]
                out.append(pltpu.make_async_copy(self.own(u, phase), self.held[u], self.local_sems.at[u, 0]))
            else:
                source = self.held[u].at[rows8(away - seen[unit.sums[0] + 1], sent)]
        else:
            step = 2 * unit.bits - 1 - phase
            which, _, sent, _ = unit.steps[step]
            source = target = self.own(u, step)
            if unit.sums and stage == len(unit.sums):
                source = self.held[u].at[rows8(seen[step + 1] - seen[unit.sums[0] + 1], sent)]
        return out + [
            pltpu.make_async_remote_copy(
                src_ref=source, dst_ref=target, send_sem=self.send_sems.at[u, stage],
                recv_sem=self.recv_sems.at[u, stage], device_id=(self.partner[which],), device_id_type=MESH,
            )
        ]

    def store(self, u):
        unit, seen = self.units[u], self.offsets[u]
        step = unit.sums[-1]
        source = self.held[u].at[rows8(seen[step + 1] - seen[unit.sums[0] + 1], unit.steps[step][2])]
        return pltpu.make_async_copy(source, self.own(u, step), self.local_sems.at[u, 1])

    def returns(self, u):
        unit = self.units[u]
        back = 2 * unit.bits - 1 - unit.phases[0]
        return unit.phases.index(back) if unit.sums and back in unit.phases else None

    def begin(self, u, stage):
        if stage == self.returns(u):
            pl.semaphore_wait(self.free_sems.at[u], 1)
        for copy in self.copies(u, stage):
            copy.start()

    def end(self, u, stage):
        unit, seen = self.units[u], self.offsets[u]
        for copy in self.copies(u, stage):
            copy.wait()
        phase, sums = unit.phases[stage], len(unit.sums)
        if stage == 0 and self.returns(u) is not None:
            partner = self.partner[unit.steps[phase][0]]
            pl.semaphore_signal(self.free_sems.at[u], inc=1, device_id=(partner,), device_id_type=MESH)
        if phase < unit.bits:
            _, _, sent, landing = unit.steps[phase]
            add_rows(self.held[u], seen[phase + 1] - seen[unit.sums[0] + 1], self.landed[u], landing, sent)
            if stage == sums - 1:
                self.store(u).start()
        elif sums and stage == sums:
            self.store(u).wait()

    def close(self):
        for u, unit in enumerate(self.units):
            if unit.sums and unit.stages == len(unit.sums):
                self.store(u).wait()

    def run(self, slot):
        for place, group in enumerate(self.groups):
            for u, unit in enumerate(self.units):
                stage = slot - place
                if unit.group != group:
                    continue
                if unit.phases[0] >= unit.bits and unit.phases[-1] == 2 * unit.bits - 1 and stage >= unit.stages - 1:
                    stage = unit.stages - 1 if slot == self.slots - 1 else -1
                if 0 <= stage < unit.stages:
                    self.end(u, stage)
                    if stage + 1 < unit.stages:
                        self.begin(u, stage + 1)


def gather_kernel(moves, *refs):
    count = len(moves)
    ins, row_ref, vectors_ref, (*outs, sems) = refs[:count], refs[count], refs[count + 1], refs[count + 2 :]
    buffers, outs = outs[-count:], outs[:-count]
    loads = [pltpu.make_async_copy(source, buffer, sems.at[0, i]) for i, (source, buffer) in enumerate(zip(ins, buffers))]
    for load in loads:
        load.start()
    for i, ref in enumerate(outs[moves[-1][0] + 1 :]):
        ref[...] = vectors_ref[i : i + 1].reshape(ref.shape)
    stores = []
    for i, (out, row, column) in enumerate(moves):
        rows, columns = buffers[i].shape[-2:]
        loads[i].wait()
        if i == count - 1:
            for batch in range(row_ref.shape[0]):
                buffers[i][batch, rows - 1 :] += row_ref[batch]
            stores.append(pltpu.make_async_copy(buffers[i], outs[out], sems.at[1, i]))
            stores[-1].start()
            break
        stores.append(pltpu.make_async_copy(buffers[i], outs[out].at[pl.ds(row, rows), pl.ds(column, columns)], sems.at[1, i]))
        stores[-1].start()
    for store in stores:
        store.wait()


def gathered(arrays, spans, hidden_width, tokens, last_row, vectors, count):
    width = arrays[0].shape[0]
    moves, shapes = [], [(width, hidden_width), (hidden_width, width)]
    for low, _ in spans:
        moves += [(0, 0, low), (1, low, 0)]
    arrays = arrays + [tokens]
    for array in arrays[len(moves) :]:
        moves.append((len(shapes), 0, 0))
        shapes.append(array.shape)
    return call(
        functools.partial(gather_kernel, moves),
        (1,),
        [(a, "any", None) for a in arrays] + [(last_row, last_row.shape, None), (vectors, vectors.shape, None)],
        [(shape, f32, "any", None) for shape in shapes] + [((width,), f32, (width,), None)] * count,
        "gather",
        scratch=[pltpu.VMEM(a.shape, f32) for a in arrays] + [pltpu.SemaphoreType.DMA((2, len(moves)))],
    )


def local(
    incoming_hidden,
    packed_run_lengths,
    prior_standardize_factor,
    prior_standardize_addend,
    respond_interpolant,
    address_interpolant,
    content_interpolant,
    valve_interpolant,
    respond_transform,
    address_transform,
    content_transform,
    valve_transform,
    damping_rates,
    immediate_boost,
    cluster_normal_factor,
    cluster_normal_shift_term,
    readout_transform,
    posterior_standardize_factor,
    posterior_standardize_addend,
    dense_address_interpolant,
    dense_respond_interpolant,
    dense_address_transform,
    dense_content_transform,
    dense_respond_transform,
    objective_adjoint,
):
    batches, length, width = incoming_hidden.shape
    hidden_width = dense_address_transform.shape[1]
    pairs = width // PAIR
    depth = lax.axis_size("seq").bit_length() - 1
    lengths = packed_run_lengths
    vectors = [
        prior_standardize_factor, prior_standardize_addend, respond_interpolant, address_interpolant,
        content_interpolant, valve_interpolant, damping_rates, immediate_boost, cluster_normal_factor,
        cluster_normal_shift_term, posterior_standardize_factor, posterior_standardize_addend,
        dense_address_interpolant, dense_respond_interpolant,
    ]

    def table(w):
        return (w, w.shape, None)

    def rows_of(a):
        return (a, (1,) + a.shape[1:], lambda b, *_: (b,) + (0,) * (a.ndim - 1))

    def rows_out(shape, dtype=f32):
        return (shape, dtype, (1,) + tuple(shape[1:]), lambda b, *_: (b,) + (0,) * (len(shape) - 1))

    def sum_out(*shape):
        return (shape, f32, shape, None)

    tokens, states, one_row = (batches, length, width), (batches, pairs, LANE_FEATURES, PAIR), (batches, 1, width)
    square_flops = 2 * batches * length * width * width
    before = moved(incoming_hidden[:, -1, :].astype(f32), 1)[:, None, :]
    cols, row, vectors = call(
        tokens_kernel,
        (1,),
        [(lengths, "smem", None)] + [table(v) for v in vectors],
        [sum_out(batches, length, 8), sum_out(batches, 1, length), sum_out(16, width)],
        "tokens",
    )
    common = [rows_of(incoming_hidden), rows_of(before), rows_of(cols), table(vectors)]
    keys, values, end_state = call(
        functools.partial(project_kernel, (MIX_K, MIX_V), True),
        (batches,),
        common + [table(address_transform), table(content_transform)],
        [rows_out(tokens)] * 2 + [rows_out(states)],
        "project_keys",
        flops=4 * square_flops,
    )
    nearest = Carrier([end_state], lengths, vectors, length, 1, 0, 2)
    recept, valve, *near_state = call(
        functools.partial(project_kernel, (MIX_R, MIX_G), False),
        (batches,),
        common + [table(respond_transform), table(valve_transform)],
        [rows_out(tokens)] * 2,
        "project_recept",
        flops=4 * square_flops,
        hosts=[(nearest, [batches // 2, batches])],
        collective_id=1,
    )
    by_pair = lambda a: (a, (1, length, PAIR), lambda b, p: (b, 0, p))
    pair_vectors = (vectors, (vectors.shape[0], PAIR), lambda b, p: (0, p))
    pair_state = lambda s: (s, (1, 1, LANE_FEATURES, PAIR), lambda b, p: (b, p, 0, 0))
    pair_out = (tokens, f32, (1, length, PAIR), lambda b, p: (b, 0, p))
    further = Carrier(near_state, lengths, vectors, length, 1, 2)
    steps = batches * pairs
    mixed, state = call(
        mix_kernel,
        (batches, pairs),
        [by_pair(recept), by_pair(keys), by_pair(values), rows_of(cols), rows_of(row), pair_vectors],
        [pair_out],
        "mix",
        flops=3 * 2 * batches * length * length * width * 2,
        hosts=[(further, [(i + 1) * steps // further.slots for i in range(further.slots)])],
        collective_id=2,
    )
    tiles = length // BLOCK
    tiled = lambda a: (a, (1, BLOCK, a.shape[2]), lambda b, i: (b, i, 0))
    tiled_out = (tokens, f32, (1, BLOCK, width), lambda b, i: (b, i, 0))
    wkv, attended, second, second_row = call(
        readout_kernel,
        (batches, tiles),
        [
            tiled(mixed), tiled(recept), rows_of(state), tiled(valve), tiled(cols), table(vectors),
            tiled(incoming_hidden), table(readout_transform),
        ],
        [tiled_out] * 3 + [rows_out(one_row)],
        "readout",
        flops=2 * square_flops,
    )
    tile_rows = lambda a: (a, (1, BLOCK, a.shape[2]), lambda b, i: (b, tiles - 1 - i, 0))
    ahead = (second, (1, 8, width), lambda b, i: (b, jnp.maximum((tiles - 1 - i) * (BLOCK // 8) - 1, 0), 0))
    tile_out = lambda dtype: (tokens, dtype, (1, BLOCK, width), lambda b, i: (b, tiles - 1 - i, 0))
    spans = [(at, min(1024, hidden_width - at)) for at in range(0, hidden_width, 1024)]
    ends = 2 * depth

    even = [(0, 0, 128, 0), (0, 128, 128, 1), (0, 256, 512, 2), (1, 0, 512, 0), (1, 512, 512, 1)]
    rest_units = [(2, 0, 768, 0), (0, 0, 768, 1), (1, 0, 512, 2), (1, 512, 128, 2)]
    one = [(0, 0, 256, 0), (0, 256, 256, 1), (0, 512, 256, 2)]

    def layout_of(units, group, begin, end, base=0):
        return [(base + i, first, rows, 1, group, order, begin, end) for i, first, rows, order in units]

    def hosted(arrays, units, begin, end, when):
        summer = Summer(arrays, layout_of(units, 0, begin, end))
        return summer, [when[min(i, len(when) - 1)] for i in range(summer.slots)]

    def channel(part, kept, hosts, collective_id, shift=None):
        low, size = spans[part]
        first, last = part == 0, part == len(spans) - 1
        ins = [
            tile_rows(second), ahead, rows_of(second_row), tile_rows(objective_adjoint), tile_rows(cols), table(vectors),
            (dense_address_transform, "any", None), (dense_content_transform, "any", None),
        ]
        ins += [table(dense_respond_transform)] if first or last else []
        ins += [tile_rows(a) for a in kept]
        ins += [tile_rows(attended)] if last else []
        if last:
            outs = [tile_out(bf16), tile_out(f32), sum_out(*one_row), sum_out(width, width), sum_out(2, width)]
        else:
            outs = [tile_out(f32)] * (3 if first else 2)
        return call(
            functools.partial(channel_kernel, low, size, first, last, shift),
            (batches, tiles),
            ins,
            outs + [sum_out(width, size), sum_out(size, width)],
            "channel_%d" % part,
            scratch=[
                pltpu.VMEM((BLOCK, 8), f32), pltpu.VMEM((width, size), bf16), pltpu.VMEM((size, width), bf16),
                pltpu.SemaphoreType.DMA((2,)), pltpu.VMEM((1, width), f32),
            ],
            flops=7 * 2 * batches * length * width * (2 * size + (width if last else 0)),
            hosts=hosts,
            collective_id=collective_id,
        )

    steps = batches * tiles
    shift = RowShift(one_row, 1, second_row)
    gate, total, d_inner, *part_a, second_row = channel(0, [], [(shift, [1])], 8, shift)
    total, d_inner, *rest = channel(1, [gate, total, d_inner], [hosted(part_a, even, 0, 4, [1, 3, 4])], 6)
    part_b, part_a = rest[:2], rest[2:]
    block, d_second, _, grad_filter, channel_vectors, *rest = channel(
        2,
        [gate, total, d_inner],
        [hosted(part_b, even, 0, 3, [1, 3, 4]), hosted(part_a, even, 4, depth + 2, [2, 3, 4]), (RowShift(one_row, -1, which=2), [steps] * 2)],
        7,
    )
    part_c, part_b, part_a, back_second = [rest[0], rest[1], grad_filter], rest[2:4], rest[4:6], rest[6]
    d_attended, d_wkv, d_valve, carry, grad_output, attention_vectors, *rest = call(
        attention_back_kernel,
        (batches, tiles),
        [
            tiled(d_second), rows_of(back_second), tiled(attended), tiled(objective_adjoint), tiled(wkv),
            tiled(valve), tiled(recept), tiled(cols), table(vectors), table(readout_transform),
        ],
        [tiled_out] * 3 + [rows_out(states), sum_out(width, width), sum_out(4, width)],
        "attention_back",
        flops=2 * square_flops,
        hosts=[
            hosted(part_c, rest_units, 0, 1, [3]),
            hosted(part_b, even, 3, depth + 1, [1, 4]),
            hosted(part_a, even, depth + 2, ends - 1, [2, 4]),
        ],
        collective_id=3,
    )
    part_c, part_b, part_a = rest[:3], rest[3:5], rest[5:7]
    steps = batches * pairs
    arriving = Carrier([carry], lengths, vectors, length, -1)
    d_recept, d_keys, d_values, mix_vectors, out_state, *rest = call(
        mix_back_kernel,
        (batches, pairs),
        [
            by_pair(recept), by_pair(keys), by_pair(values), by_pair(d_wkv), pair_state(state), rows_of(cols), rows_of(row),
            pair_vectors,
        ],
        [pair_out] * 3 + [((batches, 2, width), f32, (1, 2, PAIR), lambda b, p: (b, 0, p))],
        "mix_back",
        flops=9 * 2 * batches * length * length * width * 2,
        hosts=[
            (arriving, [(i + 1) * steps // arriving.slots for i in range(arriving.slots)]),
            hosted(part_b, even, depth + 1, ends - 1, [2, 5, 9]),
            hosted(part_c, rest_units, 1, depth, [5, 8, 10, 12]),
            hosted(part_a, even, ends - 1, ends, [6]),
        ],
        collective_id=4,
    )
    part_b, part_c, part_a = rest[:2], rest[2:5], rest[5:7]
    steps = 4 * batches
    wide = lambda: pltpu.VMEM((length, width), f32)
    grad_recept, grad_keys, grad_values, grad_gate_w, d_keys, d_values, decay_vector, *rest = call(
        weights_back_kernel,
        (batches, 4),
        common
        + [
            rows_of(d_recept), rows_of(d_keys), rows_of(d_values), rows_of(d_valve), rows_of(keys), rows_of(values),
            rows_of(state), rows_of(out_state),
        ],
        [sum_out(width, width)] * 4 + [rows_out(tokens)] * 2 + [sum_out(1, width)],
        "weights_back",
        scratch=[wide(), wide()],
        flops=3 * 4 * square_flops,
        hosts=[
            hosted([grad_output], one, 0, depth, [1, 3, 4, 6, 8]),
            hosted(part_c, rest_units, depth, ends - 1, [3, 4, 6, 8]),
            hosted(part_b, even, ends - 1, ends, [8]),
        ],
        collective_id=5,
    )
    grad_output, part_c, part_b = rest[0], rest[1:4], rest[4:6]
    layout, part = [], width // 6
    for half in range(2):
        low = half * width // 2
        layout += layout_of([(i, low, width // 2, (i + half) % 3) for i in range(3)], half, 0, ends, 4)
        layout += layout_of([(3, low + i * part, part, i) for i in range(3)], half, 0, ends, 4)
    layout += layout_of(rest_units, 2, ends - 1, ends) + layout_of(one, 2, depth, ends, 3)
    summer = Summer(part_c + [grad_output, grad_recept, grad_keys, grad_values, grad_gate_w], layout)
    d_x, _, _, *rest = call(
        inputs_back_kernel,
        (batches, 4),
        common
        + [
            rows_of(d_attended), rows_of(d_recept), rows_of(d_keys), rows_of(d_values), rows_of(d_valve),
            rows_of(mix_vectors), table(attention_vectors), table(channel_vectors), table(decay_vector),
        ]
        + [table(w) for w in (respond_transform, address_transform, content_transform, valve_transform)],
        [rows_out(tokens), sum_out(*one_row), sum_out(*vectors.shape)],
        "inputs_back",
        scratch=[wide(), wide(), wide()],
        flops=2 * 4 * square_flops,
        hosts=[
            (summer, [3, 6, 8] + [steps] * (summer.slots - 3)),
            (VectorSum(2, 1, vectors.shape, one_row), [steps] * (depth + 1)),
        ],
        collective_id=0,
    )
    summed, vectors, last_row = rest[:8], rest[8], rest[9]
    w_expand, w_shrink, w_filter, w_output, w_recept, w_keys, w_values, w_gate, grad_tokens, *vectors = gathered(
        part_a + part_b + list(summed), spans, hidden_width, d_x, last_row, vectors, MIX_F + 1
    )
    return (
        block, grad_tokens, *[vectors[i] for i in range(6)], w_recept, w_keys, w_values, w_gate,
        vectors[6], vectors[7], vectors[8], vectors[9], w_output, vectors[10], vectors[11], vectors[12], vectors[13],
        w_expand, w_shrink, w_filter,
    )


def solution(mesh):
    rows = P(None, "seq", None)
    return jax.shard_map(
        local,
        mesh=mesh,
        in_specs=(rows,) + (P(),) * 23 + (rows,),
        out_specs=(rows, rows) + (P(),) * 22,
        check_vma=False,
    )
```
